512 devices in a mesh: dp: 16 (over y_lo, x, core), ctx: 32 (over y_hi, z).
Axes of the slice: x: 4, y: 4 (y_hi: 2, y_lo: 2; y = y_hi * 2 + y_lo), z: 16, core: 2. Of those that a mesh axis runs over, the one named last changes fastest.
Arguments:
- tokens: bfloat16 [16, 32, 128, 3072], P('dp', 'ctx'), may hold values from -6 to 6
- modulation: float32 [16, 3, 3072], P('dp'), may hold values from -3 to 3
- query_key_value_weight: bfloat16 [3072, 1536], P('dp'), may hold values from -0.109375 to 0.109375
- output_projection_weight: bfloat16 [512, 3072], P(None, 'dp'), may hold values from -0.25 to 0.25
- adapter_down_maps: bfloat16 [3072, 64], P('dp'), may hold values from -0.109375 to 0.109375
- adapter_up_maps: bfloat16 [64, 512], P('dp'), may hold values from -1 to 1
- output_gradient: bfloat16 [16, 32, 128, 3072], P('dp', 'ctx'), may hold values from -6 to 6
Outputs:
- mixed_out: bfloat16 [16, 32, 128, 3072], P('dp', 'ctx')
- tokens_grad: bfloat16 [16, 32, 128, 3072], P('dp', 'ctx')
- modulation_grad: float32 [16, 3, 3072], P('dp')
- down_grad: float32 [3072, 64], P('dp')
- up_grad: float32 [64, 512], P('dp')
The draws below stay inside these ranges and needn't reach their ends.
All inputs are finite; a program needn't handle non-finite values.
Results may differ from the reference program's by a relative error of at most 0.019.
Values may be sent and summed in bfloat16 or wider, within the bound.
No kernel may reach another device: no remote copies, remote signals or barrier semaphores. Data moves between devices by JAX's collectives and lax.ppermute only.
A program may use at most 128 MiB of HBM per device.

```python
import jax
import jax.numpy as jnp
from jax import lax

MODEL_WIDTH = 3072
LOCAL_HEADS = 4
HEAD_SIZE = 128
ADAPTER_RANK = 32
FRAMES = 32
CLIPS = 16
POS = 128
TOKENS = 65536


def steps_of(own_key, dims, cuts, low, high):
    loudness = 1.0
    for position, blocks in cuts:
        heights = jax.random.uniform(jax.random.fold_in(jax.random.fold_in(own_key, 6), position), (blocks,), jnp.float32, low / len(cuts), high / len(cuts))
        loudness = loudness * jnp.repeat(jnp.exp(heights), dims[position] // blocks).reshape((-1,) + (1,) * (len(dims) - 1 - position))
    return loudness


def normal_values(rng, dims, width, bound, pieces=(), held_as=jnp.bfloat16):
    factor_of = steps_of(rng, dims, pieces, -0.22, 0.18) if pieces else 1.0
    array = jax.random.normal(rng, dims, jnp.float32) * width * factor_of
    return jnp.minimum(jnp.maximum(array, -bound), bound).astype(held_as)


def setup_inputs(seed: int = 0) -> dict:
    seeds = jax.random.split(jax.random.key(seed), 8)
    tokens = normal_values(seeds[0], (CLIPS, FRAMES, POS, MODEL_WIDTH), 1.0, 6.0, ((0, 16), (1, 32)))
    modulation = normal_values(seeds[1], (CLIPS, 3, MODEL_WIDTH), 0.5, 3.0, ((0, 16),), jnp.float32)
    query_key_value_weight = normal_values(seeds[2], (MODEL_WIDTH, 3 * LOCAL_HEADS * HEAD_SIZE), MODEL_WIDTH ** -0.5, 0.109375, ((0, 16),))
    output_projection_weight = normal_values(seeds[3], (LOCAL_HEADS * HEAD_SIZE, MODEL_WIDTH), (LOCAL_HEADS * HEAD_SIZE) ** -0.5, 0.25, ((1, 16),))
    adapter_down_maps = normal_values(seeds[4], (MODEL_WIDTH, 2 * ADAPTER_RANK), MODEL_WIDTH ** -0.5, 0.109375, ((0, 16),))
    adapter_up_maps = normal_values(seeds[5], (2 * ADAPTER_RANK, LOCAL_HEADS * HEAD_SIZE), ADAPTER_RANK ** -0.5, 1.0, ((0, 16),))
    output_gradient = normal_values(seeds[6], (CLIPS, FRAMES, POS, MODEL_WIDTH), 1.0, 6.0, ((0, 16), (1, 32)))
    return {"tokens": tokens, "modulation": modulation, "query_key_value_weight": query_key_value_weight, "output_projection_weight": output_projection_weight, "adapter_down_maps": adapter_down_maps, "adapter_up_maps": adapter_up_maps, "output_gradient": output_gradient}


EPSILON = 1e-06

def times_transposed(left, right):
    return lax.dot_general(left, right, (((1,), (1,)), ((), ())), preferred_element_type=jnp.float32)

def transposed_times(left, right):
    return lax.dot_general(left, right, (((0,), (0,)), ((), ())), preferred_element_type=jnp.float32)

def normalize_rows(flat_tokens, modulation_per_clip):
    values = flat_tokens.astype(jnp.float32)
    center = values - lax.optimization_barrier(jnp.mean(values, -1, keepdims=True))
    inverse_value = lax.rsqrt(lax.optimization_barrier(jnp.mean(center * center, -1, keepdims=True)) + EPSILON)
    normalized_input = center * inverse_value
    hidden_state = (normalized_input * (1.0 + modulation_per_clip[1]) + modulation_per_clip[0]).astype(jnp.bfloat16)
    return (normalized_input, inverse_value, hidden_state)

def projection_forward(hidden_state, qkv_full, down_full, up_full, adapter_inner_rank):
    head_size_value = up_full.shape[1]
    base_proj = jnp.dot(hidden_state, qkv_full, preferred_element_type=jnp.float32)
    low_rank_product = jnp.dot(hidden_state, down_full, preferred_element_type=jnp.float32).astype(jnp.bfloat16)
    delta_query = jnp.dot(low_rank_product[:, :adapter_inner_rank], up_full[:adapter_inner_rank], preferred_element_type=jnp.float32)
    delta_value = jnp.dot(low_rank_product[:, adapter_inner_rank:], up_full[adapter_inner_rank:], preferred_element_type=jnp.float32)
    query_unnormalized = base_proj[:, :head_size_value] + delta_query
    key_unnormalized = base_proj[:, head_size_value:2 * head_size_value]
    value_row_matrix = (base_proj[:, 2 * head_size_value:] + delta_value).astype(jnp.bfloat16)
    return (low_rank_product, query_unnormalized, key_unnormalized, value_row_matrix)

def head_stats(raw_rows, head_dim):
    grouped = raw_rows.reshape(raw_rows.shape[0], -1, head_dim)
    inverse_value = lax.rsqrt(lax.optimization_barrier(jnp.mean(grouped * grouped, -1, keepdims=True)) + EPSILON)
    return (grouped, inverse_value)

def head_normed(raw_rows, head_dim):
    grouped, inverse_value = head_stats(raw_rows, head_dim)
    return (grouped * inverse_value).reshape(raw_rows.shape).astype(jnp.bfloat16)

def head_norm_back(raw_rows, incoming_grad, head_dim):
    grouped, inverse_value = head_stats(raw_rows, head_dim)
    incoming = incoming_grad.astype(jnp.float32).reshape(grouped.shape)
    inner_mean = lax.optimization_barrier(jnp.mean(grouped * incoming, -1, keepdims=True))
    return (inverse_value * incoming - grouped * inverse_value ** 3 * inner_mean).reshape(raw_rows.shape)

def split_heads(rows_in, head_dim):
    frame_count, place_count, head_size_value = rows_in.shape
    return rows_in.reshape(frame_count, place_count, head_size_value // head_dim, head_dim).astype(jnp.float32)

def attend(query_rows, key_rows, value_row_matrix, head_dim):
    score_scale = head_dim ** (-0.5)
    query_heads = split_heads(query_rows, head_dim)
    key_heads = split_heads(key_rows, head_dim)
    value_heads = split_heads(value_row_matrix, head_dim)
    scores = jnp.einsum('fphd,gphd->phfg', query_heads, key_heads) * score_scale
    expo = jnp.exp(scores)
    attention_weights = expo / lax.optimization_barrier(jnp.sum(expo, -1, keepdims=True))
    weights_low = attention_weights.astype(jnp.bfloat16).astype(jnp.float32)
    attended = jnp.einsum('phfg,gphd->fphd', weights_low, value_heads).astype(jnp.bfloat16)
    return (attended.reshape(query_rows.shape), attention_weights)

def attend_back(attended_grad, attention_weights, query_rows, key_rows, value_row_matrix, head_dim):
    score_scale = head_dim ** (-0.5)
    grad_heads = split_heads(attended_grad, head_dim)
    query_heads = split_heads(query_rows, head_dim)
    key_heads = split_heads(key_rows, head_dim)
    value_heads = split_heads(value_row_matrix, head_dim)
    weights_low = attention_weights.astype(jnp.bfloat16).astype(jnp.float32)
    prob_grad = jnp.einsum('fphd,gphd->phfg', grad_heads, value_heads)
    value_gradient = jnp.einsum('phfg,fphd->gphd', weights_low, grad_heads).astype(jnp.bfloat16)
    score_grad = attention_weights * (prob_grad - lax.optimization_barrier(jnp.sum(attention_weights * prob_grad, -1, keepdims=True)))
    score_low = (score_grad * score_scale).astype(jnp.bfloat16).astype(jnp.float32)
    query_grad = jnp.einsum('phfg,gphd->fphd', score_low, key_heads).astype(jnp.bfloat16)
    key_grad = jnp.einsum('phfg,fphd->gphd', score_low, query_heads).astype(jnp.bfloat16)
    shape_rows = query_rows.shape
    return (query_grad.reshape(shape_rows), key_grad.reshape(shape_rows), value_gradient.reshape(shape_rows))

def projection_backward(query_normalized_gradient, key_normalized_gradient, value_gradient, query_unnormalized, key_unnormalized, hidden_state, low_rank_product, normalized_input, inverse_value, modulation_per_clip, qkv_full, down_full, up_full, adapter_inner_rank, head_dim):
    head_size_value = up_full.shape[1]
    query_back = head_norm_back(query_unnormalized, query_normalized_gradient, head_dim)
    key_back = head_norm_back(key_unnormalized, key_normalized_gradient, head_dim)
    joined_grad = jnp.concatenate([query_back, key_back, value_gradient.astype(jnp.float32)], 1).astype(jnp.bfloat16)
    query_block = joined_grad[:, :head_size_value]
    value_block = joined_grad[:, 2 * head_size_value:]
    up_grad = jnp.concatenate([transposed_times(low_rank_product[:, :adapter_inner_rank], query_block), transposed_times(low_rank_product[:, adapter_inner_rank:], value_block)], 0)
    low_grad = jnp.concatenate([times_transposed(query_block, up_full[:adapter_inner_rank]), times_transposed(value_block, up_full[adapter_inner_rank:])], 1).astype(jnp.bfloat16)
    hidden_grad = times_transposed(joined_grad, qkv_full) + times_transposed(low_grad, down_full)
    down_grad = transposed_times(hidden_state, low_grad)
    shift_gradient = lax.optimization_barrier(jnp.sum(hidden_grad, 0))
    scale_gradient = lax.optimization_barrier(jnp.sum(hidden_grad * normalized_input, 0))
    normed_grad = hidden_grad * (1.0 + modulation_per_clip[1])
    first_mean = lax.optimization_barrier(jnp.mean(normed_grad, -1, keepdims=True))
    second_mean = lax.optimization_barrier(jnp.mean(normed_grad * normalized_input, -1, keepdims=True))
    token_gradient_rows = inverse_value * (normed_grad - first_mean - normalized_input * second_mean)
    return (token_gradient_rows, shift_gradient, scale_gradient, down_grad, up_grad)

def reference(tokens, modulation, query_key_value_weight, output_projection_weight, adapter_down_maps, adapter_up_maps, output_gradient):
    head_size_value = LOCAL_HEADS * HEAD_SIZE
    frame_shape = (FRAMES, POS, head_size_value)

    def clip_pass(inputs):
        tokens_clip, modulation_per_clip, upstream_clip = inputs
        flat_tokens = tokens_clip.reshape(-1, MODEL_WIDTH)
        normalized_input, inverse_value, hidden_state = normalize_rows(flat_tokens, modulation_per_clip)
        low_rank_product, query_unnormalized, key_unnormalized, value_row_matrix = projection_forward(hidden_state, query_key_value_weight, adapter_down_maps, adapter_up_maps, ADAPTER_RANK)
        query_rows = head_normed(query_unnormalized, HEAD_SIZE)
        key_rows = head_normed(key_unnormalized, HEAD_SIZE)
        attended, attention_weights = attend(query_rows.reshape(frame_shape), key_rows.reshape(frame_shape), value_row_matrix.reshape(frame_shape), HEAD_SIZE)
        branch_out = jnp.dot(attended.reshape(-1, head_size_value), output_projection_weight, preferred_element_type=jnp.float32)
        mixed_out = (flat_tokens.astype(jnp.float32) + modulation_per_clip[2] * branch_out).astype(jnp.bfloat16)
        upstream = upstream_clip.reshape(-1, MODEL_WIDTH).astype(jnp.float32)
        gate_grad = lax.optimization_barrier(jnp.sum(upstream * branch_out, 0))
        branch_grad = (upstream * modulation_per_clip[2]).astype(jnp.bfloat16)
        attended_grad = times_transposed(branch_grad, output_projection_weight).astype(jnp.bfloat16)
        query_normalized_gradient, key_normalized_gradient, value_gradient = attend_back(attended_grad.reshape(frame_shape), attention_weights, query_rows.reshape(frame_shape), key_rows.reshape(frame_shape), value_row_matrix.reshape(frame_shape), HEAD_SIZE)
        token_gradient_rows, shift_gradient, scale_gradient, down_section, up_section = projection_backward(query_normalized_gradient.reshape(-1, head_size_value), key_normalized_gradient.reshape(-1, head_size_value), value_gradient.reshape(-1, head_size_value), query_unnormalized, key_unnormalized, hidden_state, low_rank_product, normalized_input, inverse_value, modulation_per_clip, query_key_value_weight, adapter_down_maps, adapter_up_maps, ADAPTER_RANK, HEAD_SIZE)
        tokens_grad = (upstream + token_gradient_rows).astype(jnp.bfloat16)
        modulation_part = jnp.stack([shift_gradient, scale_gradient, gate_grad], 0)
        return (mixed_out.reshape(tokens_clip.shape), tokens_grad.reshape(tokens_clip.shape), modulation_part, down_section, up_section)
    mixed_out, tokens_grad, modulation_parts, down_parts, up_parts = lax.map(clip_pass, (tokens, modulation, output_gradient))
    grad_scale = TOKENS ** (-0.5)
    return (mixed_out, tokens_grad, modulation_parts * grad_scale, lax.optimization_barrier(jnp.sum(down_parts, 0)) * grad_scale, lax.optimization_barrier(jnp.sum(up_parts, 0)) * grad_scale)
```

```python
import functools

import jax
import jax.numpy as jnp
from jax import lax
from jax.experimental import pallas as pl
from jax.experimental.pallas import tpu as pltpu
from jax.sharding import PartitionSpec as P

HEAD = 128
EPS = 1e-06
F32 = jnp.float32
BF16 = jnp.bfloat16
NT = (((1,), (1,)), ((), ()))
TN = (((0,), (0,)), ((), ()))
NN = (((1,), (0,)), ((), ()))


def dot(a, b, dims=NN):
    return lax.dot_general(a, b, dims, preferred_element_type=F32)


def call(body, out_shape, grid=None, in_specs=None, out_specs=None, scratch=(), flops=0, moved=0, vmem=24):
    extra = {} if grid is None else {"grid": grid, "in_specs": in_specs, "out_specs": out_specs}
    return pl.pallas_call(
        body,
        out_shape=out_shape,
        scratch_shapes=list(scratch),
        compiler_params=pltpu.CompilerParams(vmem_limit_bytes=vmem * 2**20),
        cost_estimate=pl.CostEstimate(flops=flops, bytes_accessed=moved, transcendentals=0),
        **extra,
    )


def shape(dims, dtype):
    return jax.ShapeDtypeStruct(dims, dtype)


def whole(*dims):
    return pl.BlockSpec(dims, lambda i: (0,) * len(dims))


def split_up(up, rank):
    row = lax.broadcasted_iota(jnp.int32, up.shape, 0)
    zero = jnp.zeros_like(up)
    return jnp.where(row < rank, up, zero), jnp.where(row < rank, zero, up)


def unpack_blocks(ref, t, heads):
    groups = ref.shape[0] // heads
    columns = [
        jnp.concatenate([ref[g * heads + h, t] for g in range(groups)], 0) for h in range(heads)
    ]
    return jnp.concatenate(columns, 1)


def normalize(x, mod, upstream, hidden, hidden_t, branch_grad, mean_out, rstd_out):
    values = x[...].astype(F32)
    mean = jnp.mean(values, -1, keepdims=True)
    center = values - mean
    rstd = lax.rsqrt(jnp.mean(center * center, -1, keepdims=True) + EPS)
    mean_out[...] = mean
    rstd_out[...] = rstd
    state = (center * rstd * (1.0 + mod[1:2, :]) + mod[0:1, :]).astype(BF16)
    hidden[...] = state
    hidden_t[...] = state.T
    branch_grad[...] = (upstream[...].astype(F32) * mod[2:3, :]).astype(BF16)


def attended_grads(steps, branch_grad, w, grad_out, acc):
    k = pl.program_id(0)

    @pl.when(k == 0)
    def _():
        acc[...] = jnp.zeros_like(acc)

    acc[...] += dot(branch_grad[...], w[...].reshape(-1, w.shape[2]))

    @pl.when(k == steps - 1)
    def _():
        grad = acc[...].astype(BF16)
        positions = grad_out.shape[2]
        heads = grad.shape[1] // HEAD
        for g in range(grad.shape[0] // positions):
            for h in range(heads):
                grad_out[g * heads + h, 0] = grad[
                    g * positions : (g + 1) * positions, h * HEAD : (h + 1) * HEAD
                ]


def head_scales(x):
    parts = []
    for h in range(x.shape[1] // HEAD):
        v = x[:, h * HEAD : (h + 1) * HEAD]
        parts.append(lax.rsqrt(jnp.mean(v * v, -1, keepdims=True) + EPS))
    return parts


def projections(steps, rank, hidden, w, up, sent, raw, low_out, acc):
    k = pl.program_id(0)

    @pl.when(k == 0)
    def _():
        acc[...] = jnp.zeros_like(acc)

    acc[...] += dot(hidden[...], w[...])

    @pl.when(k == steps - 1)
    def _():
        n = up.shape[1]
        heads = n // HEAD
        up_q, up_v = split_up(up[...], rank)
        low_rows = acc[:, 3 * n :].astype(BF16)
        low_out[...] = low_rows
        q = acc[:, :n] + dot(low_rows, up_q)
        kk = acc[:, n : 2 * n]
        v = acc[:, 2 * n : 3 * n] + dot(low_rows, up_v)
        raw[:, :n] = q
        raw[:, n:] = kk
        positions = sent.shape[2]
        for t, x in enumerate((q, kk, v)):
            scales = head_scales(x) if t < 2 else None
            for h in range(heads):
                rows = x[:, h * HEAD : (h + 1) * HEAD]
                if t < 2:
                    rows = rows * scales[h]
                rows = rows.astype(BF16)
                for g in range(x.shape[0] // positions):
                    sent[g * heads + h, t] = rows[g * positions : (g + 1) * positions]


def attention(rows_in, grad_in, back):
    frames, _, positions, _ = rows_in.shape
    group = 8
    total = frames * group
    row = lax.broadcasted_iota(jnp.int32, (total, total), 0) % group
    col = lax.broadcasted_iota(jnp.int32, (total, total), 1) % group
    same = row == col
    scale = HEAD**-0.5
    halves = []
    for p in range(positions // group):

        def rows_of(ref, t):
            x = ref[:, t].astype(F32)[:, p * group : (p + 1) * group]
            return x.reshape(total, HEAD).astype(BF16)

        q, k, v = (rows_of(rows_in, t) for t in range(3))
        g = rows_of(grad_in, 0)
        s = dot(q, k, NT) * scale
        e = jnp.where(same, jnp.exp(s), 0.0)
        a = e / jnp.sum(e, -1, keepdims=True)
        low = a.astype(BF16)
        attended = dot(low, v)
        dp = dot(g, v, NT)
        dv = dot(low, g, TN)
        inner = jnp.sum(a * dp, -1, keepdims=True)
        ds = (a * (dp - inner) * scale).astype(BF16)
        dq = dot(ds, k)
        dk = dot(ds, q, TN)
        halves.append([x.reshape(frames, group, HEAD) for x in (dq, dk, dv, attended)])
    for t in range(4):
        x = jnp.concatenate([h[t] for h in halves], 1).astype(BF16)
        back[:, t] = x


def norm_back(raw, incoming):
    parts = []
    for h in range(raw.shape[1] // HEAD):
        x = raw[:, h * HEAD : (h + 1) * HEAD]
        u = incoming[:, h * HEAD : (h + 1) * HEAD].astype(F32)
        r = lax.rsqrt(jnp.mean(x * x, -1, keepdims=True) + EPS)
        parts.append(r * u - x * (r * r * r * jnp.mean(x * u, -1, keepdims=True)))
    return jnp.concatenate(parts, 1).astype(BF16)


def adapter_terms(rank, scale, back, raw, low, up, hidden_t, joined, low_grad, sections):
    n = up.shape[1]
    heads = n // HEAD
    dq = norm_back(raw[:, :n], unpack_blocks(back, 0, heads))
    dk = norm_back(raw[:, n:], unpack_blocks(back, 1, heads))
    dv = unpack_blocks(back, 2, heads)
    joined[:, :n] = dq
    joined[:, n : 2 * n] = dk
    joined[:, 2 * n :] = dv
    up_q, up_v = split_up(up[...], rank)
    lg = (dot(dq, up_q, NT) + dot(dv, up_v, NT)).astype(BF16)
    low_grad[...] = lg
    down = dot(hidden_t[...], jnp.concatenate([lg, lg], 1)) * scale
    low_rows = low[...]
    row = lax.broadcasted_iota(jnp.int32, (2 * rank, n), 0)
    up_grad = jnp.where(row < rank, dot(low_rows, dq, TN), dot(low_rows, dv, TN)) * scale
    parts = sections.shape[0]
    per, half = down.shape[0] // parts, down.shape[0] // parts // 2
    own = 2 * rank // parts
    left = lax.broadcasted_iota(jnp.int32, (half, HEAD), 1) < 2 * rank
    for d in range(parts):
        sections[d, :half] = jnp.where(
            left, down[d * per : d * per + half], down[d * per + half : (d + 1) * per]
        ).astype(BF16)
        sections[d, half:] = jnp.concatenate(
            [up_grad[d * own : (d + 1) * own, h * HEAD : (h + 1) * HEAD] for h in range(heads)], 0
        ).astype(BF16)


def finish(
    steps, grad_scale, joined, low_grad, back, w, out_t, x, mean, rstd, mod, upstream,
    tokens_grad, mixed, mod_rows, held, sums, s1, s2, attended,
):
    j = pl.program_id(0)
    width = w.shape[0]
    total = steps * width
    n3 = joined.shape[1]
    at = pl.ds(pl.multiple_of(j * width, width), width)

    @pl.when(j == 0)
    def _():
        s1[...] = jnp.zeros_like(s1)
        s2[...] = jnp.zeros_like(s2)
        attended[...] = unpack_blocks(back, 3, out_t.shape[2] // HEAD)

    hg = dot(joined[...], w[:, :n3], NT) + dot(low_grad[...], w[:, n3:], NT)
    out = dot(attended[...], out_t[...].reshape(-1, out_t.shape[2]), NT)
    values = x[:, at].astype(F32)
    up_rows = upstream[:, at].astype(F32)
    mixed[:, at] = (values + mod[2:3, at] * out).astype(BF16)
    normed = (values - mean[...]) * rstd[...]
    ng = hg * (1.0 + mod[1:2, at])
    sums[0:1, at] = jnp.sum(hg, 0, keepdims=True) * grad_scale
    sums[1:2, at] = jnp.sum(hg * normed, 0, keepdims=True) * grad_scale
    sums[2:3, at] = jnp.sum(up_rows * out, 0, keepdims=True) * grad_scale
    held[:, at] = ng
    s1[...] += jnp.sum(ng, -1, keepdims=True)
    s2[...] += jnp.sum(ng * normed, -1, keepdims=True)

    @pl.when(j == steps - 1)
    def _():
        m1 = s1[...] * (1.0 / total)
        m2 = s2[...] * (1.0 / total)
        for i in range(steps):
            c = slice(i * width, (i + 1) * width)
            nrm = (x[:, c].astype(F32) - mean[...]) * rstd[...]
            tokens_grad[:, c] = (
                upstream[:, c].astype(F32) + rstd[...] * (held[:, c] - m1 - nrm * m2)
            ).astype(BF16)
        tiles = total // HEAD
        for r in range(3):
            for i in range(tiles):
                mod_rows[r * tiles + i : r * tiles + i + 1, :] = sums[
                    r : r + 1, i * HEAD : (i + 1) * HEAD
                ]


def spread(rows_a, rows_b, arrived, mod_rows, both):
    share = jnp.sum(arrived[...].astype(F32), 0)
    for j in range(both.shape[0]):
        parts = []
        for rows, src in ((rows_a, share), (rows_b, mod_rows)):
            if (j + 1) * rows <= src.shape[0]:
                parts.append(src[j * rows : (j + 1) * rows, :])
            else:
                parts.append(jnp.zeros((rows, HEAD), F32))
        left = both.shape[1] - rows_a - rows_b
        if left:
            parts.append(jnp.zeros((left, HEAD), F32))
        both[j] = jnp.concatenate(parts, 0).astype(BF16)


def summed(arrived, out):
    total = jnp.sum(arrived[...].astype(F32), 0).astype(BF16)
    out[...] = jnp.broadcast_to(total[None], out.shape)


def collected(rows_a, rows_b, shares, down_t, up_grad, mod_grad):
    values = shares[...].astype(F32)
    half = down_t.shape[1] // 2
    cols = down_t.shape[0]
    own = up_grad.shape[0]
    blocks = half // rows_a
    a = jnp.concatenate([values[j, :rows_a] for j in range(blocks)], 0)
    down = jnp.concatenate([a[:, :cols], a[:, cols:]], 0)
    down_t[...] = down.T
    for h in range(up_grad.shape[1] // HEAD):
        first = half + h * own
        j, r = first // rows_a, first % rows_a
        up_grad[:, h * HEAD : (h + 1) * HEAD] = values[j, r : r + own]
    tiles = mod_grad.shape[2] // HEAD
    for i in range(3 * tiles):
        j, r = i // rows_b, rows_a + i % rows_b
        mod_grad[i // tiles, :, (i % tiles) * HEAD : (i % tiles + 1) * HEAD] = values[j, r : r + 1]


def per_device(tokens, modulation, qkv, out_w, down_w, up_w, output_gradient):
    dp, ctx = lax.axis_size("dp"), lax.axis_size("ctx")
    m, width = tokens.shape[2], tokens.shape[3]
    n = up_w.shape[1]
    heads = n // HEAD
    rank = down_w.shape[1] // 2
    positions = m // (ctx // heads)
    mod = modulation[0]
    grad_scale = (dp * ctx * m) ** (-0.5)
    own = width // dp

    w = lax.all_gather(jnp.concatenate([qkv, down_w], 1), "dp", axis=0, tiled=True)
    small = jnp.concatenate([out_w.T, up_w, jnp.zeros((8 - up_w.shape[0] % 8, n), BF16)], 0)
    out_up = lax.all_to_all(
        jnp.broadcast_to(small[None], (dp, *small.shape)), "dp", 0, 0, tiled=True
    )
    up = out_up[:, own : own + up_w.shape[0]].reshape(2 * rank, n)

    x = tokens.reshape(m, width)
    upstream = output_gradient.reshape(m, width)
    hidden, hidden_t, branch_grad, mean, rstd = call(
        normalize,
        (
            shape((m, width), BF16),
            shape((width, m), BF16),
            shape((m, width), BF16),
            shape((m, 1), F32),
            shape((m, 1), F32),
        ),
        flops=20 * m * width,
        moved=10 * m * width,
    )(x, mod, upstream)

    per = 4
    steps = dp // per
    grad_sent = call(
        functools.partial(attended_grads, steps),
        shape((ctx, 1, positions, HEAD), BF16),
        grid=(steps,),
        in_specs=[
            pl.BlockSpec((m, per * own), lambda k: (0, k)),
            pl.BlockSpec((per, own, n), lambda k: (k, 0, 0)),
        ],
        out_specs=whole(ctx, 1, positions, HEAD),
        scratch=[pltpu.VMEM((m, n), F32)],
        flops=2 * m * width * n,
        moved=2 * width * n,
    )(branch_grad, out_up)
    grad_in = lax.all_to_all(grad_sent, "ctx", 0, 0, tiled=True)

    steps, kb = 6, width // 6
    cols = w.shape[1]
    sent, raw, low = call(
        functools.partial(projections, steps, rank),
        (
            shape((ctx, 3, positions, HEAD), BF16),
            shape((m, 2 * n), F32),
            shape((m, 2 * rank), BF16),
        ),
        grid=(steps,),
        in_specs=[
            pl.BlockSpec((m, kb), lambda k: (0, k)),
            pl.BlockSpec((kb, cols), lambda k: (k, 0)),
            whole(2 * rank, n),
        ],
        out_specs=(whole(ctx, 3, positions, HEAD), whole(m, 2 * n), whole(m, 2 * rank)),
        scratch=[pltpu.VMEM((m, cols), F32)],
        flops=2 * m * width * cols,
        moved=2 * width * cols,
    )(hidden, w, up)
    rows_in = lax.all_to_all(sent, "ctx", 0, 0, tiled=True)

    back_sent = call(
        attention,
        shape((ctx, 4, positions, HEAD), BF16),
        flops=7 * 2 * 2 * 256 * 256 * 128,
        moved=8 * m * n * 2,
    )(rows_in, grad_in)
    back = lax.all_to_all(back_sent, "ctx", 0, 0, tiled=True)

    own_rows = own // 2 + (2 * rank // dp) * heads
    joined, low_grad, sections = call(
        functools.partial(adapter_terms, rank, grad_scale),
        (
            shape((m, 3 * n), BF16),
            shape((m, 2 * rank), BF16),
            shape((dp, own_rows, HEAD), BF16),
        ),
        flops=2 * m * width * HEAD + 8 * m * n * 64,
        moved=m * width * 2 + m * n * 20,
    )(back, raw, low, up, hidden_t)
    arrived = lax.all_to_all(sections, "dp", 0, 0, tiled=True)

    per = 2
    steps, cb = dp // per, per * own
    tokens_grad, mixed, mod_rows = call(
        functools.partial(finish, steps, grad_scale),
        (
            shape((m, width), BF16),
            shape((m, width), BF16),
            shape((3 * width // HEAD, HEAD), F32),
        ),
        grid=(steps,),
        in_specs=[
            whole(m, 3 * n),
            whole(m, 2 * rank),
            whole(ctx, 4, positions, HEAD),
            pl.BlockSpec((cb, cols), lambda k: (k, 0)),
            pl.BlockSpec((per, own, n), lambda k: (k, 0, 0)),
            whole(m, width),
            whole(m, 1),
            whole(m, 1),
            whole(3, width),
            whole(m, width),
        ],
        out_specs=(whole(m, width), whole(m, width), whole(3 * width // HEAD, HEAD)),
        scratch=[
            pltpu.VMEM((m, width), F32),
            pltpu.VMEM((3, width), F32),
            pltpu.VMEM((m, 1), F32),
            pltpu.VMEM((m, 1), F32),
            pltpu.VMEM((m, n), BF16),
        ],
        flops=2 * m * width * (cols + n),
        moved=2 * width * (cols + n) + 8 * m * width,
    )(joined, low_grad, back, w, out_up, x, mean, rstd, mod, upstream)

    rows_a = -(-own_rows // ctx)
    rows_b = -(-mod_rows.shape[0] // ctx)
    rows = 8 * -(-(rows_a + rows_b) // 8)
    both = call(
        functools.partial(spread, rows_a, rows_b), shape((ctx, rows, HEAD), BF16), moved=2**19
    )(arrived, mod_rows)
    part = call(summed, shape((ctx, rows, HEAD), BF16), moved=2**17)(
        lax.all_to_all(both, "ctx", 0, 0, tiled=True)
    )
    down_t, up_grad, mod_grad = call(
        functools.partial(collected, rows_a, rows_b),
        (
            shape((2 * rank, own), F32),
            shape((2 * rank // dp, n), F32),
            shape((3, 1, width), F32),
        ),
        moved=2**18,
    )(lax.all_to_all(part, "ctx", 0, 0, tiled=True))
    return (
        mixed.reshape(tokens.shape),
        tokens_grad.reshape(tokens.shape),
        mod_grad.reshape(1, 3, width),
        down_t.T,
        up_grad,
    )


def solution(mesh):
    return jax.shard_map(
        per_device,
        mesh=mesh,
        in_specs=(
            P("dp", "ctx", None, None),
            P("dp", None, None),
            P("dp", None),
            P(None, "dp"),
            P("dp", None),
            P("dp", None),
            P("dp", "ctx", None, None),
        ),
        out_specs=(
            P("dp", "ctx", None, None),
            P("dp", "ctx", None, None),
            P("dp", None, None),
            P("dp", None),
            P("dp", None),
        ),
        check_vma=False,
    )
```

```python
import functools

import jax
import jax.numpy as jnp
from jax import lax
from jax.experimental import pallas as pl
from jax.experimental.pallas import tpu as pltpu
from jax.sharding import PartitionSpec as P

HEAD = 128
EPS = 1e-06
F32 = jnp.float32
BF16 = jnp.bfloat16
NT = (((1,), (1,)), ((), ()))
TN = (((0,), (0,)), ((), ()))
NN = (((1,), (0,)), ((), ()))


def dot(a, b, dims=NN):
    return lax.dot_general(a, b, dims, preferred_element_type=F32)


def call(body, out_shape, grid=None, in_specs=None, out_specs=None, scratch=(), flops=0, moved=0, vmem=60):
    extra = {} if grid is None else {"grid": grid, "in_specs": in_specs, "out_specs": out_specs}
    return pl.pallas_call(
        body,
        out_shape=out_shape,
        scratch_shapes=list(scratch),
        compiler_params=pltpu.CompilerParams(vmem_limit_bytes=vmem * 2**20),
        cost_estimate=pl.CostEstimate(flops=flops, bytes_accessed=moved, transcendentals=0),
        **extra,
    )


def shape(dims, dtype):
    return jax.ShapeDtypeStruct(dims, dtype)


def whole(*dims):
    return pl.BlockSpec(dims, lambda i: (0,) * len(dims))


def split_up(up, rank):
    row = lax.broadcasted_iota(jnp.int32, up.shape, 0)
    zero = jnp.zeros_like(up)
    return jnp.where(row < rank, up, zero), jnp.where(row < rank, zero, up)


def unpack_blocks(ref, t, heads):
    groups = ref.shape[0] // heads
    columns = [
        jnp.concatenate([ref[g * heads + h, t] for g in range(groups)], 0) for h in range(heads)
    ]
    return jnp.concatenate(columns, 1)


def normalize(x, mod, upstream, hidden, hidden_t, branch_grad, mean_out, rstd_out):
    values = x[...].astype(F32)
    mean = jnp.mean(values, -1, keepdims=True)
    center = values - mean
    rstd = lax.rsqrt(jnp.mean(center * center, -1, keepdims=True) + EPS)
    mean_out[...] = mean
    rstd_out[...] = rstd
    state = (center * rstd * (1.0 + mod[1]) + mod[0]).astype(BF16)
    hidden[...] = state
    hidden_t[...] = state.T
    branch_grad[...] = (upstream[...].astype(F32) * mod[2]).astype(BF16)


def pack(qkv, out_t, down_t, packed):
    n, k = out_t.shape[1], qkv.shape[1]
    packed[:, :k] = qkv[...]
    packed[:, k : k + n] = out_t[...]
    packed[:, k + n :] = down_t[...].astype(F32).T.astype(BF16)


def head_scales(x):
    parts = []
    for h in range(x.shape[1] // HEAD):
        v = x[:, h * HEAD : (h + 1) * HEAD]
        parts.append(lax.rsqrt(jnp.mean(v * v, -1, keepdims=True) + EPS))
    return parts


def projections(steps, rank, hidden, branch_grad, w, up, sent, raw, low_out, acc):
    k = pl.program_id(0)
    n = up.shape[1]

    @pl.when(k == 0)
    def _():
        acc[...] = jnp.zeros_like(acc)

    acc[:, : 3 * n] += dot(hidden[...], w[:, : 3 * n])
    acc[:, 3 * n : 4 * n] += dot(branch_grad[...], w[:, 3 * n : 4 * n])
    acc[:, 4 * n :] += dot(hidden[...], w[:, 4 * n :])

    @pl.when(k == steps - 1)
    def _():
        heads = n // HEAD
        up_q, up_v = split_up(up[...], rank)
        low_rows = acc[:, 4 * n :].astype(BF16)
        low_out[...] = low_rows
        q = acc[:, :n] + dot(low_rows, up_q)
        kk = acc[:, n : 2 * n]
        v = acc[:, 2 * n : 3 * n] + dot(low_rows, up_v)
        raw[:, :n] = q
        raw[:, n:] = kk
        positions = sent.shape[2]
        for t, x in enumerate((q, kk, v, acc[:, 3 * n : 4 * n])):
            scales = head_scales(x) if t < 2 else None
            for h in range(heads):
                rows = x[:, h * HEAD : (h + 1) * HEAD]
                if t < 2:
                    rows = rows * scales[h]
                rows = rows.astype(BF16)
                for g in range(x.shape[0] // positions):
                    sent[g * heads + h, t] = rows[g * positions : (g + 1) * positions]


def attention(rows_in, back):
    frames, _, positions, _ = rows_in.shape
    group = 8
    total = frames * group
    row = lax.broadcasted_iota(jnp.int32, (total, total), 0) % group
    col = lax.broadcasted_iota(jnp.int32, (total, total), 1) % group
    same = row == col
    scale = HEAD**-0.5
    halves = []
    for p in range(positions // group):

        def rows_of(ref, t):
            x = ref[:, t].astype(F32)[:, p * group : (p + 1) * group]
            return x.reshape(total, HEAD).astype(BF16)

        q, k, v, g = (rows_of(rows_in, t) for t in range(4))
        s = dot(q, k, NT) * scale
        e = jnp.where(same, jnp.exp(s), 0.0)
        a = e / jnp.sum(e, -1, keepdims=True)
        low = a.astype(BF16)
        attended = dot(low, v)
        dp = dot(g, v, NT)
        dv = dot(low, g, TN)
        inner = jnp.sum(a * dp, -1, keepdims=True)
        ds = (a * (dp - inner) * scale).astype(BF16)
        dq = dot(ds, k)
        dk = dot(ds, q, TN)
        halves.append([x.reshape(frames, group, HEAD) for x in (dq, dk, dv, attended)])
    for t in range(4):
        x = jnp.concatenate([h[t] for h in halves], 1).astype(BF16)
        back[:, t] = x


def norm_back(raw, incoming):
    parts = []
    for h in range(raw.shape[1] // HEAD):
        x = raw[:, h * HEAD : (h + 1) * HEAD]
        u = incoming[:, h * HEAD : (h + 1) * HEAD].astype(F32)
        r = lax.rsqrt(jnp.mean(x * x, -1, keepdims=True) + EPS)
        parts.append(r * u - x * (r * r * r * jnp.mean(x * u, -1, keepdims=True)))
    return jnp.concatenate(parts, 1).astype(BF16)


def adapter_terms(rank, scale, back, raw, low, up, hidden_t, joined, low_grad, sections):
    n = up.shape[1]
    heads = n // HEAD
    dq = norm_back(raw[:, :n], unpack_blocks(back, 0, heads))
    dk = norm_back(raw[:, n:], unpack_blocks(back, 1, heads))
    dv = unpack_blocks(back, 2, heads)
    joined[:, :n] = dq
    joined[:, n : 2 * n] = dk
    joined[:, 2 * n :] = dv
    up_q, up_v = split_up(up[...], rank)
    lg = (dot(dq, up_q, NT) + dot(dv, up_v, NT)).astype(BF16)
    low_grad[...] = lg
    down = dot(hidden_t[...], jnp.concatenate([lg, lg], 1)) * scale
    low_rows = low[...]
    row = lax.broadcasted_iota(jnp.int32, (2 * rank, n), 0)
    up_grad = jnp.where(row < rank, dot(low_rows, dq, TN), dot(low_rows, dv, TN)) * scale
    parts = sections.shape[0]
    per, half = down.shape[0] // parts, down.shape[0] // parts // 2
    own = 2 * rank // parts
    left = lax.broadcasted_iota(jnp.int32, (half, HEAD), 1) < 2 * rank
    for d in range(parts):
        sections[d, :half] = jnp.where(
            left, down[d * per : d * per + half], down[d * per + half : (d + 1) * per]
        ).astype(BF16)
        sections[d, half:] = jnp.concatenate(
            [up_grad[d * own : (d + 1) * own, h * HEAD : (h + 1) * HEAD] for h in range(heads)], 0
        ).astype(BF16)


def finish(
    steps, grad_scale, joined, low_grad, back, w, x, mean, rstd, mod, upstream,
    tokens_grad, mixed, mod_rows, held, sums, s1, s2, attended,
):
    j = pl.program_id(0)
    width = w.shape[0]
    total = steps * width
    n3 = joined.shape[1]
    at = pl.ds(pl.multiple_of(j * width, width), width)

    @pl.when(j == 0)
    def _():
        s1[...] = jnp.zeros_like(s1)
        s2[...] = jnp.zeros_like(s2)
        attended[...] = unpack_blocks(back, 3, n3 // 3 // HEAD)

    n4 = n3 + n3 // 3
    hg = dot(joined[...], w[:, :n3], NT) + dot(low_grad[...], w[:, n4:], NT)
    out = dot(attended[...], w[:, n3:n4], NT)
    values = x[:, at].astype(F32)
    up_rows = upstream[:, at].astype(F32)
    mixed[:, at] = (values + mod[2, :, at] * out).astype(BF16)
    normed = (values - mean[...]) * rstd[...]
    ng = hg * (1.0 + mod[1, :, at])
    sums[0:1, at] = jnp.sum(hg, 0, keepdims=True) * grad_scale
    sums[1:2, at] = jnp.sum(hg * normed, 0, keepdims=True) * grad_scale
    sums[2:3, at] = jnp.sum(up_rows * out, 0, keepdims=True) * grad_scale
    held[:, at] = ng
    s1[...] += jnp.sum(ng, -1, keepdims=True)
    s2[...] += jnp.sum(ng * normed, -1, keepdims=True)

    @pl.when(j == steps - 1)
    def _():
        m1 = s1[...] * (1.0 / total)
        m2 = s2[...] * (1.0 / total)
        for i in range(steps):
            c = slice(i * width, (i + 1) * width)
            nrm = (x[:, c].astype(F32) - mean[...]) * rstd[...]
            tokens_grad[:, c] = (
                upstream[:, c].astype(F32) + rstd[...] * (held[:, c] - m1 - nrm * m2)
            ).astype(BF16)
        tiles = total // HEAD
        for r in range(3):
            for i in range(tiles):
                mod_rows[r * tiles + i : r * tiles + i + 1, :] = sums[
                    r : r + 1, i * HEAD : (i + 1) * HEAD
                ]


def spread(rows_a, rows_b, arrived, mod_rows, both):
    share = jnp.sum(arrived[...].astype(F32), 0)
    for j in range(both.shape[0]):
        parts = []
        for rows, src in ((rows_a, share), (rows_b, mod_rows)):
            if (j + 1) * rows <= src.shape[0]:
                parts.append(src[j * rows : (j + 1) * rows, :])
            else:
                parts.append(jnp.zeros((rows, HEAD), F32))
        left = both.shape[1] - rows_a - rows_b
        if left:
            parts.append(jnp.zeros((left, HEAD), F32))
        both[j] = jnp.concatenate(parts, 0).astype(BF16)


def summed(arrived, out):
    total = jnp.sum(arrived[...].astype(F32), 0).astype(BF16)
    out[...] = jnp.broadcast_to(total[None], out.shape)


def collected(rows_a, rows_b, shares, down_t, up_grad, mod_grad):
    values = shares[...].astype(F32)
    half = down_t.shape[1] // 2
    cols = down_t.shape[0]
    own = up_grad.shape[0]
    blocks = half // rows_a
    a = jnp.concatenate([values[j, :rows_a] for j in range(blocks)], 0)
    down = jnp.concatenate([a[:, :cols], a[:, cols:]], 0)
    down_t[...] = down.T
    for h in range(up_grad.shape[1] // HEAD):
        first = half + h * own
        j, r = first // rows_a, first % rows_a
        up_grad[:, h * HEAD : (h + 1) * HEAD] = values[j, r : r + own]
    tiles = mod_grad.shape[2] // HEAD
    for i in range(3 * tiles):
        j, r = i // rows_b, rows_a + i % rows_b
        mod_grad[i // tiles, :, (i % tiles) * HEAD : (i % tiles + 1) * HEAD] = values[j, r : r + 1]


def per_device(tokens, modulation, qkv, out_w, down_w, up_w, output_gradient):
    dp, ctx = lax.axis_size("dp"), lax.axis_size("ctx")
    m, width = tokens.shape[2], tokens.shape[3]
    n = up_w.shape[1]
    heads = n // HEAD
    rank = down_w.shape[1] // 2
    positions = m // (ctx // heads)
    mod = modulation.transpose(1, 0, 2)
    grad_scale = (dp * ctx * m) ** (-0.5)
    own = width // dp

    cols = 4 * n + 2 * rank
    packed = call(pack, shape((own, cols), BF16), moved=4 * own * cols)(qkv, out_w.T, down_w.T)
    w = lax.all_gather(packed, "dp", axis=0, tiled=True)
    up = lax.all_to_all(
        jnp.broadcast_to(up_w[None], (dp, *up_w.shape)), "dp", 0, 0, tiled=True
    ).reshape(2 * rank, n)

    x = tokens.reshape(m, width)
    upstream = output_gradient.reshape(m, width)
    hidden, hidden_t, branch_grad, mean, rstd = call(
        normalize,
        (
            shape((m, width), BF16),
            shape((width, m), BF16),
            shape((m, width), BF16),
            shape((m, 1), F32),
            shape((m, 1), F32),
        ),
        flops=20 * m * width,
        moved=10 * m * width,
    )(x, mod, upstream)

    steps, kb = 6, width // 6
    sent, raw, low = call(
        functools.partial(projections, steps, rank),
        (
            shape((ctx, 4, positions, HEAD), BF16),
            shape((m, 2 * n), F32),
            shape((m, 2 * rank), BF16),
        ),
        grid=(steps,),
        in_specs=[
            pl.BlockSpec((m, kb), lambda k: (0, k)),
            pl.BlockSpec((m, kb), lambda k: (0, k)),
            pl.BlockSpec((kb, cols), lambda k: (k, 0)),
            whole(2 * rank, n),
        ],
        out_specs=(whole(ctx, 4, positions, HEAD), whole(m, 2 * n), whole(m, 2 * rank)),
        scratch=[pltpu.VMEM((m, cols), F32)],
        flops=2 * m * width * cols,
        moved=2 * width * cols,
    )(hidden, branch_grad, w, up)
    rows_in = lax.all_to_all(sent, "ctx", 0, 0, tiled=True)

    back_sent = call(
        attention,
        shape((ctx, 4, positions, HEAD), BF16),
        flops=7 * 2 * 2 * 256 * 256 * 128,
        moved=8 * m * n * 2,
        vmem=16,
    )(rows_in)
    back = lax.all_to_all(back_sent, "ctx", 0, 0, tiled=True)

    own_rows = own // 2 + (2 * rank // dp) * heads
    joined, low_grad, sections = call(
        functools.partial(adapter_terms, rank, grad_scale),
        (
            shape((m, 3 * n), BF16),
            shape((m, 2 * rank), BF16),
            shape((dp, own_rows, HEAD), BF16),
        ),
        flops=2 * m * width * HEAD + 8 * m * n * 64,
        moved=m * width * 2 + m * n * 20,
    )(back, raw, low, up, hidden_t)
    arrived = lax.all_to_all(sections, "dp", 0, 0, tiled=True)

    per = 2
    steps, cb = dp // per, per * own
    tokens_grad, mixed, mod_rows = call(
        functools.partial(finish, steps, grad_scale),
        (
            shape((m, width), BF16),
            shape((m, width), BF16),
            shape((3 * width // HEAD, HEAD), F32),
        ),
        grid=(steps,),
        in_specs=[
            whole(m, 3 * n),
            whole(m, 2 * rank),
            whole(ctx, 4, positions, HEAD),
            pl.BlockSpec((cb, cols), lambda k: (k, 0)),
            whole(m, width),
            whole(m, 1),
            whole(m, 1),
            whole(3, 1, width),
            whole(m, width),
        ],
        out_specs=(whole(m, width), whole(m, width), whole(3 * width // HEAD, HEAD)),
        scratch=[
            pltpu.VMEM((m, width), F32),
            pltpu.VMEM((3, width), F32),
            pltpu.VMEM((m, 1), F32),
            pltpu.VMEM((m, 1), F32),
            pltpu.VMEM((m, n), BF16),
        ],
        flops=2 * m * width * cols,
        moved=2 * width * cols + 8 * m * width,
    )(joined, low_grad, back, w, x, mean, rstd, mod, upstream)

    rows_a = -(-own_rows // ctx)
    rows_b = -(-mod_rows.shape[0] // ctx)
    rows = 8 * -(-(rows_a + rows_b) // 8)
    both = call(
        functools.partial(spread, rows_a, rows_b), shape((ctx, rows, HEAD), BF16), moved=2**19, vmem=8
    )(arrived, mod_rows)
    part = call(summed, shape((ctx, rows, HEAD), BF16), moved=2**17, vmem=8)(
        lax.all_to_all(both, "ctx", 0, 0, tiled=True)
    )
    down_t, up_grad, mod_grad = call(
        functools.partial(collected, rows_a, rows_b),
        (
            shape((2 * rank, own), F32),
            shape((2 * rank // dp, n), F32),
            shape((3, 1, width), F32),
        ),
        moved=2**18,
        vmem=8,
    )(lax.all_to_all(part, "ctx", 0, 0, tiled=True))
    return (
        mixed.reshape(tokens.shape),
        tokens_grad.reshape(tokens.shape),
        mod_grad.reshape(1, 3, width),
        down_t.T,
        up_grad,
    )


def solution(mesh):
    return jax.shard_map(
        per_device,
        mesh=mesh,
        in_specs=(
            P("dp", "ctx", None, None),
            P("dp", None, None),
            P("dp", None),
            P(None, "dp"),
            P("dp", None),
            P("dp", None),
            P("dp", "ctx", None, None),
        ),
        out_specs=(
            P("dp", "ctx", None, None),
            P("dp", "ctx", None, None),
            P("dp", None, None),
            P("dp", None),
            P("dp", None),
        ),
        check_vma=False,
    )
```

```python
import functools

import jax
import jax.numpy as jnp
from jax import lax
from jax.experimental import pallas as pl
from jax.experimental.pallas import tpu as pltpu
from jax.sharding import Mesh
from jax.sharding import PartitionSpec as P

HEAD = 128
EPS = 1e-06
F32 = jnp.float32
BF16 = jnp.bfloat16
NT = (((1,), (1,)), ((), ()))
TN = (((0,), (0,)), ((), ()))
CTX = ("yh", "far", "near")
NN = (((1,), (0,)), ((), ()))


def dot(a, b, dims=NN):
    return lax.dot_general(a, b, dims, preferred_element_type=F32)


def call(body, out_shape, grid=None, in_specs=None, out_specs=None, scratch=(), flops=0, moved=0, vmem=60):
    extra = {} if grid is None else {"grid": grid, "in_specs": in_specs, "out_specs": out_specs}
    return pl.pallas_call(
        body,
        out_shape=out_shape,
        scratch_shapes=list(scratch),
        compiler_params=pltpu.CompilerParams(vmem_limit_bytes=vmem * 2**20),
        cost_estimate=pl.CostEstimate(flops=flops, bytes_accessed=moved, transcendentals=0),
        **extra,
    )


def shape(dims, dtype):
    return jax.ShapeDtypeStruct(dims, dtype)


def whole(*dims):
    return pl.BlockSpec(dims, lambda i: (0,) * len(dims))


def split_up(up, rank):
    row = lax.broadcasted_iota(jnp.int32, up.shape, 0)
    zero = jnp.zeros_like(up)
    return jnp.where(row < rank, up, zero), jnp.where(row < rank, zero, up)


def unpack_blocks(ref, t, heads):
    groups = ref.shape[0] // heads
    columns = [
        jnp.concatenate([ref[g * heads + h, t] for g in range(groups)], 0) for h in range(heads)
    ]
    return jnp.concatenate(columns, 1)


def normalize(x, mod, upstream, hidden, hidden_t, branch_grad, mean_out, rstd_out):
    values = x[...].astype(F32)
    mean = jnp.mean(values, -1, keepdims=True)
    center = values - mean
    rstd = lax.rsqrt(jnp.mean(center * center, -1, keepdims=True) + EPS)
    mean_out[...] = mean
    rstd_out[...] = rstd
    state = (center * rstd * (1.0 + mod[1]) + mod[0]).astype(BF16)
    hidden[...] = state
    hidden_t[...] = state.T
    branch_grad[...] = (upstream[...].astype(F32) * mod[2]).astype(BF16)


def pack(qkv, out_t, down_t, packed):
    n, k = out_t.shape[1], qkv.shape[1]
    packed[:, :k] = qkv[...]
    packed[:, k : k + n] = out_t[...]
    down = down_t[...].astype(F32).T
    packed[:, k + n :] = jnp.concatenate([down, jnp.zeros_like(down)], 1).astype(BF16)


def head_scales(x):
    parts = []
    for h in range(x.shape[1] // HEAD):
        v = x[:, h * HEAD : (h + 1) * HEAD]
        parts.append(lax.rsqrt(jnp.mean(v * v, -1, keepdims=True) + EPS))
    return parts


def projections(rank, hidden, branch_grad, w, w_down, up, sent, raw, low_out):
    t = pl.program_id(0)
    n = w.shape[1]
    heads = n // HEAD
    positions = sent.shape[2]

    def store(x, normed):
        scales = head_scales(x) if normed else None
        for h in range(heads):
            rows = x[:, h * HEAD : (h + 1) * HEAD]
            if normed:
                rows = rows * scales[h]
            rows = rows.astype(BF16)
            for g in range(x.shape[0] // positions):
                sent[g * heads + h, 0] = rows[g * positions : (g + 1) * positions]

    @pl.when(t == 0)
    def _():
        low_out[...] = dot(hidden[...], w_down[...])[:, : 2 * rank].astype(BF16)
        up_q, _ = split_up(up[...], rank)
        q = dot(hidden[...], w[...]) + dot(low_out[...], up_q)
        raw[:, :n] = q
        store(q, True)

    @pl.when(t == 1)
    def _():
        k = dot(hidden[...], w[...])
        raw[:, n:] = k
        store(k, True)

    @pl.when(t == 2)
    def _():
        _, up_v = split_up(up[...], rank)
        store(dot(hidden[...], w[...]) + dot(low_out[...], up_v), False)

    @pl.when(t == 3)
    def _():
        store(dot(branch_grad[...], w[...]), False)


def attention(rows_in, back):
    frames, _, positions, _ = rows_in.shape
    group = 8
    total = frames * group
    row = lax.broadcasted_iota(jnp.int32, (total, total), 0) % group
    col = lax.broadcasted_iota(jnp.int32, (total, total), 1) % group
    same = row == col
    scale = HEAD**-0.5
    halves = []
    for p in range(positions // group):

        def rows_of(ref, t):
            x = ref[:, t].astype(F32)[:, p * group : (p + 1) * group]
            return x.reshape(total, HEAD).astype(BF16)

        q, k, v, g = (rows_of(rows_in, t) for t in range(4))
        s = dot(q, k, NT) * scale
        e = jnp.where(same, jnp.exp(s), 0.0)
        a = e / jnp.sum(e, -1, keepdims=True)
        low = a.astype(BF16)
        attended = dot(low, v)
        dp = dot(g, v, NT)
        dv = dot(low, g, TN)
        inner = jnp.sum(a * dp, -1, keepdims=True)
        ds = (a * (dp - inner) * scale).astype(BF16)
        dq = dot(ds, k)
        dk = dot(ds, q, TN)
        halves.append([x.reshape(frames, group, HEAD) for x in (dq, dk, dv, attended)])
    for t in range(4):
        x = jnp.concatenate([h[t] for h in halves], 1).astype(BF16)
        back[:, t] = x


def norm_back(raw, incoming):
    parts = []
    for h in range(raw.shape[1] // HEAD):
        x = raw[:, h * HEAD : (h + 1) * HEAD]
        u = incoming[:, h * HEAD : (h + 1) * HEAD].astype(F32)
        r = lax.rsqrt(jnp.mean(x * x, -1, keepdims=True) + EPS)
        parts.append(r * u - x * (r * r * r * jnp.mean(x * u, -1, keepdims=True)))
    return jnp.concatenate(parts, 1).astype(BF16)


def adapter_terms(rank, scale, back, raw, low, up, hidden_t, joined, low_grad, sections):
    n = up.shape[1]
    heads = n // HEAD
    dq = norm_back(raw[:, :n], unpack_blocks(back, 0, heads))
    dk = norm_back(raw[:, n:], unpack_blocks(back, 1, heads))
    dv = unpack_blocks(back, 2, heads)
    joined[:, :n] = dq
    joined[:, n : 2 * n] = dk
    joined[:, 2 * n :] = dv
    up_q, up_v = split_up(up[...], rank)
    lg = (dot(dq, up_q, NT) + dot(dv, up_v, NT)).astype(BF16)
    low_grad[...] = lg
    down = dot(hidden_t[...], jnp.concatenate([lg, lg], 1)) * scale
    low_rows = low[...]
    row = lax.broadcasted_iota(jnp.int32, (2 * rank, n), 0)
    up_grad = jnp.where(row < rank, dot(low_rows, dq, TN), dot(low_rows, dv, TN)) * scale
    parts = sections.shape[0]
    per, half = down.shape[0] // parts, down.shape[0] // parts // 2
    own = 2 * rank // parts
    left = lax.broadcasted_iota(jnp.int32, (half, HEAD), 1) < 2 * rank
    for d in range(parts):
        sections[d, :half] = jnp.where(
            left, down[d * per : d * per + half], down[d * per + half : (d + 1) * per]
        ).astype(BF16)
        sections[d, half:] = jnp.concatenate(
            [up_grad[d * own : (d + 1) * own, h * HEAD : (h + 1) * HEAD] for h in range(heads)], 0
        ).astype(BF16)


def finish(
    steps, grad_scale, joined, low_grad, back, w, x, mean, rstd, mod, upstream,
    tokens_grad, mixed, mod_rows, held, sums, s1, s2, attended,
):
    j = pl.program_id(0)
    width = w.shape[0]
    total = steps * width
    n3 = joined.shape[1]
    at = pl.ds(pl.multiple_of(j * width, width), width)

    @pl.when(j == 0)
    def _():
        s1[...] = jnp.zeros_like(s1)
        s2[...] = jnp.zeros_like(s2)
        attended[...] = unpack_blocks(back, 3, n3 // 3 // HEAD)

    n4 = n3 + n3 // 3
    hg = dot(joined[...], w[:, :n3], NT) + dot(low_grad[...], w[:, n4 : n4 + low_grad.shape[1]], NT)
    out = dot(attended[...], w[:, n3:n4], NT)
    values = x[:, at].astype(F32)
    up_rows = upstream[:, at].astype(F32)
    mixed[:, at] = (values + mod[2, :, at] * out).astype(BF16)
    normed = (values - mean[...]) * rstd[...]
    ng = hg * (1.0 + mod[1, :, at])
    sums[0:1, at] = jnp.sum(hg, 0, keepdims=True) * grad_scale
    sums[1:2, at] = jnp.sum(hg * normed, 0, keepdims=True) * grad_scale
    sums[2:3, at] = jnp.sum(up_rows * out, 0, keepdims=True) * grad_scale
    held[:, at] = ng
    s1[...] += jnp.sum(ng, -1, keepdims=True)
    s2[...] += jnp.sum(ng * normed, -1, keepdims=True)

    @pl.when(j == steps - 1)
    def _():
        m1 = s1[...] * (1.0 / total)
        m2 = s2[...] * (1.0 / total)
        for i in range(steps):
            c = slice(i * width, (i + 1) * width)
            nrm = (x[:, c].astype(F32) - mean[...]) * rstd[...]
            tokens_grad[:, c] = (
                upstream[:, c].astype(F32) + rstd[...] * (held[:, c] - m1 - nrm * m2)
            ).astype(BF16)
        tiles = total // HEAD
        for r in range(3):
            for i in range(tiles):
                mod_rows[r * tiles + i : r * tiles + i + 1, :] = sums[
                    r : r + 1, i * HEAD : (i + 1) * HEAD
                ]


def spread(arrived, mod_rows, both):
    share = jnp.sum(arrived[...].astype(F32), 0).astype(BF16)
    rows = mod_rows[...].astype(BF16)
    parts = both.shape[0]
    rows_a, rows_b = share.shape[0] // parts, rows.shape[0] // parts
    pad = jnp.zeros((both.shape[1] - rows_a - rows_b, HEAD), F32)
    for j in range(parts):
        piece = jnp.concatenate(
            [
                share[j * rows_a : (j + 1) * rows_a].astype(F32),
                rows[j * rows_b : (j + 1) * rows_b].astype(F32),
                pad,
            ],
            0,
        )
        both[j] = piece.astype(BF16)


def summed(arrived, out):
    total = jnp.sum(arrived[...].astype(F32), 0).astype(BF16)
    out[...] = jnp.broadcast_to(total[None], out.shape)


def collected(rows_a, rows_b, shares, down_t, up_grad, mod_grad):
    values = shares[...].astype(F32)
    parts = values.shape[0]
    cols = down_t.shape[0]
    own = up_grad.shape[0]
    half = down_t.shape[1] // 2
    a = jnp.concatenate([values[j, :rows_a] for j in range(parts)], 0)
    b = jnp.concatenate([values[j, rows_a : rows_a + rows_b] for j in range(parts)], 0)
    down_t[...] = jnp.concatenate([a[:half, :cols], a[:half, cols:]], 0).T
    for h in range(up_grad.shape[1] // HEAD):
        up_grad[:, h * HEAD : (h + 1) * HEAD] = a[half + h * own : half + (h + 1) * own]
    tiles = mod_grad.shape[2] // HEAD
    for i in range(3 * tiles):
        mod_grad[i // tiles, :, (i % tiles) * HEAD : (i % tiles + 1) * HEAD] = b[i : i + 1]


def per_device(tokens, modulation, qkv, out_w, down_w, up_w, output_gradient):
    dp, ctx = lax.axis_size("dp"), lax.axis_size(CTX)
    m, width = tokens.shape[2], tokens.shape[3]
    n = up_w.shape[1]
    heads = n // HEAD
    rank = down_w.shape[1] // 2
    positions = m // (ctx // heads)
    mod = modulation.transpose(1, 0, 2)
    grad_scale = (dp * ctx * m) ** (-0.5)
    own = width // dp

    cols = 4 * n + HEAD
    packed = call(pack, shape((own, cols), BF16), moved=4 * own * cols)(qkv, out_w.T, down_w.T)
    w = lax.all_gather(packed, "dp", axis=0, tiled=True)
    up = lax.all_to_all(
        jnp.broadcast_to(up_w[None], (dp, *up_w.shape)), "dp", 0, 0, tiled=True
    ).reshape(2 * rank, n)

    x = tokens.reshape(m, width)
    upstream = output_gradient.reshape(m, width)
    hidden, hidden_t, branch_grad, mean, rstd = call(
        normalize,
        (
            shape((m, width), BF16),
            shape((width, m), BF16),
            shape((m, width), BF16),
            shape((m, 1), F32),
            shape((m, 1), F32),
        ),
        flops=20 * m * width,
        moved=10 * m * width,
    )(x, mod, upstream)

    sent, raw, low = call(
        functools.partial(projections, rank),
        (
            shape((ctx, 4, positions, HEAD), BF16),
            shape((m, 2 * n), F32),
            shape((m, 2 * rank), BF16),
        ),
        grid=(4,),
        in_specs=[
            whole(m, width),
            whole(m, width),
            pl.BlockSpec((width, n), lambda t: (0, t)),
            pl.BlockSpec((width, HEAD), lambda t: (0, 4 * n // HEAD)),
            whole(2 * rank, n),
        ],
        out_specs=(
            pl.BlockSpec((ctx, 1, positions, HEAD), lambda t: (0, t, 0, 0)),
            whole(m, 2 * n),
            whole(m, 2 * rank),
        ),
        flops=2 * m * width * cols,
        moved=2 * width * cols,
    )(hidden, branch_grad, w, w, up)
    rows_in = lax.all_to_all(sent, CTX, 0, 0, tiled=True)

    back_sent = call(
        attention,
        shape((ctx, 4, positions, HEAD), BF16),
        flops=7 * 2 * 2 * 256 * 256 * 128,
        moved=8 * m * n * 2,
        vmem=16,
    )(rows_in)
    back = lax.all_to_all(back_sent, CTX, 0, 0, tiled=True)

    own_rows = own // 2 + (2 * rank // dp) * heads
    joined, low_grad, sections = call(
        functools.partial(adapter_terms, rank, grad_scale),
        (
            shape((m, 3 * n), BF16),
            shape((m, 2 * rank), BF16),
            shape((dp, own_rows, HEAD), BF16),
        ),
        flops=2 * m * width * HEAD + 8 * m * n * 64,
        moved=m * width * 2 + m * n * 20,
    )(back, raw, low, up, hidden_t)
    arrived = lax.all_to_all(sections, "dp", 0, 0, tiled=True)

    per = 2
    steps, cb = dp // per, per * own
    tokens_grad, mixed, mod_rows = call(
        functools.partial(finish, steps, grad_scale),
        (
            shape((m, width), BF16),
            shape((m, width), BF16),
            shape((3 * width // HEAD, HEAD), F32),
        ),
        grid=(steps,),
        in_specs=[
            whole(m, 3 * n),
            whole(m, 2 * rank),
            whole(ctx, 4, positions, HEAD),
            pl.BlockSpec((cb, cols), lambda k: (k, 0)),
            whole(m, width),
            whole(m, 1),
            whole(m, 1),
            whole(3, 1, width),
            whole(m, width),
        ],
        out_specs=(whole(m, width), whole(m, width), whole(3 * width // HEAD, HEAD)),
        scratch=[
            pltpu.VMEM((m, width), F32),
            pltpu.VMEM((3, width), F32),
            pltpu.VMEM((m, 1), F32),
            pltpu.VMEM((m, 1), F32),
            pltpu.VMEM((m, n), BF16),
        ],
        flops=2 * m * width * cols,
        moved=2 * width * cols + 8 * m * width,
    )(joined, low_grad, back, w, x, mean, rstd, mod, upstream)

    near, far = lax.axis_size("near"), lax.axis_size("yh") * lax.axis_size("far")
    rows_a, rows_b = own_rows // near, mod_rows.shape[0] // near
    rows = 16 * -(-(rows_a + rows_b) // 16)
    both = call(spread, shape((near, rows, HEAD), BF16), moved=2**19, vmem=8)(arrived, mod_rows)
    part = call(summed, shape((far, rows, HEAD), BF16), moved=2**17, vmem=8)(
        lax.all_to_all(both, "near", 0, 0, tiled=True)
    )
    part = call(summed, shape((near, rows, HEAD), BF16), moved=2**17, vmem=8)(
        lax.all_to_all(part, ("yh", "far"), 0, 0, tiled=True)
    )
    down_t, up_grad, mod_grad = call(
        functools.partial(collected, rows_a, rows_b),
        (
            shape((2 * rank, own), F32),
            shape((2 * rank // dp, n), F32),
            shape((3, 1, width), F32),
        ),
        moved=2**18,
        vmem=8,
    )(lax.all_to_all(part, "near", 0, 0, tiled=True))
    return (
        mixed.reshape(tokens.shape),
        tokens_grad.reshape(tokens.shape),
        mod_grad.reshape(1, 3, width),
        down_t.T,
        up_grad,
    )


def solution(mesh):
    dp, ctx = mesh.devices.shape
    fine = Mesh(mesh.devices.reshape(dp, 2, ctx // 8, 4), ("dp", *CTX))
    return jax.shard_map(
        per_device,
        mesh=fine,
        in_specs=(
            P("dp", CTX, None, None),
            P("dp", None, None),
            P("dp", None),
            P(None, "dp"),
            P("dp", None),
            P("dp", None),
            P("dp", CTX, None, None),
        ),
        out_specs=(
            P("dp", CTX, None, None),
            P("dp", CTX, None, None),
            P("dp", None, None),
            P("dp", None),
            P("dp", None),
        ),
        check_vma=False,
    )
```

```python
import functools

import jax
import jax.numpy as jnp
from jax import lax
from jax.experimental import pallas as pl
from jax.experimental.pallas import tpu as pltpu
from jax.sharding import Mesh
from jax.sharding import PartitionSpec as P

HEAD = 128
EPS = 1e-06
F32 = jnp.float32
BF16 = jnp.bfloat16
NT = (((1,), (1,)), ((), ()))
TN = (((0,), (0,)), ((), ()))
CTX = ("yh", "far", "near")
NN = (((1,), (0,)), ((), ()))


def dot(a, b, dims=NN):
    return lax.dot_general(a, b, dims, preferred_element_type=F32)


def call(body, out_shape, grid=None, in_specs=None, out_specs=None, scratch=(), flops=0, moved=0, vmem=60):
    extra = {} if grid is None else {"grid": grid, "in_specs": in_specs, "out_specs": out_specs}
    return pl.pallas_call(
        body,
        out_shape=out_shape,
        scratch_shapes=list(scratch),
        compiler_params=pltpu.CompilerParams(vmem_limit_bytes=vmem * 2**20),
        cost_estimate=pl.CostEstimate(flops=flops, bytes_accessed=moved, transcendentals=0),
        **extra,
    )


def shape(dims, dtype):
    return jax.ShapeDtypeStruct(dims, dtype)


def whole(*dims):
    return pl.BlockSpec(dims, lambda i: (0,) * len(dims))


def split_up(up, rank):
    row = lax.broadcasted_iota(jnp.int32, up.shape, 0)
    zero = jnp.zeros_like(up)
    return jnp.where(row < rank, up, zero), jnp.where(row < rank, zero, up)


def unpack_blocks(ref, t, heads):
    groups, frames = ref.shape[0] // heads, ref.shape[1]
    columns = [
        jnp.concatenate(
            [ref[g * heads + h, f, t] for f in range(frames) for g in range(groups)], 0
        )
        for h in range(heads)
    ]
    return jnp.concatenate(columns, 1)


def normalize(x, mod, upstream, hidden, hidden_t, branch_grad, mean_out, rstd_out):
    values = x[...].astype(F32)
    mean = jnp.mean(values, -1, keepdims=True)
    center = values - mean
    rstd = lax.rsqrt(jnp.mean(center * center, -1, keepdims=True) + EPS)
    mean_out[...] = mean
    rstd_out[...] = rstd
    state = (center * rstd * (1.0 + mod[1]) + mod[0]).astype(BF16)
    hidden[...] = state
    hidden_t[...] = state.T
    branch_grad[...] = (upstream[...].astype(F32) * mod[2]).astype(BF16)


def pack(qkv, out_t, down_t, packed):
    n, k = out_t.shape[1], qkv.shape[1]
    packed[:, :k] = qkv[...]
    packed[:, k : k + n] = out_t[...]
    down = down_t[...].astype(F32).T
    packed[:, k + n :] = jnp.concatenate([down, jnp.zeros_like(down)], 1).astype(BF16)


def head_scales(x):
    parts = []
    for h in range(x.shape[1] // HEAD):
        v = x[:, h * HEAD : (h + 1) * HEAD]
        parts.append(lax.rsqrt(jnp.mean(v * v, -1, keepdims=True) + EPS))
    return parts


def projections(rank, hidden, branch_grad, w, w_down, up, sent, raw, low_out):
    t = pl.program_id(0)
    n = w.shape[1]
    heads = n // HEAD
    frames, positions = sent.shape[1], sent.shape[3]
    half = hidden.shape[0] // frames

    def store(x, normed):
        scales = head_scales(x) if normed else None
        for h in range(heads):
            rows = x[:, h * HEAD : (h + 1) * HEAD]
            if normed:
                rows = rows * scales[h]
            rows = rows.astype(BF16)
            for f in range(frames):
                for g in range(half // positions):
                    at = f * half + g * positions
                    sent[g * heads + h, f, 0] = rows[at : at + positions]

    @pl.when(t == 0)
    def _():
        low_out[...] = dot(hidden[...], w_down[...])[:, : 2 * rank].astype(BF16)
        up_q, _ = split_up(up[...], rank)
        q = dot(hidden[...], w[...]) + dot(low_out[...], up_q)
        raw[:, :n] = q
        store(q, True)

    @pl.when(t == 1)
    def _():
        k = dot(hidden[...], w[...])
        raw[:, n:] = k
        store(k, True)

    @pl.when(t == 2)
    def _():
        _, up_v = split_up(up[...], rank)
        store(dot(hidden[...], w[...]) + dot(low_out[...], up_v), False)

    @pl.when(t == 3)
    def _():
        store(dot(branch_grad[...], w[...]), False)


def attention(rows_in, back):
    frames, _, positions, _ = rows_in.shape
    group = 8
    total = frames * group
    row = lax.broadcasted_iota(jnp.int32, (total, total), 0) % group
    col = lax.broadcasted_iota(jnp.int32, (total, total), 1) % group
    same = row == col
    scale = HEAD**-0.5
    halves = []
    for p in range(positions // group):

        def rows_of(ref, t):
            x = ref[:, t].astype(F32)[:, p * group : (p + 1) * group]
            return x.reshape(total, HEAD).astype(BF16)

        q, k, v, g = (rows_of(rows_in, t) for t in range(4))
        s = dot(q, k, NT) * scale
        e = jnp.where(same, jnp.exp(s), 0.0)
        a = e / jnp.sum(e, -1, keepdims=True)
        low = a.astype(BF16)
        attended = dot(low, v)
        dp = dot(g, v, NT)
        dv = dot(low, g, TN)
        inner = jnp.sum(a * dp, -1, keepdims=True)
        ds = (a * (dp - inner) * scale).astype(BF16)
        dq = dot(ds, k)
        dk = dot(ds, q, TN)
        halves.append([x.reshape(frames, group, HEAD) for x in (dq, dk, dv, attended)])
    for t in range(4):
        x = jnp.concatenate([h[t] for h in halves], 1).astype(BF16)
        back[:, t] = x


def norm_back(raw, incoming):
    parts = []
    for h in range(raw.shape[1] // HEAD):
        x = raw[:, h * HEAD : (h + 1) * HEAD]
        u = incoming[:, h * HEAD : (h + 1) * HEAD].astype(F32)
        r = lax.rsqrt(jnp.mean(x * x, -1, keepdims=True) + EPS)
        parts.append(r * u - x * (r * r * r * jnp.mean(x * u, -1, keepdims=True)))
    return jnp.concatenate(parts, 1).astype(BF16)


def adapter_terms(rank, scale, back, raw, low, up, hidden_t, joined, low_grad, sections):
    n = up.shape[1]
    heads = n // HEAD
    dq = norm_back(raw[:, :n], unpack_blocks(back, 0, heads))
    dk = norm_back(raw[:, n:], unpack_blocks(back, 1, heads))
    dv = unpack_blocks(back, 2, heads)
    joined[:, :n] = dq
    joined[:, n : 2 * n] = dk
    joined[:, 2 * n :] = dv
    up_q, up_v = split_up(up[...], rank)
    lg = (dot(dq, up_q, NT) + dot(dv, up_v, NT)).astype(BF16)
    low_grad[...] = lg
    down = dot(hidden_t[...], jnp.concatenate([lg, lg], 1)) * scale
    low_rows = low[...]
    row = lax.broadcasted_iota(jnp.int32, (2 * rank, n), 0)
    up_grad = jnp.where(row < rank, dot(low_rows, dq, TN), dot(low_rows, dv, TN)) * scale
    parts = sections.shape[0]
    per, half = down.shape[0] // parts, down.shape[0] // parts // 2
    own = 2 * rank // parts
    left = lax.broadcasted_iota(jnp.int32, (half, HEAD), 1) < 2 * rank
    for d in range(parts):
        sections[d, :half] = jnp.where(
            left, down[d * per : d * per + half], down[d * per + half : (d + 1) * per]
        ).astype(BF16)
        sections[d, half:] = jnp.concatenate(
            [up_grad[d * own : (d + 1) * own, h * HEAD : (h + 1) * HEAD] for h in range(heads)], 0
        ).astype(BF16)


def finish(
    steps, grad_scale, joined, low_grad, back, w, x, mean, rstd, mod, upstream,
    grad_own, grad_other, mixed_own, mixed_other, mod_rows, held, sums, s1, s2, attended,
):
    j = pl.program_id(0)
    width = w.shape[0]
    total = steps * width
    n3 = joined.shape[1]
    at = pl.ds(pl.multiple_of(j * width, width), width)

    @pl.when(j == 0)
    def _():
        s1[...] = jnp.zeros_like(s1)
        s2[...] = jnp.zeros_like(s2)
        attended[...] = unpack_blocks(back, 3, n3 // 3 // HEAD)

    n4 = n3 + n3 // 3
    hg = dot(joined[...], w[:, :n3], NT) + dot(low_grad[...], w[:, n4 : n4 + low_grad.shape[1]], NT)
    out = dot(attended[...], w[:, n3:n4], NT)
    values = x[:, at].astype(F32)
    up_rows = upstream[:, at].astype(F32)
    half = mixed_own.shape[0]
    mixed = (values + mod[2, :, at] * out).astype(BF16)
    mixed_own[:, at] = mixed[:half]
    mixed_other[:, at] = mixed[half:]
    normed = (values - mean[...]) * rstd[...]
    ng = hg * (1.0 + mod[1, :, at])
    sums[0:1, at] = jnp.sum(hg, 0, keepdims=True) * grad_scale
    sums[1:2, at] = jnp.sum(hg * normed, 0, keepdims=True) * grad_scale
    sums[2:3, at] = jnp.sum(up_rows * out, 0, keepdims=True) * grad_scale
    held[:, at] = ng
    s1[...] += jnp.sum(ng, -1, keepdims=True)
    s2[...] += jnp.sum(ng * normed, -1, keepdims=True)

    @pl.when(j == steps - 1)
    def _():
        m1 = s1[...] * (1.0 / total)
        m2 = s2[...] * (1.0 / total)
        for i in range(steps):
            c = slice(i * width, (i + 1) * width)
            nrm = (x[:, c].astype(F32) - mean[...]) * rstd[...]
            grad = (
                upstream[:, c].astype(F32) + rstd[...] * (held[:, c] - m1 - nrm * m2)
            ).astype(BF16)
            grad_own[:, c] = grad[:half]
            grad_other[:, c] = grad[half:]
        tiles = total // HEAD
        for r in range(3):
            for i in range(tiles):
                mod_rows[r * tiles + i : r * tiles + i + 1, :] = sums[
                    r : r + 1, i * HEAD : (i + 1) * HEAD
                ]


def halves(place, own_a, other_a, own_b, other_b, out_a, out_b):
    @pl.when(pl.program_id(0) == 0)
    def _():
        out_a[...] = own_a[...]
        out_b[...] = own_b[...]

    @pl.when(pl.program_id(0) == 1)
    def _():
        out_a[...] = other_a[...]
        out_b[...] = other_b[...]


def spread(arrived, mod_rows, both):
    share = jnp.sum(arrived[...].astype(F32), 0).astype(BF16)
    rows = mod_rows[...].astype(BF16)
    parts = both.shape[0]
    rows_a, rows_b = share.shape[0] // parts, rows.shape[0] // parts
    pad = jnp.zeros((both.shape[1] - rows_a - rows_b, HEAD), F32)
    for j in range(parts):
        piece = jnp.concatenate(
            [
                share[j * rows_a : (j + 1) * rows_a].astype(F32),
                rows[j * rows_b : (j + 1) * rows_b].astype(F32),
                pad,
            ],
            0,
        )
        both[j] = piece.astype(BF16)


def summed(arrived, out):
    total = jnp.sum(arrived[...].astype(F32), 0).astype(BF16)
    out[...] = jnp.broadcast_to(total[None], out.shape)


def collected(rows_a, rows_b, shares, down_t, up_grad, mod_grad):
    values = shares[...].astype(F32)
    parts = values.shape[0]
    cols = down_t.shape[0]
    own = up_grad.shape[0]
    half = down_t.shape[1] // 2
    a = jnp.concatenate([values[j, :rows_a] for j in range(parts)], 0)
    b = jnp.concatenate([values[j, rows_a : rows_a + rows_b] for j in range(parts)], 0)
    down_t[...] = jnp.concatenate([a[:half, :cols], a[:half, cols:]], 0).T
    for h in range(up_grad.shape[1] // HEAD):
        up_grad[:, h * HEAD : (h + 1) * HEAD] = a[half + h * own : half + (h + 1) * own]
    tiles = mod_grad.shape[2] // HEAD
    for i in range(3 * tiles):
        mod_grad[i // tiles, :, (i % tiles) * HEAD : (i % tiles + 1) * HEAD] = b[i : i + 1]


def per_device(tokens, modulation, qkv, out_w, down_w, up_w, output_gradient):
    dp, ctx = lax.axis_size("dp"), lax.axis_size(CTX)
    m, width = tokens.shape[2], tokens.shape[3]
    n = up_w.shape[1]
    heads = n // HEAD
    rank = down_w.shape[1] // 2
    pair, along = lax.axis_size("yh"), lax.axis_size(("far", "near"))
    half = m // pair
    positions = half // (along // heads)
    mod = modulation.transpose(1, 0, 2)
    grad_scale = (dp * ctx * m) ** (-0.5)
    own = width // dp

    cols = 4 * n + HEAD
    packed = call(pack, shape((own, cols), BF16), moved=4 * own * cols)(qkv, out_w.T, down_w.T)
    w = lax.all_gather(packed, "dp", axis=0, tiled=True)
    up = lax.all_to_all(
        jnp.broadcast_to(up_w[None], (dp, *up_w.shape)), "dp", 0, 0, tiled=True
    ).reshape(2 * rank, n)

    side = lax.axis_index("yh")
    swap = [(0, 1), (1, 0)]

    def by_place(rows):
        own_rows = lax.dynamic_slice_in_dim(rows, side * half, half, 0)
        other = lax.dynamic_slice_in_dim(rows, (1 - side) * half, half, 0)
        return jnp.concatenate([own_rows, lax.ppermute(other, "yh", swap)], 0)

    _, tokens, output_gradient = lax.optimization_barrier((packed, tokens, output_gradient))
    x = by_place(tokens.reshape(m, width))
    upstream = by_place(output_gradient.reshape(m, width))
    hidden, hidden_t, branch_grad, mean, rstd = call(
        normalize,
        (
            shape((m, width), BF16),
            shape((width, m), BF16),
            shape((m, width), BF16),
            shape((m, 1), F32),
            shape((m, 1), F32),
        ),
        flops=20 * m * width,
        moved=10 * m * width,
    )(x, mod, upstream)

    sent, raw, low = call(
        functools.partial(projections, rank),
        (
            shape((along, pair, 4, positions, HEAD), BF16),
            shape((m, 2 * n), F32),
            shape((m, 2 * rank), BF16),
        ),
        grid=(4,),
        in_specs=[
            whole(m, width),
            whole(m, width),
            pl.BlockSpec((width, n), lambda t: (0, t)),
            pl.BlockSpec((width, HEAD), lambda t: (0, 4 * n // HEAD)),
            whole(2 * rank, n),
        ],
        out_specs=(
            pl.BlockSpec((along, pair, 1, positions, HEAD), lambda t: (0, 0, t, 0, 0)),
            whole(m, 2 * n),
            whole(m, 2 * rank),
        ),
        flops=2 * m * width * cols,
        moved=2 * width * cols,
    )(hidden, branch_grad, w, w, up)
    rows_in = lax.all_to_all(sent, ("far", "near"), 0, 0, tiled=True)

    back_sent = call(
        attention,
        shape((ctx, 4, positions, HEAD), BF16),
        flops=7 * 2 * 2 * 256 * 256 * 128,
        moved=8 * m * n * 2,
        vmem=16,
    )(rows_in.reshape(ctx, 4, positions, HEAD))
    back = lax.all_to_all(
        back_sent.reshape(along, pair, 4, positions, HEAD), ("far", "near"), 0, 0, tiled=True
    )

    own_rows = own // 2 + (2 * rank // dp) * heads
    joined, low_grad, sections = call(
        functools.partial(adapter_terms, rank, grad_scale),
        (
            shape((m, 3 * n), BF16),
            shape((m, 2 * rank), BF16),
            shape((dp, own_rows, HEAD), BF16),
        ),
        flops=2 * m * width * HEAD + 8 * m * n * 64,
        moved=m * width * 2 + m * n * 20,
    )(back, raw, low, up, hidden_t)
    arrived = lax.all_to_all(sections, "dp", 0, 0, tiled=True)

    per = 2
    steps, cb = dp // per, per * own
    grad_own, grad_other, mixed_own, mixed_other, mod_rows = call(
        functools.partial(finish, steps, grad_scale),
        (
            *(shape((half, width), BF16),) * 4,
            shape((3 * width // HEAD, HEAD), F32),
        ),
        grid=(steps,),
        in_specs=[
            whole(m, 3 * n),
            whole(m, 2 * rank),
            whole(along, pair, 4, positions, HEAD),
            pl.BlockSpec((cb, cols), lambda k: (k, 0)),
            whole(m, width),
            whole(m, 1),
            whole(m, 1),
            whole(3, 1, width),
            whole(m, width),
        ],
        out_specs=(*(whole(half, width),) * 4, whole(3 * width // HEAD, HEAD)),
        scratch=[
            pltpu.VMEM((m, width), F32),
            pltpu.VMEM((3, width), F32),
            pltpu.VMEM((m, 1), F32),
            pltpu.VMEM((m, 1), F32),
            pltpu.VMEM((m, n), BF16),
        ],
        flops=2 * m * width * cols,
        moved=2 * width * cols + 8 * m * width,
    )(joined, low_grad, back, w, x, mean, rstd, mod, upstream)

    grad_other = lax.ppermute(grad_other, "yh", swap)
    mixed_other = lax.ppermute(mixed_other, "yh", swap)
    fixed = pl.BlockSpec((half, width), lambda i, s: (0, 0))
    placed = pl.BlockSpec((half, width), lambda i, s: (i + s[0] - 2 * i * s[0], 0))
    tokens_grad, mixed = pl.pallas_call(
        halves,
        out_shape=(shape((m, width), BF16),) * 2,
        grid_spec=pltpu.PrefetchScalarGridSpec(
            num_scalar_prefetch=1, grid=(2,), in_specs=[fixed] * 4, out_specs=(placed, placed)
        ),
        compiler_params=pltpu.CompilerParams(vmem_limit_bytes=16 * 2**20),
        cost_estimate=pl.CostEstimate(flops=0, bytes_accessed=8 * m * width, transcendentals=0),
    )(side.astype(jnp.int32).reshape(1), grad_own, grad_other, mixed_own, mixed_other)

    near, far = lax.axis_size("near"), lax.axis_size("yh") * lax.axis_size("far")
    rows_a, rows_b = own_rows // near, mod_rows.shape[0] // near
    rows = 16 * -(-(rows_a + rows_b) // 16)
    both = call(spread, shape((near, rows, HEAD), BF16), moved=2**19, vmem=8)(arrived, mod_rows)
    part = call(summed, shape((far, rows, HEAD), BF16), moved=2**17, vmem=8)(
        lax.all_to_all(both, "near", 0, 0, tiled=True)
    )
    part = call(summed, shape((near, rows, HEAD), BF16), moved=2**17, vmem=8)(
        lax.all_to_all(part, ("yh", "far"), 0, 0, tiled=True)
    )
    down_t, up_grad, mod_grad = call(
        functools.partial(collected, rows_a, rows_b),
        (
            shape((2 * rank, own), F32),
            shape((2 * rank // dp, n), F32),
            shape((3, 1, width), F32),
        ),
        moved=2**18,
        vmem=8,
    )(lax.all_to_all(part, "near", 0, 0, tiled=True))
    return (
        mixed.reshape(tokens.shape),
        tokens_grad.reshape(tokens.shape),
        mod_grad.reshape(1, 3, width),
        down_t.T,
        up_grad,
    )


def solution(mesh):
    dp, ctx = mesh.devices.shape
    fine = Mesh(mesh.devices.reshape(dp, 2, ctx // 8, 4), ("dp", *CTX))
    return jax.shard_map(
        per_device,
        mesh=fine,
        in_specs=(
            P("dp", CTX, None, None),
            P("dp", None, None),
            P("dp", None),
            P(None, "dp"),
            P("dp", None),
            P("dp", None),
            P("dp", CTX, None, None),
        ),
        out_specs=(
            P("dp", CTX, None, None),
            P("dp", CTX, None, None),
            P("dp", None, None),
            P("dp", None),
            P("dp", None),
        ),
        check_vma=False,
    )
```

```python
import functools

import jax
import jax.numpy as jnp
from jax import lax
from jax.experimental import pallas as pl
from jax.experimental.pallas import tpu as pltpu
from jax.sharding import Mesh
from jax.sharding import PartitionSpec as P

HEAD = 128
EPS = 1e-06
F32 = jnp.float32
BF16 = jnp.bfloat16
NT = (((1,), (1,)), ((), ()))
TN = (((0,), (0,)), ((), ()))
CTX = ("yh", "far", "near")
NN = (((1,), (0,)), ((), ()))


def dot(a, b, dims=NN):
    return lax.dot_general(a, b, dims, preferred_element_type=F32)


def call(body, out_shape, grid=None, in_specs=None, out_specs=None, scratch=(), flops=0, moved=0, vmem=20):
    extra = {} if grid is None else {"grid": grid, "in_specs": in_specs, "out_specs": out_specs}
    return pl.pallas_call(
        body,
        out_shape=out_shape,
        scratch_shapes=list(scratch),
        compiler_params=pltpu.CompilerParams(vmem_limit_bytes=vmem * 2**20),
        cost_estimate=pl.CostEstimate(flops=flops, bytes_accessed=moved, transcendentals=0),
        **extra,
    )


def shape(dims, dtype):
    return jax.ShapeDtypeStruct(dims, dtype)


def whole(*dims):
    return pl.BlockSpec(dims, lambda i: (0,) * len(dims))


def split_up(up, rank):
    row = lax.broadcasted_iota(jnp.int32, up.shape, 0)
    zero = jnp.zeros_like(up)
    return jnp.where(row < rank, up, zero), jnp.where(row < rank, zero, up)


def unpack_blocks(ref, t, heads):
    groups = ref.shape[0] // heads
    columns = [
        jnp.concatenate([ref[g * heads + h, t] for g in range(groups)], 0) for h in range(heads)
    ]
    return jnp.concatenate(columns, 1)


def normalize(x, mod, upstream, hidden, hidden_t, branch_grad, mean_out, rstd_out):
    values = x[...].astype(F32)
    mean = jnp.mean(values, -1, keepdims=True)
    center = values - mean
    rstd = lax.rsqrt(jnp.mean(center * center, -1, keepdims=True) + EPS)
    mean_out[...] = mean
    rstd_out[...] = rstd
    state = (center * rstd * (1.0 + mod[1]) + mod[0]).astype(BF16)
    hidden[...] = state
    hidden_t[...] = state.T
    branch_grad[...] = (upstream[...].astype(F32) * mod[2]).astype(BF16)


def pack(qkv, out_t, down_t, packed):
    n, k = out_t.shape[1], qkv.shape[1]
    packed[:, :k] = qkv[...]
    packed[:, k : k + n] = out_t[...]
    down = down_t[...].astype(F32).T
    packed[:, k + n :] = jnp.concatenate([down, jnp.zeros_like(down)], 1).astype(BF16)


def head_scales(x):
    parts = []
    for h in range(x.shape[1] // HEAD):
        v = x[:, h * HEAD : (h + 1) * HEAD]
        parts.append(lax.rsqrt(jnp.mean(v * v, -1, keepdims=True) + EPS))
    return parts


def projections(rank, hidden, branch_grad, w_top, w_low, w_down, up, sent, raw, low_out):
    t = pl.program_id(0)
    half, n = w_top.shape
    heads = n // HEAD
    positions = sent.shape[2]

    def product(rows):
        return dot(rows[:, :half], w_top[...]) + dot(rows[:, half:], w_low[...])

    def store(x, normed):
        scales = head_scales(x) if normed else None
        for h in range(heads):
            rows = x[:, h * HEAD : (h + 1) * HEAD]
            if normed:
                rows = rows * scales[h]
            rows = rows.astype(BF16)
            for g in range(x.shape[0] // positions):
                sent[g * heads + h, 0] = rows[g * positions : (g + 1) * positions]

    @pl.when(t == 0)
    def _():
        low_out[...] = dot(hidden[...], w_down[...])[:, : 2 * rank].astype(BF16)
        up_q, _ = split_up(up[...], rank)
        q = product(hidden) + dot(low_out[...], up_q)
        raw[:, :n] = q
        store(q, True)

    @pl.when(t == 1)
    def _():
        k = product(hidden)
        raw[:, n:] = k
        store(k, True)

    @pl.when(t == 2)
    def _():
        _, up_v = split_up(up[...], rank)
        store(product(hidden) + dot(low_out[...], up_v), False)

    @pl.when(t == 3)
    def _():
        store(product(branch_grad), False)


def attention(rows_in, back):
    frames, _, positions, _ = rows_in.shape
    group = 8
    total = frames * group
    row = lax.broadcasted_iota(jnp.int32, (total, total), 0) % group
    col = lax.broadcasted_iota(jnp.int32, (total, total), 1) % group
    same = row == col
    scale = HEAD**-0.5
    halves = []
    for p in range(positions // group):

        def rows_of(ref, t):
            x = ref[:, t].astype(F32)[:, p * group : (p + 1) * group]
            return x.reshape(total, HEAD).astype(BF16)

        q, k, v, g = (rows_of(rows_in, t) for t in range(4))
        s = dot(q, k, NT) * scale
        e = jnp.where(same, jnp.exp(s), 0.0)
        a = e / jnp.sum(e, -1, keepdims=True)
        low = a.astype(BF16)
        attended = dot(low, v)
        dp = dot(g, v, NT)
        dv = dot(low, g, TN)
        inner = jnp.sum(a * dp, -1, keepdims=True)
        ds = (a * (dp - inner) * scale).astype(BF16)
        dq = dot(ds, k)
        dk = dot(ds, q, TN)
        halves.append([x.reshape(frames, group, HEAD) for x in (dq, dk, dv, attended)])
    for t in range(4):
        x = jnp.concatenate([h[t] for h in halves], 1).astype(BF16)
        back[:, t] = x


def norm_back(raw, incoming):
    parts = []
    for h in range(raw.shape[1] // HEAD):
        x = raw[:, h * HEAD : (h + 1) * HEAD]
        u = incoming[:, h * HEAD : (h + 1) * HEAD].astype(F32)
        r = lax.rsqrt(jnp.mean(x * x, -1, keepdims=True) + EPS)
        parts.append(r * u - x * (r * r * r * jnp.mean(x * u, -1, keepdims=True)))
    return jnp.concatenate(parts, 1).astype(BF16)


def adapter_terms(rank, scale, back, raw, low, up, hidden_t, joined, low_grad, sections):
    n = up.shape[1]
    heads = n // HEAD
    dq = norm_back(raw[:, :n], unpack_blocks(back, 0, heads))
    dk = norm_back(raw[:, n:], unpack_blocks(back, 1, heads))
    dv = unpack_blocks(back, 2, heads)
    joined[:, :n] = dq
    joined[:, n : 2 * n] = dk
    joined[:, 2 * n :] = dv
    up_q, up_v = split_up(up[...], rank)
    lg = (dot(dq, up_q, NT) + dot(dv, up_v, NT)).astype(BF16)
    low_grad[...] = lg
    down = dot(hidden_t[...], jnp.concatenate([lg, lg], 1)) * scale
    low_rows = low[...]
    row = lax.broadcasted_iota(jnp.int32, (2 * rank, n), 0)
    up_grad = jnp.where(row < rank, dot(low_rows, dq, TN), dot(low_rows, dv, TN)) * scale
    near = heads
    parts = sections.shape[0] // near
    per, half = down.shape[0] // parts, down.shape[0] // parts // 2
    own, rows = 2 * rank // parts, half // near
    left = lax.broadcasted_iota(jnp.int32, (half, HEAD), 1) < 2 * rank
    for d in range(parts):
        both = jnp.where(
            left, down[d * per : d * per + half], down[d * per + half : (d + 1) * per]
        ).astype(BF16)
        mine = up_grad[d * own : (d + 1) * own].astype(BF16)
        for i in range(near):
            sections[d * near + i, :rows] = both[i * rows : (i + 1) * rows]
            sections[d * near + i, rows:] = mine[:, i * HEAD : (i + 1) * HEAD]


def finish(
    steps, grad_scale, joined, low_grad, back, w, x, mean, rstd, mod, upstream,
    tokens_grad, mixed, mod_rows, held, sums, s1, s2, attended,
):
    j = pl.program_id(0)
    width = w.shape[0]
    total = steps * width
    n3 = joined.shape[1]
    at = pl.ds(pl.multiple_of(j * width, width), width)

    @pl.when(j == 0)
    def _():
        s1[...] = jnp.zeros_like(s1)
        s2[...] = jnp.zeros_like(s2)
        attended[...] = unpack_blocks(back, 3, n3 // 3 // HEAD)

    n4 = n3 + n3 // 3
    hg = dot(joined[...], w[:, :n3], NT) + dot(low_grad[...], w[:, n4 : n4 + low_grad.shape[1]], NT)
    out = dot(attended[...], w[:, n3:n4], NT)
    values = x[:, at].astype(F32)
    up_rows = upstream[:, at].astype(F32)
    mixed[:, at] = (values + mod[2, :, at] * out).astype(BF16)
    normed = (values - mean[...]) * rstd[...]
    ng = hg * (1.0 + mod[1, :, at])
    sums[0:1, at] = jnp.sum(hg, 0, keepdims=True) * grad_scale
    sums[1:2, at] = jnp.sum(hg * normed, 0, keepdims=True) * grad_scale
    sums[2:3, at] = jnp.sum(up_rows * out, 0, keepdims=True) * grad_scale
    held[:, at] = ng
    s1[...] += jnp.sum(ng, -1, keepdims=True)
    s2[...] += jnp.sum(ng * normed, -1, keepdims=True)

    @pl.when(j == steps - 1)
    def _():
        m1 = s1[...] * (1.0 / total)
        m2 = s2[...] * (1.0 / total)
        for i in range(steps):
            c = slice(i * width, (i + 1) * width)
            nrm = (x[:, c].astype(F32) - mean[...]) * rstd[...]
            tokens_grad[:, c] = (
                upstream[:, c].astype(F32) + rstd[...] * (held[:, c] - m1 - nrm * m2)
            ).astype(BF16)
        tiles = total // HEAD
        for r in range(3):
            for i in range(tiles):
                mod_rows[r * tiles + i : r * tiles + i + 1, :] = sums[
                    r : r + 1, i * HEAD : (i + 1) * HEAD
                ]


def spread(arrived, mod_rows, both):
    share = jnp.sum(arrived[...].astype(F32), 0).astype(BF16)
    rows = mod_rows[...].astype(BF16)
    a, b = share.shape[0], rows.shape[0]
    first = 8 * -(-a // 8)
    for j in range(both.shape[0]):
        both[j, :a] = share
        both[j, first : first + b] = rows


def summed(arrived, out):
    total = jnp.sum(arrived[...].astype(F32), 0).astype(BF16)
    out[...] = jnp.broadcast_to(total[None], out.shape)


def collected(shares, down_t, up_grad, mod_grad):
    values = shares[...].astype(F32)
    near = values.shape[0]
    cols, own = down_t.shape[0], up_grad.shape[0]
    rows = down_t.shape[1] // 2 // near
    first = 8 * -(-(rows + own) // 8)
    a = jnp.concatenate([values[i, :rows] for i in range(near)], 0)
    down_t[...] = jnp.concatenate([a[:, :cols], a[:, cols:]], 0).T
    for i in range(near):
        up_grad[:, i * HEAD : (i + 1) * HEAD] = values[i, rows : rows + own]
    tiles = mod_grad.shape[2] // HEAD
    b = jnp.sum(values[:, first : first + 3 * tiles], 0)
    for i in range(3 * tiles):
        mod_grad[i // tiles, :, (i % tiles) * HEAD : (i % tiles + 1) * HEAD] = b[i : i + 1]


def per_device(tokens, modulation, qkv, out_w, down_w, up_w, output_gradient):
    dp, ctx = lax.axis_size("dp"), lax.axis_size(CTX)
    m, width = tokens.shape[2], tokens.shape[3]
    n = up_w.shape[1]
    heads = n // HEAD
    rank = down_w.shape[1] // 2
    positions = m // (ctx // heads)
    mod = modulation.transpose(1, 0, 2)
    grad_scale = (dp * ctx * m) ** (-0.5)
    own = width // dp

    cols = 4 * n + HEAD
    packed = call(pack, shape((own, cols), BF16), moved=4 * own * cols, vmem=60)(qkv, out_w.T, down_w.T)
    w = lax.all_gather(packed, "dp", axis=0, tiled=True)
    w = pltpu.with_memory_space_constraint(w, pltpu.HBM)
    up = lax.all_to_all(
        jnp.broadcast_to(up_w[None], (dp, *up_w.shape)), "dp", 0, 0, tiled=True
    ).reshape(2 * rank, n)

    x = tokens.reshape(m, width)
    upstream = output_gradient.reshape(m, width)
    hidden, hidden_t, branch_grad, mean, rstd = call(
        normalize,
        (
            shape((m, width), BF16),
            shape((width, m), BF16),
            shape((m, width), BF16),
            shape((m, 1), F32),
            shape((m, 1), F32),
        ),
        flops=20 * m * width,
        moved=10 * m * width,
    )(x, mod, upstream)

    sent, raw, low = call(
        functools.partial(projections, rank),
        (
            shape((ctx, 4, positions, HEAD), BF16),
            shape((m, 2 * n), F32),
            shape((m, 2 * rank), BF16),
        ),
        grid=(4,),
        in_specs=[
            whole(m, width),
            whole(m, width),
            pl.BlockSpec((width // 2, n), lambda t: (0, t)),
            pl.BlockSpec((width // 2, n), lambda t: (1, t)),
            pl.BlockSpec((width, HEAD), lambda t: (0, 4 * n // HEAD)),
            whole(2 * rank, n),
        ],
        out_specs=(
            pl.BlockSpec((ctx, 1, positions, HEAD), lambda t: (0, t, 0, 0)),
            whole(m, 2 * n),
            whole(m, 2 * rank),
        ),
        flops=2 * m * width * cols,
        moved=2 * width * cols,
    )(
        pltpu.with_memory_space_constraint(hidden, pltpu.HBM),
        pltpu.with_memory_space_constraint(branch_grad, pltpu.HBM),
        w, w, w, up,
    )
    rows_in = lax.all_to_all(sent, CTX, 0, 0, tiled=True)

    back_sent = call(
        attention,
        shape((ctx, 4, positions, HEAD), BF16),
        flops=7 * 2 * 2 * 256 * 256 * 128,
        moved=8 * m * n * 2,
        vmem=16,
    )(rows_in)
    back = lax.all_to_all(back_sent, CTX, 0, 0, tiled=True)

    near, far = lax.axis_size("near"), lax.axis_size("yh") * lax.axis_size("far")
    assert near == heads
    own_rows = own // 2 // near + 2 * rank // dp
    joined, low_grad, sections = call(
        functools.partial(adapter_terms, rank, grad_scale),
        (
            shape((m, 3 * n), BF16),
            shape((m, 2 * rank), BF16),
            shape((dp * near, own_rows, HEAD), BF16),
        ),
        flops=2 * m * width * HEAD + 8 * m * n * 64,
        moved=m * width * 2 + m * n * 20,
    )(back, raw, low, up, hidden_t)
    arrived = lax.all_to_all(sections, ("dp", "near"), 0, 0, tiled=True)

    per = 2
    steps, cb = dp // per, per * own
    tokens_grad, mixed, mod_rows = call(
        functools.partial(finish, steps, grad_scale),
        (
            shape((m, width), BF16),
            shape((m, width), BF16),
            shape((3 * width // HEAD, HEAD), F32),
        ),
        grid=(steps,),
        in_specs=[
            whole(m, 3 * n),
            whole(m, 2 * rank),
            whole(ctx, 4, positions, HEAD),
            pl.BlockSpec((cb, cols), lambda k: (k, 0)),
            whole(m, width),
            whole(m, 1),
            whole(m, 1),
            whole(3, 1, width),
            whole(m, width),
        ],
        out_specs=(whole(m, width), whole(m, width), whole(3 * width // HEAD, HEAD)),
        scratch=[
            pltpu.VMEM((m, width), F32),
            pltpu.VMEM((3, width), F32),
            pltpu.VMEM((m, 1), F32),
            pltpu.VMEM((m, 1), F32),
            pltpu.VMEM((m, n), BF16),
        ],
        flops=2 * m * width * cols,
        moved=2 * width * cols + 8 * m * width,
    )(joined, low_grad, back, w, x, mean, rstd, mod, upstream)

    rows = 8 * -(-own_rows // 8) + mod_rows.shape[0]
    part = call(spread, shape((far, rows, HEAD), BF16), moved=2**20, vmem=8)(arrived, mod_rows)
    part = call(summed, shape((near, rows, HEAD), BF16), moved=2**18, vmem=8)(
        lax.all_to_all(part, ("yh", "far"), 0, 0, tiled=True)
    )
    down_t, up_grad, mod_grad = call(
        collected,
        (
            shape((2 * rank, own), F32),
            shape((2 * rank // dp, n), F32),
            shape((3, 1, width), F32),
        ),
        moved=2**18,
        vmem=8,
    )(lax.all_to_all(part, "near", 0, 0, tiled=True))
    return (
        mixed.reshape(tokens.shape),
        tokens_grad.reshape(tokens.shape),
        mod_grad.reshape(1, 3, width),
        down_t.T,
        up_grad,
    )


def solution(mesh):
    dp, ctx = mesh.devices.shape
    fine = Mesh(mesh.devices.reshape(dp, 2, ctx // 8, 4), ("dp", *CTX))
    return jax.shard_map(
        per_device,
        mesh=fine,
        in_specs=(
            P("dp", CTX, None, None),
            P("dp", None, None),
            P("dp", None),
            P(None, "dp"),
            P("dp", None),
            P("dp", None),
            P("dp", CTX, None, None),
        ),
        out_specs=(
            P("dp", CTX, None, None),
            P("dp", CTX, None, None),
            P("dp", None, None),
            P("dp", None),
            P("dp", None),
        ),
        check_vma=False,
    )
```

```python
import functools

import jax
import jax.numpy as jnp
from jax import lax
from jax.experimental import pallas as pl
from jax.experimental.pallas import tpu as pltpu
from jax.sharding import Mesh
from jax.sharding import PartitionSpec as P

HEAD = 128
EPS = 1e-06
F32 = jnp.float32
BF16 = jnp.bfloat16
NT = (((1,), (1,)), ((), ()))
TN = (((0,), (0,)), ((), ()))
CTX = ("yh", "far", "near")
NN = (((1,), (0,)), ((), ()))


def dot(a, b, dims=NN):
    return lax.dot_general(a, b, dims, preferred_element_type=F32)


def call(body, out_shape, grid=None, in_specs=None, out_specs=None, scratch=(), flops=0, moved=0, vmem=20):
    extra = {} if in_specs is None else {"in_specs": in_specs, "out_specs": out_specs}
    if grid is not None:
        extra["grid"] = grid
    return pl.pallas_call(
        body,
        out_shape=out_shape,
        scratch_shapes=list(scratch),
        compiler_params=pltpu.CompilerParams(vmem_limit_bytes=vmem * 2**20),
        cost_estimate=pl.CostEstimate(flops=flops, bytes_accessed=moved, transcendentals=0),
        **extra,
    )


def shape(dims, dtype):
    return jax.ShapeDtypeStruct(dims, dtype)


def whole(*dims):
    return pl.BlockSpec(dims, lambda i: (0,) * len(dims))


def split_up(up, rank):
    row = lax.broadcasted_iota(jnp.int32, up.shape, 0)
    zero = jnp.zeros_like(up)
    return jnp.where(row < rank, up, zero), jnp.where(row < rank, zero, up)


def unpack_blocks(ref, t, heads):
    groups = ref.shape[0] // heads
    columns = [
        jnp.concatenate([ref[g * heads + h, t] for g in range(groups)], 0) for h in range(heads)
    ]
    return jnp.concatenate(columns, 1)


def normalize(x, mod, upstream, hidden, hidden_t, branch_grad, mean_out, rstd_out):
    values = x[...].astype(F32)
    mean = jnp.mean(values, -1, keepdims=True)
    center = values - mean
    rstd = lax.rsqrt(jnp.mean(center * center, -1, keepdims=True) + EPS)
    mean_out[...] = mean
    rstd_out[...] = rstd
    state = (center * rstd * (1.0 + mod[1]) + mod[0]).astype(BF16)
    hidden[...] = state
    hidden_t[...] = state.T
    branch_grad[...] = (upstream[...].astype(F32) * mod[2]).astype(BF16)


def pack(qkv, out_t, down_t, packed):
    n, k = out_t.shape[1], qkv.shape[1]
    packed[:, :k] = qkv[...]
    packed[:, k : k + n] = out_t[...]
    down = down_t[...].astype(F32).T
    packed[:, k + n :] = jnp.concatenate([down, jnp.zeros_like(down)], 1).astype(BF16)


def head_scales(x):
    parts = []
    for h in range(x.shape[1] // HEAD):
        v = x[:, h * HEAD : (h + 1) * HEAD]
        parts.append(lax.rsqrt(jnp.mean(v * v, -1, keepdims=True) + EPS))
    return parts


def projections(rank, hidden_at, branch_at, w_at, up, sent, raw, low_out, hidden, branch, w, sems):
    n = up.shape[1]
    heads = n // HEAD
    positions = sent.shape[2]

    def fetch(src, dst, i):
        return pltpu.make_async_copy(src, dst, sems.at[i])

    def columns(i, start, size):
        at = pl.ds(start, size)
        return fetch(w_at.at[:, at], w.at[:, at], i)

    blocks = [columns(i, i * n, n) for i in range(4)]
    down = columns(4, 4 * n, HEAD)
    rows = fetch(hidden_at, hidden, 5)
    grads = fetch(branch_at, branch, 6)
    for copy in (rows, down, *blocks[:3], grads, blocks[3]):
        copy.start()

    def store(t, x):
        scales = head_scales(x) if t < 2 else None
        for h in range(heads):
            part = x[:, h * HEAD : (h + 1) * HEAD]
            if t < 2:
                part = part * scales[h]
            part = part.astype(BF16)
            for g in range(x.shape[0] // positions):
                sent[g * heads + h, t] = part[g * positions : (g + 1) * positions]

    up_q, up_v = split_up(up[...], rank)
    rows.wait()
    down.wait()
    low = dot(hidden[...], w[:, 4 * n :])[:, : 2 * rank].astype(BF16)
    low_out[...] = low
    blocks[0].wait()
    q = dot(hidden[...], w[:, :n]) + dot(low, up_q)
    raw[:, :n] = q
    store(0, q)
    blocks[1].wait()
    k = dot(hidden[...], w[:, n : 2 * n])
    raw[:, n:] = k
    store(1, k)
    blocks[2].wait()
    store(2, dot(hidden[...], w[:, 2 * n : 3 * n]) + dot(low, up_v))
    grads.wait()
    blocks[3].wait()
    store(3, dot(branch[...], w[:, 3 * n : 4 * n]))


def attention(rows_in, back):
    frames, _, positions, _ = rows_in.shape
    group = 8
    total = frames * group
    row = lax.broadcasted_iota(jnp.int32, (total, total), 0) % group
    col = lax.broadcasted_iota(jnp.int32, (total, total), 1) % group
    same = row == col
    scale = HEAD**-0.5
    halves = []
    for p in range(positions // group):

        def rows_of(ref, t):
            x = ref[:, t].astype(F32)[:, p * group : (p + 1) * group]
            return x.reshape(total, HEAD).astype(BF16)

        q, k, v, g = (rows_of(rows_in, t) for t in range(4))
        s = dot(q, k, NT) * scale
        e = jnp.where(same, jnp.exp(s), 0.0)
        a = e / jnp.sum(e, -1, keepdims=True)
        low = a.astype(BF16)
        attended = dot(low, v)
        dp = dot(g, v, NT)
        dv = dot(low, g, TN)
        inner = jnp.sum(a * dp, -1, keepdims=True)
        ds = (a * (dp - inner) * scale).astype(BF16)
        dq = dot(ds, k)
        dk = dot(ds, q, TN)
        halves.append([x.reshape(frames, group, HEAD) for x in (dq, dk, dv, attended)])
    for t in range(4):
        x = jnp.concatenate([h[t] for h in halves], 1).astype(BF16)
        back[:, t] = x


def norm_back(raw, incoming):
    parts = []
    for h in range(raw.shape[1] // HEAD):
        x = raw[:, h * HEAD : (h + 1) * HEAD]
        u = incoming[:, h * HEAD : (h + 1) * HEAD].astype(F32)
        r = lax.rsqrt(jnp.mean(x * x, -1, keepdims=True) + EPS)
        parts.append(r * u - x * (r * r * r * jnp.mean(x * u, -1, keepdims=True)))
    return jnp.concatenate(parts, 1).astype(BF16)


def adapter_terms(rank, scale, back, raw, low, up, hidden_t, joined, low_grad, sections):
    n = up.shape[1]
    heads = n // HEAD
    dq = norm_back(raw[:, :n], unpack_blocks(back, 0, heads))
    dk = norm_back(raw[:, n:], unpack_blocks(back, 1, heads))
    dv = unpack_blocks(back, 2, heads)
    joined[:, :n] = dq
    joined[:, n : 2 * n] = dk
    joined[:, 2 * n :] = dv
    up_q, up_v = split_up(up[...], rank)
    lg = (dot(dq, up_q, NT) + dot(dv, up_v, NT)).astype(BF16)
    low_grad[...] = lg
    down = dot(hidden_t[...], jnp.concatenate([lg, lg], 1)) * scale
    low_rows = low[...]
    row = lax.broadcasted_iota(jnp.int32, (2 * rank, n), 0)
    up_grad = jnp.where(row < rank, dot(low_rows, dq, TN), dot(low_rows, dv, TN)) * scale
    parts = sections.shape[0]
    per, half = down.shape[0] // parts, down.shape[0] // parts // 2
    own = 2 * rank // parts
    left = lax.broadcasted_iota(jnp.int32, (half, HEAD), 1) < 2 * rank
    for d in range(parts):
        sections[d, :half] = jnp.where(
            left, down[d * per : d * per + half], down[d * per + half : (d + 1) * per]
        ).astype(BF16)
        sections[d, half:] = jnp.concatenate(
            [up_grad[d * own : (d + 1) * own, h * HEAD : (h + 1) * HEAD] for h in range(heads)], 0
        ).astype(BF16)


def finish(
    steps, grad_scale, joined, low_grad, back, x, mean, rstd, mod, upstream, w_at,
    tokens_grad, mixed, mod_rows, held, w, sems,
):
    width = x.shape[1] // steps
    total = x.shape[1]
    n3 = joined.shape[1]
    n4 = n3 + n3 // 3
    tiles = total // HEAD
    copies = []
    for j in range(steps):
        at = pl.ds(j * width, width)
        copies.append(pltpu.make_async_copy(w_at.at[at], w.at[at], sems.at[j]))
        copies[j].start()
    attended = unpack_blocks(back, 3, n3 // 3 // HEAD)
    s1 = jnp.zeros((x.shape[0], 1), F32)
    s2 = jnp.zeros((x.shape[0], 1), F32)
    for j in range(steps):
        c = slice(j * width, (j + 1) * width)
        copies[j].wait()
        hg = dot(joined[...], w[c, :n3], NT) + dot(low_grad[...], w[c, n4 : n4 + low_grad.shape[1]], NT)
        out = dot(attended, w[c, n3:n4], NT)
        values = x[:, c].astype(F32)
        up_rows = upstream[:, c].astype(F32)
        mixed[:, c] = (values + mod[2, :, c] * out).astype(BF16)
        normed = (values - mean[...]) * rstd[...]
        ng = hg * (1.0 + mod[1, :, c])
        held[:, c] = ng
        s1 += jnp.sum(ng, -1, keepdims=True)
        s2 += jnp.sum(ng * normed, -1, keepdims=True)
        for r, term in enumerate((hg, hg * normed, up_rows * out)):
            sums = jnp.sum(term, 0, keepdims=True) * grad_scale
            for i in range(width // HEAD):
                row = r * tiles + j * (width // HEAD) + i
                mod_rows[row : row + 1, :] = sums[:, i * HEAD : (i + 1) * HEAD]
    m1 = s1 * (1.0 / total)
    m2 = s2 * (1.0 / total)
    for j in range(steps):
        c = slice(j * width, (j + 1) * width)
        normed = (x[:, c].astype(F32) - mean[...]) * rstd[...]
        tokens_grad[:, c] = (
            upstream[:, c].astype(F32) + rstd[...] * (held[:, c] - m1 - normed * m2)
        ).astype(BF16)


def spread(arrived, mod_rows, both):
    share = jnp.sum(arrived[...].astype(F32), 0).astype(BF16)
    rows = mod_rows[...].astype(BF16)
    parts = both.shape[0]
    rows_a, rows_b = share.shape[0] // parts, rows.shape[0] // parts
    pad = jnp.zeros((both.shape[1] - rows_a - rows_b, HEAD), F32)
    for j in range(parts):
        piece = jnp.concatenate(
            [
                share[j * rows_a : (j + 1) * rows_a].astype(F32),
                rows[j * rows_b : (j + 1) * rows_b].astype(F32),
                pad,
            ],
            0,
        )
        both[j] = piece.astype(BF16)


def summed(arrived, out):
    total = jnp.sum(arrived[...].astype(F32), 0).astype(BF16)
    out[...] = jnp.broadcast_to(total[None], out.shape)


def collected(rows_a, rows_b, shares, down_t, up_grad, mod_grad):
    values = shares[...].astype(F32)
    parts = values.shape[0]
    cols = down_t.shape[0]
    own = up_grad.shape[0]
    half = down_t.shape[1] // 2
    a = jnp.concatenate([values[j, :rows_a] for j in range(parts)], 0)
    b = jnp.concatenate([values[j, rows_a : rows_a + rows_b] for j in range(parts)], 0)
    down_t[...] = jnp.concatenate([a[:half, :cols], a[:half, cols:]], 0).T
    for h in range(up_grad.shape[1] // HEAD):
        up_grad[:, h * HEAD : (h + 1) * HEAD] = a[half + h * own : half + (h + 1) * own]
    tiles = mod_grad.shape[2] // HEAD
    for i in range(3 * tiles):
        mod_grad[i // tiles, :, (i % tiles) * HEAD : (i % tiles + 1) * HEAD] = b[i : i + 1]


def per_device(tokens, modulation, qkv, out_w, down_w, up_w, output_gradient):
    dp, ctx = lax.axis_size("dp"), lax.axis_size(CTX)
    m, width = tokens.shape[2], tokens.shape[3]
    n = up_w.shape[1]
    heads = n // HEAD
    rank = down_w.shape[1] // 2
    positions = m // (ctx // heads)
    mod = modulation.transpose(1, 0, 2)
    grad_scale = (dp * ctx * m) ** (-0.5)
    own = width // dp

    cols = 4 * n + HEAD
    packed = call(pack, shape((own, cols), BF16), moved=4 * own * cols, vmem=60)(qkv, out_w.T, down_w.T)
    w = lax.all_gather(packed, "dp", axis=0, tiled=True)
    w = pltpu.with_memory_space_constraint(w, pltpu.HBM)
    up = lax.all_to_all(
        jnp.broadcast_to(up_w[None], (dp, *up_w.shape)), "dp", 0, 0, tiled=True
    ).reshape(2 * rank, n)

    x = tokens.reshape(m, width)
    upstream = output_gradient.reshape(m, width)
    hidden, hidden_t, branch_grad, mean, rstd = call(
        normalize,
        (
            shape((m, width), BF16),
            shape((width, m), BF16),
            shape((m, width), BF16),
            shape((m, 1), F32),
            shape((m, 1), F32),
        ),
        flops=20 * m * width,
        moved=10 * m * width,
    )(x, mod, upstream)

    sent, raw, low = call(
        functools.partial(projections, rank),
        (
            shape((ctx, 4, positions, HEAD), BF16),
            shape((m, 2 * n), F32),
            shape((m, 2 * rank), BF16),
        ),
        in_specs=[pl.BlockSpec(memory_space=pl.ANY)] * 3 + [pl.BlockSpec(memory_space=pltpu.VMEM)],
        out_specs=(pl.BlockSpec(memory_space=pltpu.VMEM),) * 3,
        scratch=[
            pltpu.VMEM((m, width), BF16),
            pltpu.VMEM((m, width), BF16),
            pltpu.VMEM((width, cols), BF16),
            pltpu.SemaphoreType.DMA((7,)),
        ],
        vmem=32,
        flops=2 * m * width * cols,
        moved=2 * width * cols,
    )(
        pltpu.with_memory_space_constraint(hidden, pltpu.HBM),
        pltpu.with_memory_space_constraint(branch_grad, pltpu.HBM),
        w,
        up,
    )
    rows_in = lax.all_to_all(sent, CTX, 0, 0, tiled=True)

    back_sent = call(
        attention,
        shape((ctx, 4, positions, HEAD), BF16),
        flops=7 * 2 * 2 * 256 * 256 * 128,
        moved=8 * m * n * 2,
        vmem=16,
    )(rows_in)
    back = lax.all_to_all(back_sent, CTX, 0, 0, tiled=True)

    own_rows = own // 2 + (2 * rank // dp) * heads
    joined, low_grad, sections = call(
        functools.partial(adapter_terms, rank, grad_scale),
        (
            shape((m, 3 * n), BF16),
            shape((m, 2 * rank), BF16),
            shape((dp, own_rows, HEAD), BF16),
        ),
        flops=2 * m * width * HEAD + 8 * m * n * 64,
        moved=m * width * 2 + m * n * 20,
    )(back, raw, low, up, hidden_t)
    arrived = lax.all_to_all(sections, "dp", 0, 0, tiled=True)

    steps = dp // 2
    tokens_grad, mixed, mod_rows = call(
        functools.partial(finish, steps, grad_scale),
        (
            shape((m, width), BF16),
            shape((m, width), BF16),
            shape((3 * width // HEAD, HEAD), F32),
        ),
        in_specs=[pl.BlockSpec(memory_space=pltpu.VMEM)] * 8 + [pl.BlockSpec(memory_space=pl.ANY)],
        out_specs=(pl.BlockSpec(memory_space=pltpu.VMEM),) * 3,
        scratch=[
            pltpu.VMEM((m, width), F32),
            pltpu.VMEM((width, cols), BF16),
            pltpu.SemaphoreType.DMA((steps,)),
        ],
        flops=2 * m * width * cols,
        moved=2 * width * cols + 8 * m * width,
        vmem=32,
    )(joined, low_grad, back, x, mean, rstd, mod, upstream, w)

    near, far = lax.axis_size("near"), lax.axis_size("yh") * lax.axis_size("far")
    rows_a, rows_b = own_rows // near, mod_rows.shape[0] // near
    rows = 16 * -(-(rows_a + rows_b) // 16)
    both = call(spread, shape((near, rows, HEAD), BF16), moved=2**19, vmem=8)(arrived, mod_rows)
    part = call(summed, shape((far, rows, HEAD), BF16), moved=2**17, vmem=8)(
        lax.all_to_all(both, "near", 0, 0, tiled=True)
    )
    part = call(summed, shape((near, rows, HEAD), BF16), moved=2**17, vmem=8)(
        lax.all_to_all(part, ("yh", "far"), 0, 0, tiled=True)
    )
    down_t, up_grad, mod_grad = call(
        functools.partial(collected, rows_a, rows_b),
        (
            shape((2 * rank, own), F32),
            shape((2 * rank // dp, n), F32),
            shape((3, 1, width), F32),
        ),
        moved=2**18,
        vmem=8,
    )(lax.all_to_all(part, "near", 0, 0, tiled=True))
    return (
        mixed.reshape(tokens.shape),
        tokens_grad.reshape(tokens.shape),
        mod_grad.reshape(1, 3, width),
        down_t.T,
        up_grad,
    )


def solution(mesh):
    dp, ctx = mesh.devices.shape
    fine = Mesh(mesh.devices.reshape(dp, 2, ctx // 8, 4), ("dp", *CTX))
    return jax.shard_map(
        per_device,
        mesh=fine,
        in_specs=(
            P("dp", CTX, None, None),
            P("dp", None, None),
            P("dp", None),
            P(None, "dp"),
            P("dp", None),
            P("dp", None),
            P("dp", CTX, None, None),
        ),
        out_specs=(
            P("dp", CTX, None, None),
            P("dp", CTX, None, None),
            P("dp", None, None),
            P("dp", None),
            P("dp", None),
        ),
        check_vma=False,
    )
```

```python
import functools

import jax
import jax.numpy as jnp
from jax import lax
from jax.experimental import pallas as pl
from jax.experimental.pallas import tpu as pltpu
from jax.sharding import Mesh
from jax.sharding import PartitionSpec as P

HEAD = 128
EPS = 1e-06
F32 = jnp.float32
BF16 = jnp.bfloat16
NT = (((1,), (1,)), ((), ()))
TN = (((0,), (0,)), ((), ()))
CTX = ("yh", "far", "near")
NN = (((1,), (0,)), ((), ()))


def dot(a, b, dims=NN):
    return lax.dot_general(a, b, dims, preferred_element_type=F32)


def call(body, out_shape, grid=None, in_specs=None, out_specs=None, scratch=(), flops=0, moved=0, vmem=20):
    extra = {} if in_specs is None else {"in_specs": in_specs, "out_specs": out_specs}
    if grid is not None:
        extra["grid"] = grid
    return pl.pallas_call(
        body,
        out_shape=out_shape,
        scratch_shapes=list(scratch),
        compiler_params=pltpu.CompilerParams(vmem_limit_bytes=vmem * 2**20),
        cost_estimate=pl.CostEstimate(flops=flops, bytes_accessed=moved, transcendentals=0),
        **extra,
    )


def shape(dims, dtype):
    return jax.ShapeDtypeStruct(dims, dtype)


def whole(*dims):
    return pl.BlockSpec(dims, lambda i: (0,) * len(dims))


def split_up(up, rank):
    row = lax.broadcasted_iota(jnp.int32, up.shape, 0)
    zero = jnp.zeros_like(up)
    return jnp.where(row < rank, up, zero), jnp.where(row < rank, zero, up)


def unpack_blocks(ref, t, heads):
    groups = ref.shape[0] // heads
    columns = [
        jnp.concatenate([ref[g * heads + h, t] for g in range(groups)], 0) for h in range(heads)
    ]
    return jnp.concatenate(columns, 1)


def normalize(x, mod, upstream, hidden, hidden_t, branch_grad, mean_out, rstd_out):
    values = x[...].astype(F32)
    mean = jnp.mean(values, -1, keepdims=True)
    center = values - mean
    rstd = lax.rsqrt(jnp.mean(center * center, -1, keepdims=True) + EPS)
    mean_out[...] = mean
    rstd_out[...] = rstd
    state = (center * rstd * (1.0 + mod[1]) + mod[0]).astype(BF16)
    hidden[...] = state
    hidden_t[...] = state.T
    branch_grad[...] = (upstream[...].astype(F32) * mod[2]).astype(BF16)


def pack(qkv, out_t, packed, sems):
    k, n = qkv.shape[1], out_t.shape[1]
    copies = [
        pltpu.make_async_copy(qkv, packed.at[:, pl.ds(0, k)], sems.at[0]),
        pltpu.make_async_copy(out_t, packed.at[:, pl.ds(k, n)], sems.at[1]),
    ]
    for copy in copies:
        copy.start()
    for copy in copies:
        copy.wait()


def pack_maps(down_t, up, copies):
    half = down_t.shape[1] // 2
    down = down_t[...].astype(F32).T
    both = jnp.concatenate([down[:half], down[half:]], 1).astype(BF16)
    rows = up.shape[0]
    values = up[...].astype(F32)
    ups = jnp.concatenate(
        [values[:, h * HEAD : (h + 1) * HEAD] for h in range(up.shape[1] // HEAD)], 0
    ).astype(BF16)
    for d in range(copies.shape[0]):
        copies[d, :half] = both
        copies[d, half:] = ups


def unpack_maps(maps, down, up):
    parts = maps.shape[0]
    cols, n = up.shape
    half = down.shape[0] // parts // 2
    own = cols // parts
    for d in range(parts):
        both = maps[d, :half].astype(F32)
        at = 2 * half * d
        down[at : at + half, :] = both[:, :cols].astype(BF16)
        down[at + half : at + 2 * half, :] = both[:, cols:].astype(BF16)
        rows = maps[d, half:].astype(F32)
        for h in range(n // HEAD):
            up[d * own : (d + 1) * own, h * HEAD : (h + 1) * HEAD] = rows[
                h * own : (h + 1) * own
            ]


def head_scales(x):
    parts = []
    for h in range(x.shape[1] // HEAD):
        v = x[:, h * HEAD : (h + 1) * HEAD]
        parts.append(lax.rsqrt(jnp.mean(v * v, -1, keepdims=True) + EPS))
    return parts


def projections(
    hidden_at, branch_at, w_at, down_at, up, sent, raw, low_out, hidden, branch, w, w_down, sems
):
    n = up.shape[1]
    heads = n // HEAD
    positions = sent.shape[2]

    def fetch(src, dst, i):
        return pltpu.make_async_copy(src, dst, sems.at[i])

    def columns(i, start, size):
        at = pl.ds(start, size)
        return fetch(w_at.at[:, at], w.at[:, at], i)

    blocks = [columns(i, i * n, n) for i in range(4)]
    rows = fetch(hidden_at, hidden, 4)
    grads = fetch(branch_at, branch, 5)
    down = fetch(down_at, w_down, 6)
    for copy in (rows, down, *blocks[:3], grads, blocks[3]):
        copy.start()

    def store(t, x):
        scales = head_scales(x) if t < 2 else None
        for h in range(heads):
            part = x[:, h * HEAD : (h + 1) * HEAD]
            if t < 2:
                part = part * scales[h]
            part = part.astype(BF16)
            for g in range(x.shape[0] // positions):
                sent[g * heads + h, t] = part[g * positions : (g + 1) * positions]

    up_q, up_v = split_up(up[...], up.shape[0] // 2)
    rows.wait()
    down.wait()
    low = dot(hidden[...], w_down[...]).astype(BF16)
    low_out[...] = low
    blocks[0].wait()
    q = dot(hidden[...], w[:, :n]) + dot(low, up_q)
    raw[:, :n] = q
    store(0, q)
    blocks[1].wait()
    k = dot(hidden[...], w[:, n : 2 * n])
    raw[:, n:] = k
    store(1, k)
    blocks[2].wait()
    store(2, dot(hidden[...], w[:, 2 * n : 3 * n]) + dot(low, up_v))
    grads.wait()
    blocks[3].wait()
    store(3, dot(branch[...], w[:, 3 * n : 4 * n]))


def attention(rows_in, back):
    frames, _, positions, _ = rows_in.shape
    group = 8
    total = frames * group
    row = lax.broadcasted_iota(jnp.int32, (total, total), 0) % group
    col = lax.broadcasted_iota(jnp.int32, (total, total), 1) % group
    same = row == col
    scale = HEAD**-0.5
    halves = []
    for p in range(positions // group):

        def rows_of(ref, t):
            x = ref[:, t].astype(F32)[:, p * group : (p + 1) * group]
            return x.reshape(total, HEAD).astype(BF16)

        q, k, v, g = (rows_of(rows_in, t) for t in range(4))
        s = dot(q, k, NT) * scale
        e = jnp.where(same, jnp.exp(s), 0.0)
        a = e / jnp.sum(e, -1, keepdims=True)
        low = a.astype(BF16)
        attended = dot(low, v)
        dp = dot(g, v, NT)
        dv = dot(low, g, TN)
        inner = jnp.sum(a * dp, -1, keepdims=True)
        ds = (a * (dp - inner) * scale).astype(BF16)
        dq = dot(ds, k)
        dk = dot(ds, q, TN)
        halves.append([x.reshape(frames, group, HEAD) for x in (dq, dk, dv, attended)])
    for t in range(4):
        x = jnp.concatenate([h[t] for h in halves], 1).astype(BF16)
        back[:, t] = x


def norm_back(raw, incoming):
    parts = []
    for h in range(raw.shape[1] // HEAD):
        x = raw[:, h * HEAD : (h + 1) * HEAD]
        u = incoming[:, h * HEAD : (h + 1) * HEAD].astype(F32)
        r = lax.rsqrt(jnp.mean(x * x, -1, keepdims=True) + EPS)
        parts.append(r * u - x * (r * r * r * jnp.mean(x * u, -1, keepdims=True)))
    return jnp.concatenate(parts, 1).astype(BF16)


def adapter_terms(rank, scale, back, raw, low, up, hidden_t, joined, low_grad, sections):
    n = up.shape[1]
    heads = n // HEAD
    dq = norm_back(raw[:, :n], unpack_blocks(back, 0, heads))
    dk = norm_back(raw[:, n:], unpack_blocks(back, 1, heads))
    dv = unpack_blocks(back, 2, heads)
    joined[:, :n] = dq
    joined[:, n : 2 * n] = dk
    joined[:, 2 * n :] = dv
    up_q, up_v = split_up(up[...], rank)
    lg = (dot(dq, up_q, NT) + dot(dv, up_v, NT)).astype(BF16)
    low_grad[...] = lg
    down = dot(hidden_t[...], jnp.concatenate([lg, lg], 1)) * scale
    low_rows = low[...]
    row = lax.broadcasted_iota(jnp.int32, (2 * rank, n), 0)
    up_grad = jnp.where(row < rank, dot(low_rows, dq, TN), dot(low_rows, dv, TN)) * scale
    parts = sections.shape[0]
    per, half = down.shape[0] // parts, down.shape[0] // parts // 2
    own = 2 * rank // parts
    left = lax.broadcasted_iota(jnp.int32, (half, HEAD), 1) < 2 * rank
    for d in range(parts):
        sections[d, :half] = jnp.where(
            left, down[d * per : d * per + half], down[d * per + half : (d + 1) * per]
        ).astype(BF16)
        sections[d, half:] = jnp.concatenate(
            [up_grad[d * own : (d + 1) * own, h * HEAD : (h + 1) * HEAD] for h in range(heads)], 0
        ).astype(BF16)


def finish(
    steps, grad_scale, joined, low_grad, back, x, mean, rstd, mod, upstream, w_at, down_at,
    tokens_grad, mixed, mod_rows, held, w, w_down, sems,
):
    width = x.shape[1] // steps
    total = x.shape[1]
    n3 = joined.shape[1]
    n4 = n3 + n3 // 3
    tiles = total // HEAD
    copies = []
    for j in range(steps):
        at = pl.ds(j * width, width)
        copies.append(pltpu.make_async_copy(w_at.at[at], w.at[at], sems.at[j]))
        copies[j].start()
    down = pltpu.make_async_copy(down_at, w_down, sems.at[steps])
    down.start()
    attended = unpack_blocks(back, 3, n3 // 3 // HEAD)
    s1 = jnp.zeros((x.shape[0], 1), F32)
    s2 = jnp.zeros((x.shape[0], 1), F32)
    for j in range(steps):
        c = slice(j * width, (j + 1) * width)
        copies[j].wait()
        if j == 0:
            down.wait()
        hg = dot(joined[...], w[c, :n3], NT) + dot(low_grad[...], w_down[c], NT)
        out = dot(attended, w[c, n3:n4], NT)
        values = x[:, c].astype(F32)
        up_rows = upstream[:, c].astype(F32)
        mixed[:, c] = (values + mod[2, :, c] * out).astype(BF16)
        normed = (values - mean[...]) * rstd[...]
        ng = hg * (1.0 + mod[1, :, c])
        held[:, c] = ng
        s1 += jnp.sum(ng, -1, keepdims=True)
        s2 += jnp.sum(ng * normed, -1, keepdims=True)
        for r, term in enumerate((hg, hg * normed, up_rows * out)):
            sums = jnp.sum(term, 0, keepdims=True) * grad_scale
            for i in range(width // HEAD):
                row = r * tiles + j * (width // HEAD) + i
                mod_rows[row : row + 1, :] = sums[:, i * HEAD : (i + 1) * HEAD]
    m1 = s1 * (1.0 / total)
    m2 = s2 * (1.0 / total)
    for j in range(steps):
        c = slice(j * width, (j + 1) * width)
        normed = (x[:, c].astype(F32) - mean[...]) * rstd[...]
        tokens_grad[:, c] = (
            upstream[:, c].astype(F32) + rstd[...] * (held[:, c] - m1 - normed * m2)
        ).astype(BF16)


def spread(arrived, mod_rows, copies):
    share = jnp.sum(arrived[...].astype(F32), 0).astype(BF16)
    rows = mod_rows[...].astype(BF16)
    for j in range(copies.shape[0]):
        copies[j, : share.shape[0]] = share
        copies[j, share.shape[0] :] = rows


def summed(arrived, copies):
    total = jnp.sum(arrived[...].astype(F32), 0).astype(BF16)
    copies[...] = jnp.broadcast_to(total[None], copies.shape)


def collected(arrived, down_t, up_grad, mod_grad):
    total = jnp.sum(arrived[...].astype(F32), 0)
    cols, own = down_t.shape[0], up_grad.shape[0]
    half = down_t.shape[1] // 2
    down_t[...] = jnp.concatenate([total[:half, :cols], total[:half, cols:]], 0).T
    heads = up_grad.shape[1] // HEAD
    for h in range(heads):
        up_grad[:, h * HEAD : (h + 1) * HEAD] = total[half + h * own : half + (h + 1) * own]
    tiles = mod_grad.shape[2] // HEAD
    first = half + heads * own
    for i in range(3 * tiles):
        mod_grad[i // tiles, :, (i % tiles) * HEAD : (i % tiles + 1) * HEAD] = total[
            first + i : first + i + 1
        ]


def per_device(tokens, modulation, qkv, out_w, down_w, up_w, output_gradient):
    dp, ctx = lax.axis_size("dp"), lax.axis_size(CTX)
    m, width = tokens.shape[2], tokens.shape[3]
    n = up_w.shape[1]
    heads = n // HEAD
    rank = down_w.shape[1] // 2
    positions = m // (ctx // heads)
    mod = modulation.transpose(1, 0, 2)
    grad_scale = (dp * ctx * m) ** (-0.5)
    own = width // dp

    cols = 4 * n
    packed = call(
        pack,
        shape((own, cols), BF16),
        in_specs=[pl.BlockSpec(memory_space=pl.ANY)] * 2,
        out_specs=pl.BlockSpec(memory_space=pl.ANY),
        scratch=[pltpu.SemaphoreType.DMA((2,))],
        moved=4 * own * cols,
        vmem=60,
    )(qkv, out_w.T)
    w = lax.all_gather(packed, "dp", axis=0, tiled=True)
    w = pltpu.with_memory_space_constraint(w, pltpu.HBM)
    own_rows = own // 2 + (2 * rank // dp) * heads
    maps = call(pack_maps, shape((dp, own_rows, HEAD), BF16), moved=2**19)(down_w.T, up_w)
    w_down, up = call(
        unpack_maps, (shape((width, 2 * rank), BF16), shape((2 * rank, n), F32)), moved=2**21
    )(lax.all_to_all(maps, "dp", 0, 0, tiled=True))
    w_down = pltpu.with_memory_space_constraint(w_down, pltpu.HBM)
    up = up.astype(BF16)

    x = tokens.reshape(m, width)
    upstream = output_gradient.reshape(m, width)
    hidden, hidden_t, branch_grad, mean, rstd = call(
        normalize,
        (
            shape((m, width), BF16),
            shape((width, m), BF16),
            shape((m, width), BF16),
            shape((m, 1), F32),
            shape((m, 1), F32),
        ),
        flops=20 * m * width,
        moved=10 * m * width,
    )(x, mod, upstream)

    sent, raw, low = call(
        projections,
        (
            shape((ctx, 4, positions, HEAD), BF16),
            shape((m, 2 * n), F32),
            shape((m, 2 * rank), BF16),
        ),
        in_specs=[pl.BlockSpec(memory_space=pl.ANY)] * 4 + [pl.BlockSpec(memory_space=pltpu.VMEM)],
        out_specs=(pl.BlockSpec(memory_space=pltpu.VMEM),) * 3,
        scratch=[
            pltpu.VMEM((m, width), BF16),
            pltpu.VMEM((m, width), BF16),
            pltpu.VMEM((width, cols), BF16),
            pltpu.VMEM((width, 2 * rank), BF16),
            pltpu.SemaphoreType.DMA((7,)),
        ],
        vmem=32,
        flops=2 * m * width * cols,
        moved=2 * width * cols,
    )(
        pltpu.with_memory_space_constraint(hidden, pltpu.HBM),
        pltpu.with_memory_space_constraint(branch_grad, pltpu.HBM),
        w,
        w_down,
        up,
    )
    rows_in = lax.all_to_all(sent, CTX, 0, 0, tiled=True)

    back_sent = call(
        attention,
        shape((ctx, 4, positions, HEAD), BF16),
        flops=7 * 2 * 2 * 256 * 256 * 128,
        moved=8 * m * n * 2,
        vmem=16,
    )(rows_in)
    back = lax.all_to_all(back_sent, CTX, 0, 0, tiled=True)

    joined, low_grad, sections = call(
        functools.partial(adapter_terms, rank, grad_scale),
        (
            shape((m, 3 * n), BF16),
            shape((m, 2 * rank), BF16),
            shape((dp, own_rows, HEAD), BF16),
        ),
        flops=2 * m * width * HEAD + 8 * m * n * 64,
        moved=m * width * 2 + m * n * 20,
    )(back, raw, low, up, hidden_t)
    arrived = lax.all_to_all(sections, "dp", 0, 0, tiled=True)

    steps = dp // 2
    tokens_grad, mixed, mod_rows = call(
        functools.partial(finish, steps, grad_scale),
        (
            shape((m, width), BF16),
            shape((m, width), BF16),
            shape((3 * width // HEAD, HEAD), F32),
        ),
        in_specs=[pl.BlockSpec(memory_space=pltpu.VMEM)] * 8 + [pl.BlockSpec(memory_space=pl.ANY)] * 2,
        out_specs=(pl.BlockSpec(memory_space=pltpu.VMEM),) * 3,
        scratch=[
            pltpu.VMEM((m, width), F32),
            pltpu.VMEM((width, cols), BF16),
            pltpu.VMEM((width, 2 * rank), BF16),
            pltpu.SemaphoreType.DMA((steps + 1,)),
        ],
        flops=2 * m * width * cols,
        moved=2 * width * cols + 8 * m * width,
        vmem=32,
    )(joined, low_grad, back, x, mean, rstd, mod, upstream, w, w_down)

    near, far = lax.axis_size("near"), lax.axis_size("yh") * lax.axis_size("far")
    rows = own_rows + mod_rows.shape[0]
    part = call(spread, shape((near, rows, HEAD), BF16), moved=2**19, vmem=8)(arrived, mod_rows)
    part = call(summed, shape((far, rows, HEAD), BF16), moved=2**19, vmem=8)(
        lax.all_to_all(part, "near", 0, 0, tiled=True)
    )
    down_t, up_grad, mod_grad = call(
        collected,
        (
            shape((2 * rank, own), F32),
            shape((2 * rank // dp, n), F32),
            shape((3, 1, width), F32),
        ),
        moved=2**19,
        vmem=8,
    )(lax.all_to_all(part, ("yh", "far"), 0, 0, tiled=True))
    return (
        mixed.reshape(tokens.shape),
        tokens_grad.reshape(tokens.shape),
        mod_grad.reshape(1, 3, width),
        down_t.T,
        up_grad,
    )


def solution(mesh):
    dp, ctx = mesh.devices.shape
    fine = Mesh(mesh.devices.reshape(dp, 2, ctx // 8, 4), ("dp", *CTX))
    return jax.shard_map(
        per_device,
        mesh=fine,
        in_specs=(
            P("dp", CTX, None, None),
            P("dp", None, None),
            P("dp", None),
            P(None, "dp"),
            P("dp", None),
            P("dp", None),
            P("dp", CTX, None, None),
        ),
        out_specs=(
            P("dp", CTX, None, None),
            P("dp", CTX, None, None),
            P("dp", None, None),
            P("dp", None),
            P("dp", None),
        ),
        check_vma=False,
    )
```

```python
import functools

import jax
import jax.numpy as jnp
from jax import lax
from jax.experimental import pallas as pl
from jax.experimental.pallas import tpu as pltpu
from jax.sharding import Mesh
from jax.sharding import PartitionSpec as P

HEAD = 128
EPS = 1e-06
F32 = jnp.float32
BF16 = jnp.bfloat16
NT = (((1,), (1,)), ((), ()))
TN = (((0,), (0,)), ((), ()))
CTX = ("yh", "far", "near")
NN = (((1,), (0,)), ((), ()))


def dot(a, b, dims=NN):
    return lax.dot_general(a, b, dims, preferred_element_type=F32)


def call(body, out_shape, grid=None, in_specs=None, out_specs=None, scratch=(), flops=0, moved=0, vmem=20):
    extra = {} if in_specs is None else {"in_specs": in_specs, "out_specs": out_specs}
    if grid is not None:
        extra["grid"] = grid
    return pl.pallas_call(
        body,
        out_shape=out_shape,
        scratch_shapes=list(scratch),
        compiler_params=pltpu.CompilerParams(vmem_limit_bytes=vmem * 2**20),
        cost_estimate=pl.CostEstimate(flops=flops, bytes_accessed=moved, transcendentals=0),
        **extra,
    )


def shape(dims, dtype):
    return jax.ShapeDtypeStruct(dims, dtype)


def whole(*dims):
    return pl.BlockSpec(dims, lambda i: (0,) * len(dims))


def split_up(up, rank):
    row = lax.broadcasted_iota(jnp.int32, up.shape, 0)
    zero = jnp.zeros_like(up)
    return jnp.where(row < rank, up, zero), jnp.where(row < rank, zero, up)


def unpack_blocks(ref, t, heads):
    groups = ref.shape[0] // heads
    columns = [
        jnp.concatenate([ref[g * heads + h, t] for g in range(groups)], 0) for h in range(heads)
    ]
    return jnp.concatenate(columns, 1)


def normalize(x, mod, upstream, hidden, hidden_t, branch_grad, mean_out, rstd_out):
    values = x[...].astype(F32)
    mean = jnp.mean(values, -1, keepdims=True)
    center = values - mean
    rstd = lax.rsqrt(jnp.mean(center * center, -1, keepdims=True) + EPS)
    mean_out[...] = mean
    rstd_out[...] = rstd
    state = (center * rstd * (1.0 + mod[1]) + mod[0]).astype(BF16)
    hidden[...] = state
    hidden_t[...] = state.T
    branch_grad[...] = (upstream[...].astype(F32) * mod[2]).astype(BF16)


def pack(qkv, out_t, packed, sems):
    k, n = qkv.shape[1], out_t.shape[1]
    copies = [
        pltpu.make_async_copy(qkv, packed.at[:, pl.ds(0, k)], sems.at[0]),
        pltpu.make_async_copy(out_t, packed.at[:, pl.ds(k, n)], sems.at[1]),
    ]
    for copy in copies:
        copy.start()
    for copy in copies:
        copy.wait()


def pack_maps(down_t, up, copies):
    half = down_t.shape[1] // 2
    down = down_t[...].astype(F32).T
    both = jnp.concatenate([down[:half], down[half:]], 1).astype(BF16)
    rows = up.shape[0]
    values = up[...].astype(F32)
    ups = jnp.concatenate(
        [values[:, h * HEAD : (h + 1) * HEAD] for h in range(up.shape[1] // HEAD)], 0
    ).astype(BF16)
    for d in range(copies.shape[0]):
        copies[d, :half] = both
        copies[d, half:] = ups


def unpack_maps(maps, down, up):
    parts = maps.shape[0]
    cols, n = up.shape
    half = down.shape[0] // parts // 2
    own = cols // parts
    for d in range(parts):
        both = maps[d, :half].astype(F32)
        at = 2 * half * d
        down[at : at + half, :] = both[:, :cols].astype(BF16)
        down[at + half : at + 2 * half, :] = both[:, cols:].astype(BF16)
        rows = maps[d, half:].astype(F32)
        for h in range(n // HEAD):
            up[d * own : (d + 1) * own, h * HEAD : (h + 1) * HEAD] = rows[
                h * own : (h + 1) * own
            ]


def head_scales(x):
    parts = []
    for h in range(x.shape[1] // HEAD):
        v = x[:, h * HEAD : (h + 1) * HEAD]
        parts.append(lax.rsqrt(jnp.mean(v * v, -1, keepdims=True) + EPS))
    return parts


def projections(
    hidden_at, branch_at, w_at, down_at, up, sent, raw, low_out, hidden, branch, w, w_down, sems
):
    n = up.shape[1]
    heads = n // HEAD
    positions = sent.shape[2]

    def fetch(src, dst, i):
        return pltpu.make_async_copy(src, dst, sems.at[i])

    def columns(i, start, size):
        at = pl.ds(start, size)
        return fetch(w_at.at[:, at], w.at[:, at], i)

    blocks = [columns(i, i * n, n) for i in range(4)]
    rows = fetch(hidden_at, hidden, 4)
    grads = fetch(branch_at, branch, 5)
    down = fetch(down_at, w_down, 6)
    for copy in (rows, down, *blocks[:3], grads, blocks[3]):
        copy.start()

    def store(t, x):
        scales = head_scales(x) if t < 2 else None
        for h in range(heads):
            part = x[:, h * HEAD : (h + 1) * HEAD]
            if t < 2:
                part = part * scales[h]
            part = part.astype(BF16)
            for g in range(x.shape[0] // positions):
                sent[g * heads + h, t] = part[g * positions : (g + 1) * positions]

    up_q, up_v = split_up(up[...], up.shape[0] // 2)
    rows.wait()
    down.wait()
    low = dot(hidden[...], w_down[...]).astype(BF16)
    low_out[...] = low
    blocks[0].wait()
    q = dot(hidden[...], w[:, :n]) + dot(low, up_q)
    raw[:, :n] = q
    store(0, q)
    blocks[1].wait()
    k = dot(hidden[...], w[:, n : 2 * n])
    raw[:, n:] = k
    store(1, k)
    blocks[2].wait()
    store(2, dot(hidden[...], w[:, 2 * n : 3 * n]) + dot(low, up_v))
    grads.wait()
    blocks[3].wait()
    store(3, dot(branch[...], w[:, 3 * n : 4 * n]))


def attention(rows_in, back):
    frames, _, positions, _ = rows_in.shape
    group = 8
    total = frames * group
    row = lax.broadcasted_iota(jnp.int32, (total, total), 0) % group
    col = lax.broadcasted_iota(jnp.int32, (total, total), 1) % group
    same = row == col
    scale = HEAD**-0.5
    halves = []
    for p in range(positions // group):

        def rows_of(ref, t):
            x = ref[:, t].astype(F32)[:, p * group : (p + 1) * group]
            return x.reshape(total, HEAD).astype(BF16)

        q, k, v, g = (rows_of(rows_in, t) for t in range(4))
        s = dot(q, k, NT) * scale
        e = jnp.where(same, jnp.exp(s), 0.0)
        a = e / jnp.sum(e, -1, keepdims=True)
        low = a.astype(BF16)
        attended = dot(low, v)
        dp = dot(g, v, NT)
        dv = dot(low, g, TN)
        inner = jnp.sum(a * dp, -1, keepdims=True)
        ds = (a * (dp - inner) * scale).astype(BF16)
        dq = dot(ds, k)
        dk = dot(ds, q, TN)
        halves.append([x.reshape(frames, group, HEAD) for x in (dq, dk, dv, attended)])
    for t in range(4):
        x = jnp.concatenate([h[t] for h in halves], 1).astype(BF16)
        back[:, t] = x


def norm_back(raw, incoming):
    parts = []
    for h in range(raw.shape[1] // HEAD):
        x = raw[:, h * HEAD : (h + 1) * HEAD]
        u = incoming[:, h * HEAD : (h + 1) * HEAD].astype(F32)
        r = lax.rsqrt(jnp.mean(x * x, -1, keepdims=True) + EPS)
        parts.append(r * u - x * (r * r * r * jnp.mean(x * u, -1, keepdims=True)))
    return jnp.concatenate(parts, 1).astype(BF16)


def adapter_terms(rank, scale, back, raw, low, up, hidden_t, joined, low_grad, sections):
    n = up.shape[1]
    heads = n // HEAD
    dq = norm_back(raw[:, :n], unpack_blocks(back, 0, heads))
    dk = norm_back(raw[:, n:], unpack_blocks(back, 1, heads))
    dv = unpack_blocks(back, 2, heads)
    joined[:, :n] = dq
    joined[:, n : 2 * n] = dk
    joined[:, 2 * n :] = dv
    up_q, up_v = split_up(up[...], rank)
    lg = (dot(dq, up_q, NT) + dot(dv, up_v, NT)).astype(BF16)
    low_grad[...] = lg
    down = dot(hidden_t[...], jnp.concatenate([lg, lg], 1)) * scale
    low_rows = low[...]
    row = lax.broadcasted_iota(jnp.int32, (2 * rank, n), 0)
    up_grad = jnp.where(row < rank, dot(low_rows, dq, TN), dot(low_rows, dv, TN)) * scale
    parts = sections.shape[0]
    per, half = down.shape[0] // parts, down.shape[0] // parts // 2
    own = 2 * rank // parts
    left = lax.broadcasted_iota(jnp.int32, (half, HEAD), 1) < 2 * rank
    for d in range(parts):
        sections[d, :half] = jnp.where(
            left, down[d * per : d * per + half], down[d * per + half : (d + 1) * per]
        ).astype(BF16)
        sections[d, half:] = jnp.concatenate(
            [up_grad[d * own : (d + 1) * own, h * HEAD : (h + 1) * HEAD] for h in range(heads)], 0
        ).astype(BF16)


def finish(
    steps, grad_scale, joined, low_grad, back, x, mean, rstd, mod, upstream, w_at, down_at,
    tokens_grad, mixed, mod_rows, held, w, w_down, sems,
):
    width = x.shape[1] // steps
    total = x.shape[1]
    n3 = joined.shape[1]
    n4 = n3 + n3 // 3
    tiles = total // HEAD
    down = pltpu.make_async_copy(down_at, w_down, sems.at[steps])
    down.start()
    copies = []
    for j in range(steps):
        at = pl.ds(j * width, width)
        copies.append(pltpu.make_async_copy(w_at.at[at], w.at[at], sems.at[j]))
        copies[j].start()
    attended = unpack_blocks(back, 3, n3 // 3 // HEAD)
    s1 = jnp.zeros((x.shape[0], 1), F32)
    s2 = jnp.zeros((x.shape[0], 1), F32)
    for j in range(steps):
        c = slice(j * width, (j + 1) * width)
        copies[j].wait()
        if j == 0:
            down.wait()
        hg = dot(joined[...], w[c, :n3], NT) + dot(low_grad[...], w_down[c], NT)
        out = dot(attended, w[c, n3:n4], NT)
        values = x[:, c].astype(F32)
        up_rows = upstream[:, c].astype(F32)
        mixed[:, c] = (values + mod[2, :, c] * out).astype(BF16)
        normed = (values - mean[...]) * rstd[...]
        ng = hg * (1.0 + mod[1, :, c])
        held[:, c] = ng
        s1 += jnp.sum(ng, -1, keepdims=True)
        s2 += jnp.sum(ng * normed, -1, keepdims=True)
        for r, term in enumerate((hg, hg * normed, up_rows * out)):
            sums = jnp.sum(term, 0, keepdims=True) * grad_scale
            for i in range(width // HEAD):
                row = r * tiles + j * (width // HEAD) + i
                mod_rows[row : row + 1, :] = sums[:, i * HEAD : (i + 1) * HEAD]
    m1 = s1 * (1.0 / total)
    m2 = s2 * (1.0 / total)
    for j in range(steps):
        c = slice(j * width, (j + 1) * width)
        normed = (x[:, c].astype(F32) - mean[...]) * rstd[...]
        tokens_grad[:, c] = (
            upstream[:, c].astype(F32) + rstd[...] * (held[:, c] - m1 - normed * m2)
        ).astype(BF16)


def spread(arrived, mod_rows, copies):
    share = jnp.sum(arrived[...].astype(F32), 0).astype(BF16)
    rows = mod_rows[...].astype(BF16)
    for j in range(copies.shape[0]):
        copies[j, : share.shape[0]] = share
        copies[j, share.shape[0] :] = rows


def summed(arrived, copies):
    total = jnp.sum(arrived[...].astype(F32), 0).astype(BF16)
    copies[...] = jnp.broadcast_to(total[None], copies.shape)


def collected(arrived, down_t, up_grad, mod_grad):
    total = jnp.sum(arrived[...].astype(F32), 0)
    cols, own = down_t.shape[0], up_grad.shape[0]
    half = down_t.shape[1] // 2
    down_t[...] = jnp.concatenate([total[:half, :cols], total[:half, cols:]], 0).T
    heads = up_grad.shape[1] // HEAD
    for h in range(heads):
        up_grad[:, h * HEAD : (h + 1) * HEAD] = total[half + h * own : half + (h + 1) * own]
    tiles = mod_grad.shape[2] // HEAD
    first = half + heads * own
    for i in range(3 * tiles):
        mod_grad[i // tiles, :, (i % tiles) * HEAD : (i % tiles + 1) * HEAD] = total[
            first + i : first + i + 1
        ]


def per_device(tokens, modulation, qkv, out_w, down_w, up_w, output_gradient):
    dp, ctx = lax.axis_size("dp"), lax.axis_size(CTX)
    m, width = tokens.shape[2], tokens.shape[3]
    n = up_w.shape[1]
    heads = n // HEAD
    rank = down_w.shape[1] // 2
    positions = m // (ctx // heads)
    mod = modulation.transpose(1, 0, 2)
    grad_scale = (dp * ctx * m) ** (-0.5)
    own = width // dp

    cols = 4 * n
    packed = call(
        pack,
        shape((own, cols), BF16),
        in_specs=[pl.BlockSpec(memory_space=pl.ANY)] * 2,
        out_specs=pl.BlockSpec(memory_space=pltpu.VMEM),
        scratch=[pltpu.SemaphoreType.DMA((2,))],
        moved=4 * own * cols,
        vmem=60,
    )(qkv, out_w.T)
    w = lax.all_gather(packed, "dp", axis=0, tiled=True)
    w = pltpu.with_memory_space_constraint(w, pltpu.HBM)
    own_rows = own // 2 + (2 * rank // dp) * heads
    maps = call(pack_maps, shape((dp, own_rows, HEAD), BF16), moved=2**19)(down_w.T, up_w)
    w_down, up = call(
        unpack_maps, (shape((width, 2 * rank), BF16), shape((2 * rank, n), F32)), moved=2**21
    )(lax.all_to_all(maps, "dp", 0, 0, tiled=True))
    w_down = pltpu.with_memory_space_constraint(w_down, pltpu.HBM)
    up = up.astype(BF16)

    x = tokens.reshape(m, width)
    upstream = output_gradient.reshape(m, width)
    hidden, hidden_t, branch_grad, mean, rstd = call(
        normalize,
        (
            shape((m, width), BF16),
            shape((width, m), BF16),
            shape((m, width), BF16),
            shape((m, 1), F32),
            shape((m, 1), F32),
        ),
        flops=20 * m * width,
        moved=10 * m * width,
    )(x, mod, upstream)

    sent, raw, low = call(
        projections,
        (
            shape((ctx, 4, positions, HEAD), BF16),
            shape((m, 2 * n), F32),
            shape((m, 2 * rank), BF16),
        ),
        in_specs=[pl.BlockSpec(memory_space=pl.ANY)] * 4 + [pl.BlockSpec(memory_space=pltpu.VMEM)],
        out_specs=(pl.BlockSpec(memory_space=pltpu.VMEM),) * 3,
        scratch=[
            pltpu.VMEM((m, width), BF16),
            pltpu.VMEM((m, width), BF16),
            pltpu.VMEM((width, cols), BF16),
            pltpu.VMEM((width, 2 * rank), BF16),
            pltpu.SemaphoreType.DMA((7,)),
        ],
        vmem=32,
        flops=2 * m * width * cols,
        moved=2 * width * cols,
    )(
        pltpu.with_memory_space_constraint(hidden, pltpu.HBM),
        pltpu.with_memory_space_constraint(branch_grad, pltpu.HBM),
        w,
        w_down,
        up,
    )
    rows_in = lax.all_to_all(sent, CTX, 0, 0, tiled=True)

    back_sent = call(
        attention,
        shape((ctx, 4, positions, HEAD), BF16),
        flops=7 * 2 * 2 * 256 * 256 * 128,
        moved=8 * m * n * 2,
        vmem=16,
    )(rows_in)
    back = lax.all_to_all(back_sent, CTX, 0, 0, tiled=True)

    joined, low_grad, sections = call(
        functools.partial(adapter_terms, rank, grad_scale),
        (
            shape((m, 3 * n), BF16),
            shape((m, 2 * rank), BF16),
            shape((dp, own_rows, HEAD), BF16),
        ),
        flops=2 * m * width * HEAD + 8 * m * n * 64,
        moved=m * width * 2 + m * n * 20,
    )(back, raw, low, up, hidden_t)
    arrived = lax.all_to_all(sections, "dp", 0, 0, tiled=True)

    steps = dp // 2
    tokens_grad, mixed, mod_rows = call(
        functools.partial(finish, steps, grad_scale),
        (
            shape((m, width), BF16),
            shape((m, width), BF16),
            shape((3 * width // HEAD, HEAD), F32),
        ),
        in_specs=[pl.BlockSpec(memory_space=pltpu.VMEM)] * 8 + [pl.BlockSpec(memory_space=pl.ANY)] * 2,
        out_specs=(pl.BlockSpec(memory_space=pltpu.VMEM),) * 3,
        scratch=[
            pltpu.VMEM((m, width), F32),
            pltpu.VMEM((width, cols), BF16),
            pltpu.VMEM((width, 2 * rank), BF16),
            pltpu.SemaphoreType.DMA((steps + 1,)),
        ],
        flops=2 * m * width * cols,
        moved=2 * width * cols + 8 * m * width,
        vmem=32,
    )(joined, low_grad, back, x, mean, rstd, mod, upstream, w, w_down)

    near, far = lax.axis_size("near"), lax.axis_size("yh") * lax.axis_size("far")
    rows = own_rows + mod_rows.shape[0]
    part = call(spread, shape((near, rows, HEAD), BF16), moved=2**19, vmem=8)(arrived, mod_rows)
    part = call(summed, shape((far, rows, HEAD), BF16), moved=2**19, vmem=8)(
        lax.all_to_all(part, "near", 0, 0, tiled=True)
    )
    down_t, up_grad, mod_grad = call(
        collected,
        (
            shape((2 * rank, own), F32),
            shape((2 * rank // dp, n), F32),
            shape((3, 1, width), F32),
        ),
        moved=2**19,
        vmem=8,
    )(lax.all_to_all(part, ("yh", "far"), 0, 0, tiled=True))
    return (
        mixed.reshape(tokens.shape),
        tokens_grad.reshape(tokens.shape),
        mod_grad.reshape(1, 3, width),
        down_t.T,
        up_grad,
    )


def solution(mesh):
    dp, ctx = mesh.devices.shape
    fine = Mesh(mesh.devices.reshape(dp, 2, ctx // 8, 4), ("dp", *CTX))
    return jax.shard_map(
        per_device,
        mesh=fine,
        in_specs=(
            P("dp", CTX, None, None),
            P("dp", None, None),
            P("dp", None),
            P(None, "dp"),
            P("dp", None),
            P("dp", None),
            P("dp", CTX, None, None),
        ),
        out_specs=(
            P("dp", CTX, None, None),
            P("dp", CTX, None, None),
            P("dp", None, None),
            P("dp", None),
            P("dp", None),
        ),
        check_vma=False,
    )
```

```python
import functools

import jax
import jax.numpy as jnp
from jax import lax
from jax.experimental import pallas as pl
from jax.experimental.pallas import tpu as pltpu
from jax.sharding import Mesh
from jax.sharding import PartitionSpec as P

HEAD = 128
EPS = 1e-06
F32 = jnp.float32
BF16 = jnp.bfloat16
NT = (((1,), (1,)), ((), ()))
TN = (((0,), (0,)), ((), ()))
CTX = ("yh", "far", "near")
NN = (((1,), (0,)), ((), ()))


def dot(a, b, dims=NN):
    return lax.dot_general(a, b, dims, preferred_element_type=F32)


def call(body, out_shape, grid=None, in_specs=None, out_specs=None, scratch=(), flops=0, moved=0, vmem=20):
    extra = {} if in_specs is None else {"in_specs": in_specs, "out_specs": out_specs}
    if grid is not None:
        extra["grid"] = grid
    return pl.pallas_call(
        body,
        out_shape=out_shape,
        scratch_shapes=list(scratch),
        compiler_params=pltpu.CompilerParams(vmem_limit_bytes=vmem * 2**20),
        cost_estimate=pl.CostEstimate(flops=flops, bytes_accessed=moved, transcendentals=0),
        **extra,
    )


def shape(dims, dtype):
    return jax.ShapeDtypeStruct(dims, dtype)


def whole(*dims):
    return pl.BlockSpec(dims, lambda i: (0,) * len(dims))


def split_up(up, rank):
    row = lax.broadcasted_iota(jnp.int32, up.shape, 0)
    zero = jnp.zeros_like(up)
    return jnp.where(row < rank, up, zero), jnp.where(row < rank, zero, up)


def unpack_blocks(ref, t, heads):
    groups = ref.shape[0] // heads
    columns = [
        jnp.concatenate([ref[g * heads + h, t] for g in range(groups)], 0) for h in range(heads)
    ]
    return jnp.concatenate(columns, 1)


def normalize(x, mod, upstream, hidden, hidden_t, branch_grad, mean_out, rstd_out):
    values = x[...].astype(F32)
    mean = jnp.mean(values, -1, keepdims=True)
    center = values - mean
    rstd = lax.rsqrt(jnp.mean(center * center, -1, keepdims=True) + EPS)
    mean_out[...] = mean
    rstd_out[...] = rstd
    state = (center * rstd * (1.0 + mod[1]) + mod[0]).astype(BF16)
    hidden[...] = state
    hidden_t[...] = state.T
    branch_grad[...] = (upstream[...].astype(F32) * mod[2]).astype(BF16)


def pack(qkv, out_t, packed, sems):
    k, n = qkv.shape[1], out_t.shape[1]
    copies = [
        pltpu.make_async_copy(qkv, packed.at[:, pl.ds(0, k)], sems.at[0]),
        pltpu.make_async_copy(out_t, packed.at[:, pl.ds(k, n)], sems.at[1]),
    ]
    for copy in copies:
        copy.start()
    for copy in copies:
        copy.wait()


def pack_maps(down_t, up, copies):
    half = down_t.shape[1] // 2
    down = down_t[...].astype(F32).T
    both = jnp.concatenate([down[:half], down[half:]], 1).astype(BF16)
    rows = up.shape[0]
    values = up[...].astype(F32)
    ups = jnp.concatenate(
        [values[:, h * HEAD : (h + 1) * HEAD] for h in range(up.shape[1] // HEAD)], 0
    ).astype(BF16)
    for d in range(copies.shape[0]):
        copies[d, :half] = both
        copies[d, half:] = ups


def unpack_maps(maps, down, up):
    parts = maps.shape[0]
    cols, n = up.shape
    half = down.shape[0] // parts // 2
    own = cols // parts
    for d in range(parts):
        both = maps[d, :half].astype(F32)
        at = 2 * half * d
        down[at : at + half, :] = both[:, :cols].astype(BF16)
        down[at + half : at + 2 * half, :] = both[:, cols:].astype(BF16)
        rows = maps[d, half:].astype(F32)
        for h in range(n // HEAD):
            up[d * own : (d + 1) * own, h * HEAD : (h + 1) * HEAD] = rows[
                h * own : (h + 1) * own
            ]


def head_scales(x):
    parts = []
    for h in range(x.shape[1] // HEAD):
        v = x[:, h * HEAD : (h + 1) * HEAD]
        parts.append(lax.rsqrt(jnp.mean(v * v, -1, keepdims=True) + EPS))
    return parts


def projections(
    hidden_at, branch_at, w_at, down_at, up, sent, raw, low_out, hidden, branch, w, w_down, sems
):
    n = up.shape[1]
    heads = n // HEAD
    positions = sent.shape[2]

    def fetch(src, dst, i):
        return pltpu.make_async_copy(src, dst, sems.at[i])

    def columns(i, start, size):
        at = pl.ds(start, size)
        return fetch(w_at.at[:, at], w.at[:, at], i)

    blocks = [columns(i, i * n, n) for i in range(4)]
    rows = fetch(hidden_at, hidden, 4)
    grads = fetch(branch_at, branch, 5)
    down = fetch(down_at, w_down, 6)
    for copy in (rows, down, *blocks[:3], grads, blocks[3]):
        copy.start()

    def store(t, x):
        scales = head_scales(x) if t < 2 else None
        for h in range(heads):
            part = x[:, h * HEAD : (h + 1) * HEAD]
            if t < 2:
                part = part * scales[h]
            part = part.astype(BF16)
            for g in range(x.shape[0] // positions):
                sent[g * heads + h, t] = part[g * positions : (g + 1) * positions]

    up_q, up_v = split_up(up[...], up.shape[0] // 2)
    rows.wait()
    down.wait()
    low = dot(hidden[...], w_down[...]).astype(BF16)
    low_out[...] = low
    blocks[0].wait()
    q = dot(hidden[...], w[:, :n]) + dot(low, up_q)
    raw[:, :n] = q
    store(0, q)
    blocks[1].wait()
    k = dot(hidden[...], w[:, n : 2 * n])
    raw[:, n:] = k
    store(1, k)
    blocks[2].wait()
    store(2, dot(hidden[...], w[:, 2 * n : 3 * n]) + dot(low, up_v))
    grads.wait()
    blocks[3].wait()
    store(3, dot(branch[...], w[:, 3 * n : 4 * n]))


def attention(rows_in, back):
    frames, _, positions, _ = rows_in.shape
    group = 8
    total = frames * group
    row = lax.broadcasted_iota(jnp.int32, (total, total), 0) % group
    col = lax.broadcasted_iota(jnp.int32, (total, total), 1) % group
    same = row == col
    scale = HEAD**-0.5
    halves = []
    for p in range(positions // group):

        def rows_of(ref, t):
            x = ref[:, t].astype(F32)[:, p * group : (p + 1) * group]
            return x.reshape(total, HEAD).astype(BF16)

        q, k, v, g = (rows_of(rows_in, t) for t in range(4))
        s = dot(q, k, NT) * scale
        e = jnp.where(same, jnp.exp(s), 0.0)
        a = e / jnp.sum(e, -1, keepdims=True)
        low = a.astype(BF16)
        attended = dot(low, v)
        dp = dot(g, v, NT)
        dv = dot(low, g, TN)
        inner = jnp.sum(a * dp, -1, keepdims=True)
        ds = (a * (dp - inner) * scale).astype(BF16)
        dq = dot(ds, k)
        dk = dot(ds, q, TN)
        halves.append([x.reshape(frames, group, HEAD) for x in (dq, dk, dv, attended)])
    for t in range(4):
        x = jnp.concatenate([h[t] for h in halves], 1).astype(BF16)
        back[:, t] = x


def norm_back(raw, incoming):
    parts = []
    for h in range(raw.shape[1] // HEAD):
        x = raw[:, h * HEAD : (h + 1) * HEAD]
        u = incoming[:, h * HEAD : (h + 1) * HEAD].astype(F32)
        r = lax.rsqrt(jnp.mean(x * x, -1, keepdims=True) + EPS)
        parts.append(r * u - x * (r * r * r * jnp.mean(x * u, -1, keepdims=True)))
    return jnp.concatenate(parts, 1).astype(BF16)


def adapter_terms(rank, scale, back, raw, low, up, hidden_t, joined, low_grad, sections):
    n = up.shape[1]
    heads = n // HEAD
    dq = norm_back(raw[:, :n], unpack_blocks(back, 0, heads))
    dk = norm_back(raw[:, n:], unpack_blocks(back, 1, heads))
    dv = unpack_blocks(back, 2, heads)
    joined[:, :n] = dq
    joined[:, n : 2 * n] = dk
    joined[:, 2 * n :] = dv
    up_q, up_v = split_up(up[...], rank)
    lg = (dot(dq, up_q, NT) + dot(dv, up_v, NT)).astype(BF16)
    low_grad[...] = lg
    down = dot(hidden_t[...], jnp.concatenate([lg, lg], 1)) * scale
    low_rows = low[...]
    row = lax.broadcasted_iota(jnp.int32, (2 * rank, n), 0)
    up_grad = jnp.where(row < rank, dot(low_rows, dq, TN), dot(low_rows, dv, TN)) * scale
    parts = sections.shape[0]
    per, half = down.shape[0] // parts, down.shape[0] // parts // 2
    own = 2 * rank // parts
    left = lax.broadcasted_iota(jnp.int32, (half, HEAD), 1) < 2 * rank
    for d in range(parts):
        sections[d, :half] = jnp.where(
            left, down[d * per : d * per + half], down[d * per + half : (d + 1) * per]
        ).astype(BF16)
        sections[d, half:] = jnp.concatenate(
            [up_grad[d * own : (d + 1) * own, h * HEAD : (h + 1) * HEAD] for h in range(heads)], 0
        ).astype(BF16)


def finish(
    steps, grad_scale, joined, low_grad, back, x, mean, rstd, mod, upstream, w_at, down_at,
    tokens_grad, mixed, mod_rows, held, w, w_down, sems,
):
    width = x.shape[1] // steps
    total = x.shape[1]
    n3 = joined.shape[1]
    n4 = n3 + n3 // 3
    tiles = total // HEAD
    down = pltpu.make_async_copy(down_at, w_down, sems.at[steps])
    down.start()
    copies = []
    for j in range(steps):
        at = pl.ds(j * width, width)
        copies.append(pltpu.make_async_copy(w_at.at[at], w.at[at], sems.at[j]))
        copies[j].start()
    attended = unpack_blocks(back, 3, n3 // 3 // HEAD)
    s1 = jnp.zeros((x.shape[0], 1), F32)
    s2 = jnp.zeros((x.shape[0], 1), F32)
    for j in range(steps):
        c = slice(j * width, (j + 1) * width)
        copies[j].wait()
        if j == 0:
            down.wait()
        hg = dot(joined[...], w[c, :n3], NT) + dot(low_grad[...], w_down[c], NT)
        out = dot(attended, w[c, n3:n4], NT)
        values = x[:, c].astype(F32)
        up_rows = upstream[:, c].astype(F32)
        mixed[:, c] = (values + mod[2, :, c] * out).astype(BF16)
        normed = (values - mean[...]) * rstd[...]
        ng = hg * (1.0 + mod[1, :, c])
        held[:, c] = ng
        s1 += jnp.sum(ng, -1, keepdims=True)
        s2 += jnp.sum(ng * normed, -1, keepdims=True)
        for r, term in enumerate((hg, hg * normed, up_rows * out)):
            sums = jnp.sum(term, 0, keepdims=True) * grad_scale
            for i in range(width // HEAD):
                row = r * tiles + j * (width // HEAD) + i
                mod_rows[row : row + 1, :] = sums[:, i * HEAD : (i + 1) * HEAD]
    m1 = s1 * (1.0 / total)
    m2 = s2 * (1.0 / total)
    for j in range(steps):
        c = slice(j * width, (j + 1) * width)
        normed = (x[:, c].astype(F32) - mean[...]) * rstd[...]
        tokens_grad[:, c] = (
            upstream[:, c].astype(F32) + rstd[...] * (held[:, c] - m1 - normed * m2)
        ).astype(BF16)


def spread(arrived, mod_rows, both):
    share = jnp.sum(arrived[...].astype(F32), 0).astype(BF16)
    rows = mod_rows[...].astype(BF16)
    parts = both.shape[0]
    rows_a, rows_b = share.shape[0] // parts, rows.shape[0] // parts
    pad = jnp.zeros((both.shape[1] - rows_a - rows_b, HEAD), F32)
    for j in range(parts):
        piece = jnp.concatenate(
            [
                share[j * rows_a : (j + 1) * rows_a].astype(F32),
                rows[j * rows_b : (j + 1) * rows_b].astype(F32),
                pad,
            ],
            0,
        )
        both[j] = piece.astype(BF16)


def summed(arrived, out):
    total = jnp.sum(arrived[...].astype(F32), 0).astype(BF16)
    out[...] = jnp.broadcast_to(total[None], out.shape)


def collected(rows_a, rows_b, shares, down_t, up_grad, mod_grad):
    values = shares[...].astype(F32)
    parts = values.shape[0]
    cols = down_t.shape[0]
    own = up_grad.shape[0]
    half = down_t.shape[1] // 2
    a = jnp.concatenate([values[j, :rows_a] for j in range(parts)], 0)
    b = jnp.concatenate([values[j, rows_a : rows_a + rows_b] for j in range(parts)], 0)
    down_t[...] = jnp.concatenate([a[:half, :cols], a[:half, cols:]], 0).T
    for h in range(up_grad.shape[1] // HEAD):
        up_grad[:, h * HEAD : (h + 1) * HEAD] = a[half + h * own : half + (h + 1) * own]
    tiles = mod_grad.shape[2] // HEAD
    for i in range(3 * tiles):
        mod_grad[i // tiles, :, (i % tiles) * HEAD : (i % tiles + 1) * HEAD] = b[i : i + 1]


def per_device(tokens, modulation, qkv, out_w, down_w, up_w, output_gradient):
    dp, ctx = lax.axis_size("dp"), lax.axis_size(CTX)
    m, width = tokens.shape[2], tokens.shape[3]
    n = up_w.shape[1]
    heads = n // HEAD
    rank = down_w.shape[1] // 2
    positions = m // (ctx // heads)
    mod = modulation.transpose(1, 0, 2)
    grad_scale = (dp * ctx * m) ** (-0.5)
    own = width // dp

    cols = 4 * n
    packed = call(
        pack,
        shape((own, cols), BF16),
        in_specs=[pl.BlockSpec(memory_space=pl.ANY)] * 2,
        out_specs=pl.BlockSpec(memory_space=pltpu.VMEM),
        scratch=[pltpu.SemaphoreType.DMA((2,))],
        moved=4 * own * cols,
        vmem=60,
    )(qkv, out_w.T)
    w = lax.all_gather(packed, "dp", axis=0, tiled=True)
    w = pltpu.with_memory_space_constraint(w, pltpu.HBM)
    own_rows = own // 2 + (2 * rank // dp) * heads
    maps = call(pack_maps, shape((dp, own_rows, HEAD), BF16), moved=2**19)(down_w.T, up_w)
    w_down, up = call(
        unpack_maps, (shape((width, 2 * rank), BF16), shape((2 * rank, n), F32)), moved=2**21
    )(lax.all_to_all(maps, "dp", 0, 0, tiled=True))
    w_down = pltpu.with_memory_space_constraint(w_down, pltpu.HBM)
    up = up.astype(BF16)

    x = tokens.reshape(m, width)
    upstream = output_gradient.reshape(m, width)
    hidden, hidden_t, branch_grad, mean, rstd = call(
        normalize,
        (
            shape((m, width), BF16),
            shape((width, m), BF16),
            shape((m, width), BF16),
            shape((m, 1), F32),
            shape((m, 1), F32),
        ),
        flops=20 * m * width,
        moved=10 * m * width,
    )(x, mod, upstream)

    sent, raw, low = call(
        projections,
        (
            shape((ctx, 4, positions, HEAD), BF16),
            shape((m, 2 * n), F32),
            shape((m, 2 * rank), BF16),
        ),
        in_specs=[pl.BlockSpec(memory_space=pl.ANY)] * 4 + [pl.BlockSpec(memory_space=pltpu.VMEM)],
        out_specs=(pl.BlockSpec(memory_space=pltpu.VMEM),) * 3,
        scratch=[
            pltpu.VMEM((m, width), BF16),
            pltpu.VMEM((m, width), BF16),
            pltpu.VMEM((width, cols), BF16),
            pltpu.VMEM((width, 2 * rank), BF16),
            pltpu.SemaphoreType.DMA((7,)),
        ],
        vmem=32,
        flops=2 * m * width * cols,
        moved=2 * width * cols,
    )(
        pltpu.with_memory_space_constraint(hidden, pltpu.HBM),
        pltpu.with_memory_space_constraint(branch_grad, pltpu.HBM),
        w,
        w_down,
        up,
    )
    rows_in = lax.all_to_all(sent, CTX, 0, 0, tiled=True)

    back_sent = call(
        attention,
        shape((ctx, 4, positions, HEAD), BF16),
        flops=7 * 2 * 2 * 256 * 256 * 128,
        moved=8 * m * n * 2,
        vmem=16,
    )(rows_in)
    back = lax.all_to_all(back_sent, CTX, 0, 0, tiled=True)

    joined, low_grad, sections = call(
        functools.partial(adapter_terms, rank, grad_scale),
        (
            shape((m, 3 * n), BF16),
            shape((m, 2 * rank), BF16),
            shape((dp, own_rows, HEAD), BF16),
        ),
        flops=2 * m * width * HEAD + 8 * m * n * 64,
        moved=m * width * 2 + m * n * 20,
    )(back, raw, low, up, hidden_t)
    arrived = lax.all_to_all(sections, "dp", 0, 0, tiled=True)

    steps = dp // 2
    tokens_grad, mixed, mod_rows = call(
        functools.partial(finish, steps, grad_scale),
        (
            shape((m, width), BF16),
            shape((m, width), BF16),
            shape((3 * width // HEAD, HEAD), F32),
        ),
        in_specs=[pl.BlockSpec(memory_space=pltpu.VMEM)] * 8 + [pl.BlockSpec(memory_space=pl.ANY)] * 2,
        out_specs=(pl.BlockSpec(memory_space=pltpu.VMEM),) * 3,
        scratch=[
            pltpu.VMEM((m, width), F32),
            pltpu.VMEM((width, cols), BF16),
            pltpu.VMEM((width, 2 * rank), BF16),
            pltpu.SemaphoreType.DMA((steps + 1,)),
        ],
        flops=2 * m * width * cols,
        moved=2 * width * cols + 8 * m * width,
        vmem=32,
    )(joined, low_grad, back, x, mean, rstd, mod, upstream, w, w_down)

    near, far = lax.axis_size("near"), lax.axis_size("yh") * lax.axis_size("far")
    rows_a, rows_b = own_rows // near, mod_rows.shape[0] // near
    rows = 16 * -(-(rows_a + rows_b) // 16)
    both = call(spread, shape((near, rows, HEAD), BF16), moved=2**19, vmem=8)(arrived, mod_rows)
    part = call(summed, shape((far, rows, HEAD), BF16), moved=2**17, vmem=8)(
        lax.all_to_all(both, "near", 0, 0, tiled=True)
    )
    part = call(summed, shape((near, rows, HEAD), BF16), moved=2**17, vmem=8)(
        lax.all_to_all(part, ("yh", "far"), 0, 0, tiled=True)
    )
    down_t, up_grad, mod_grad = call(
        functools.partial(collected, rows_a, rows_b),
        (
            shape((2 * rank, own), F32),
            shape((2 * rank // dp, n), F32),
            shape((3, 1, width), F32),
        ),
        moved=2**18,
        vmem=8,
    )(lax.all_to_all(part, "near", 0, 0, tiled=True))
    return (
        mixed.reshape(tokens.shape),
        tokens_grad.reshape(tokens.shape),
        mod_grad.reshape(1, 3, width),
        down_t.T,
        up_grad,
    )


def solution(mesh):
    dp, ctx = mesh.devices.shape
    fine = Mesh(mesh.devices.reshape(dp, 2, ctx // 8, 4), ("dp", *CTX))
    return jax.shard_map(
        per_device,
        mesh=fine,
        in_specs=(
            P("dp", CTX, None, None),
            P("dp", None, None),
            P("dp", None),
            P(None, "dp"),
            P("dp", None),
            P("dp", None),
            P("dp", CTX, None, None),
        ),
        out_specs=(
            P("dp", CTX, None, None),
            P("dp", CTX, None, None),
            P("dp", None, None),
            P("dp", None),
            P("dp", None),
        ),
        check_vma=False,
    )
```

```python
import functools

import jax
import jax.numpy as jnp
from jax import lax
from jax.experimental import pallas as pl
from jax.experimental.pallas import tpu as pltpu
from jax.sharding import Mesh
from jax.sharding import PartitionSpec as P

HEAD = 128
EPS = 1e-06
F32 = jnp.float32
BF16 = jnp.bfloat16
NT = (((1,), (1,)), ((), ()))
TN = (((0,), (0,)), ((), ()))
CTX = ("yh", "far", "near")
NN = (((1,), (0,)), ((), ()))


def dot(a, b, dims=NN):
    return lax.dot_general(a, b, dims, preferred_element_type=F32)


def call(body, out_shape, grid=None, in_specs=None, out_specs=None, scratch=(), flops=0, moved=0, vmem=20):
    extra = {} if in_specs is None else {"in_specs": in_specs, "out_specs": out_specs}
    if grid is not None:
        extra["grid"] = grid
    return pl.pallas_call(
        body,
        out_shape=out_shape,
        scratch_shapes=list(scratch),
        compiler_params=pltpu.CompilerParams(vmem_limit_bytes=vmem * 2**20),
        cost_estimate=pl.CostEstimate(flops=flops, bytes_accessed=moved, transcendentals=0),
        **extra,
    )


def shape(dims, dtype):
    return jax.ShapeDtypeStruct(dims, dtype)


def whole(*dims):
    return pl.BlockSpec(dims, lambda i: (0,) * len(dims))


def split_up(up, rank):
    row = lax.broadcasted_iota(jnp.int32, up.shape, 0)
    zero = jnp.zeros_like(up)
    return jnp.where(row < rank, up, zero), jnp.where(row < rank, zero, up)


def unpack_blocks(ref, t, heads):
    groups = ref.shape[0] // heads
    columns = [
        jnp.concatenate([ref[g * heads + h, t] for g in range(groups)], 0) for h in range(heads)
    ]
    return jnp.concatenate(columns, 1)


def normalize(x, mod, upstream, hidden, hidden_t, branch_grad, mean_out, rstd_out):
    values = x[...].astype(F32)
    mean = jnp.mean(values, -1, keepdims=True)
    center = values - mean
    rstd = lax.rsqrt(jnp.mean(center * center, -1, keepdims=True) + EPS)
    mean_out[...] = mean
    rstd_out[...] = rstd
    state = (center * rstd * (1.0 + mod[1]) + mod[0]).astype(BF16)
    hidden[...] = state
    hidden_t[...] = state.T
    branch_grad[...] = (upstream[...].astype(F32) * mod[2]).astype(BF16)


def pack(chunks, qkv, out_t, packed, held, sems):
    k, n = qkv.shape[1], out_t.shape[1]
    rows = qkv.shape[0] // chunks
    landing, leaving = [], []
    for i in range(chunks):
        at = pl.ds(i * rows, rows)
        landing.append(
            (
                pltpu.make_async_copy(qkv.at[at], held.at[at, pl.ds(0, k)], sems.at[0, i]),
                pltpu.make_async_copy(out_t.at[at], held.at[at, pl.ds(k, n)], sems.at[1, i]),
            )
        )
        leaving.append(pltpu.make_async_copy(held.at[at], packed.at[at], sems.at[2, i]))
        for copy in landing[i]:
            copy.start()
    for i in range(chunks):
        for copy in landing[i]:
            copy.wait()
        leaving[i].start()
    for copy in leaving:
        copy.wait()


def pack_maps(down_t, up, copies):
    half = down_t.shape[1] // 2
    down = down_t[...].astype(F32).T
    both = jnp.concatenate([down[:half], down[half:]], 1).astype(BF16)
    rows = up.shape[0]
    values = up[...].astype(F32)
    ups = jnp.concatenate(
        [values[:, h * HEAD : (h + 1) * HEAD] for h in range(up.shape[1] // HEAD)], 0
    ).astype(BF16)
    for d in range(copies.shape[0]):
        copies[d, :half] = both
        copies[d, half:] = ups


def unpack_maps(maps, down, up):
    parts = maps.shape[0]
    cols, n = up.shape
    half = down.shape[0] // parts // 2
    own = cols // parts
    for d in range(parts):
        both = maps[d, :half].astype(F32)
        at = 2 * half * d
        down[at : at + half, :] = both[:, :cols].astype(BF16)
        down[at + half : at + 2 * half, :] = both[:, cols:].astype(BF16)
        rows = maps[d, half:].astype(F32)
        for h in range(n // HEAD):
            up[d * own : (d + 1) * own, h * HEAD : (h + 1) * HEAD] = rows[
                h * own : (h + 1) * own
            ]


def head_scales(x):
    parts = []
    for h in range(x.shape[1] // HEAD):
        v = x[:, h * HEAD : (h + 1) * HEAD]
        parts.append(lax.rsqrt(jnp.mean(v * v, -1, keepdims=True) + EPS))
    return parts


def projections(
    hidden_at, branch_at, w_at, down_at, up, sent, raw, low_out, hidden, branch, w, w_down, sems
):
    n = up.shape[1]
    heads = n // HEAD
    positions = sent.shape[2]

    def fetch(src, dst, i):
        return pltpu.make_async_copy(src, dst, sems.at[i])

    def columns(i, start, size):
        at = pl.ds(start, size)
        return fetch(w_at.at[:, at], w.at[:, at], i)

    blocks = [columns(i, i * n, n) for i in range(4)]
    rows = fetch(hidden_at, hidden, 4)
    grads = fetch(branch_at, branch, 5)
    down = fetch(down_at, w_down, 6)
    for copy in (rows, down, *blocks[:3], grads, blocks[3]):
        copy.start()

    def store(t, x):
        scales = head_scales(x) if t < 2 else None
        for h in range(heads):
            part = x[:, h * HEAD : (h + 1) * HEAD]
            if t < 2:
                part = part * scales[h]
            part = part.astype(BF16)
            for g in range(x.shape[0] // positions):
                sent[g * heads + h, t] = part[g * positions : (g + 1) * positions]

    up_q, up_v = split_up(up[...], up.shape[0] // 2)
    rows.wait()
    down.wait()
    low = dot(hidden[...], w_down[...]).astype(BF16)
    low_out[...] = low
    blocks[0].wait()
    q = dot(hidden[...], w[:, :n]) + dot(low, up_q)
    raw[:, :n] = q
    store(0, q)
    blocks[1].wait()
    k = dot(hidden[...], w[:, n : 2 * n])
    raw[:, n:] = k
    store(1, k)
    blocks[2].wait()
    store(2, dot(hidden[...], w[:, 2 * n : 3 * n]) + dot(low, up_v))
    grads.wait()
    blocks[3].wait()
    store(3, dot(branch[...], w[:, 3 * n : 4 * n]))


def attention(rows_in, back):
    frames, _, positions, _ = rows_in.shape
    group = 8
    total = frames * group
    row = lax.broadcasted_iota(jnp.int32, (total, total), 0) % group
    col = lax.broadcasted_iota(jnp.int32, (total, total), 1) % group
    same = row == col
    scale = HEAD**-0.5
    halves = []
    for p in range(positions // group):

        def rows_of(ref, t):
            x = ref[:, t].astype(F32)[:, p * group : (p + 1) * group]
            return x.reshape(total, HEAD).astype(BF16)

        q, k, v, g = (rows_of(rows_in, t) for t in range(4))
        s = dot(q, k, NT) * scale
        e = jnp.where(same, jnp.exp(s), 0.0)
        a = e / jnp.sum(e, -1, keepdims=True)
        low = a.astype(BF16)
        attended = dot(low, v)
        dp = dot(g, v, NT)
        dv = dot(low, g, TN)
        inner = jnp.sum(a * dp, -1, keepdims=True)
        ds = (a * (dp - inner) * scale).astype(BF16)
        dq = dot(ds, k)
        dk = dot(ds, q, TN)
        halves.append([x.reshape(frames, group, HEAD) for x in (dq, dk, dv, attended)])
    for t in range(4):
        x = jnp.concatenate([h[t] for h in halves], 1).astype(BF16)
        back[:, t] = x


def norm_back(raw, incoming):
    parts = []
    for h in range(raw.shape[1] // HEAD):
        x = raw[:, h * HEAD : (h + 1) * HEAD]
        u = incoming[:, h * HEAD : (h + 1) * HEAD].astype(F32)
        r = lax.rsqrt(jnp.mean(x * x, -1, keepdims=True) + EPS)
        parts.append(r * u - x * (r * r * r * jnp.mean(x * u, -1, keepdims=True)))
    return jnp.concatenate(parts, 1).astype(BF16)


def adapter_terms(rank, scale, back, raw, low, up, hidden_t, joined, low_grad, sections):
    n = up.shape[1]
    heads = n // HEAD
    dq = norm_back(raw[:, :n], unpack_blocks(back, 0, heads))
    dk = norm_back(raw[:, n:], unpack_blocks(back, 1, heads))
    dv = unpack_blocks(back, 2, heads)
    joined[:, :n] = dq
    joined[:, n : 2 * n] = dk
    joined[:, 2 * n :] = dv
    up_q, up_v = split_up(up[...], rank)
    lg = (dot(dq, up_q, NT) + dot(dv, up_v, NT)).astype(BF16)
    low_grad[...] = lg
    down = dot(hidden_t[...], jnp.concatenate([lg, lg], 1)) * scale
    low_rows = low[...]
    row = lax.broadcasted_iota(jnp.int32, (2 * rank, n), 0)
    up_grad = jnp.where(row < rank, dot(low_rows, dq, TN), dot(low_rows, dv, TN)) * scale
    parts = sections.shape[0]
    per, half = down.shape[0] // parts, down.shape[0] // parts // 2
    own = 2 * rank // parts
    left = lax.broadcasted_iota(jnp.int32, (half, HEAD), 1) < 2 * rank
    for d in range(parts):
        sections[d, :half] = jnp.where(
            left, down[d * per : d * per + half], down[d * per + half : (d + 1) * per]
        ).astype(BF16)
        sections[d, half:] = jnp.concatenate(
            [up_grad[d * own : (d + 1) * own, h * HEAD : (h + 1) * HEAD] for h in range(heads)], 0
        ).astype(BF16)


def finish(
    steps, grad_scale, joined, low_grad, back, x, mean, rstd, mod, upstream, w_at, down_at,
    tokens_grad, mixed, mod_rows, held, w, w_down, sems,
):
    width = x.shape[1] // steps
    total = x.shape[1]
    n3 = joined.shape[1]
    n4 = n3 + n3 // 3
    tiles = total // HEAD
    down = pltpu.make_async_copy(down_at, w_down, sems.at[steps])
    down.start()
    copies = []
    for j in range(steps):
        at = pl.ds(j * width, width)
        copies.append(pltpu.make_async_copy(w_at.at[at], w.at[at], sems.at[j]))
        copies[j].start()
    attended = unpack_blocks(back, 3, n3 // 3 // HEAD)
    s1 = jnp.zeros((x.shape[0], 1), F32)
    s2 = jnp.zeros((x.shape[0], 1), F32)
    for j in range(steps):
        c = slice(j * width, (j + 1) * width)
        copies[j].wait()
        if j == 0:
            down.wait()
        hg = dot(joined[...], w[c, :n3], NT) + dot(low_grad[...], w_down[c], NT)
        out = dot(attended, w[c, n3:n4], NT)
        values = x[:, c].astype(F32)
        up_rows = upstream[:, c].astype(F32)
        mixed[:, c] = (values + mod[2, :, c] * out).astype(BF16)
        normed = (values - mean[...]) * rstd[...]
        ng = hg * (1.0 + mod[1, :, c])
        held[:, c] = ng
        s1 += jnp.sum(ng, -1, keepdims=True)
        s2 += jnp.sum(ng * normed, -1, keepdims=True)
        for r, term in enumerate((hg, hg * normed, up_rows * out)):
            sums = jnp.sum(term, 0, keepdims=True) * grad_scale
            for i in range(width // HEAD):
                row = r * tiles + j * (width // HEAD) + i
                mod_rows[row : row + 1, :] = sums[:, i * HEAD : (i + 1) * HEAD]
    m1 = s1 * (1.0 / total)
    m2 = s2 * (1.0 / total)
    for j in range(steps):
        c = slice(j * width, (j + 1) * width)
        normed = (x[:, c].astype(F32) - mean[...]) * rstd[...]
        tokens_grad[:, c] = (
            upstream[:, c].astype(F32) + rstd[...] * (held[:, c] - m1 - normed * m2)
        ).astype(BF16)


def spread(arrived, mod_rows, both):
    share = jnp.sum(arrived[...].astype(F32), 0).astype(BF16)
    rows = mod_rows[...].astype(BF16)
    parts = both.shape[0]
    rows_a, rows_b = share.shape[0] // parts, rows.shape[0] // parts
    pad = jnp.zeros((both.shape[1] - rows_a - rows_b, HEAD), F32)
    for j in range(parts):
        piece = jnp.concatenate(
            [
                share[j * rows_a : (j + 1) * rows_a].astype(F32),
                rows[j * rows_b : (j + 1) * rows_b].astype(F32),
                pad,
            ],
            0,
        )
        both[j] = piece.astype(BF16)


def summed(arrived, out):
    total = jnp.sum(arrived[...].astype(F32), 0).astype(BF16)
    out[...] = jnp.broadcast_to(total[None], out.shape)


def collected(rows_a, rows_b, shares, down_t, up_grad, mod_grad):
    values = shares[...].astype(F32)
    parts = values.shape[0]
    cols = down_t.shape[0]
    own = up_grad.shape[0]
    half = down_t.shape[1] // 2
    a = jnp.concatenate([values[j, :rows_a] for j in range(parts)], 0)
    b = jnp.concatenate([values[j, rows_a : rows_a + rows_b] for j in range(parts)], 0)
    down_t[...] = jnp.concatenate([a[:half, :cols], a[:half, cols:]], 0).T
    for h in range(up_grad.shape[1] // HEAD):
        up_grad[:, h * HEAD : (h + 1) * HEAD] = a[half + h * own : half + (h + 1) * own]
    tiles = mod_grad.shape[2] // HEAD
    for i in range(3 * tiles):
        mod_grad[i // tiles, :, (i % tiles) * HEAD : (i % tiles + 1) * HEAD] = b[i : i + 1]


def per_device(tokens, modulation, qkv, out_w, down_w, up_w, output_gradient):
    dp, ctx = lax.axis_size("dp"), lax.axis_size(CTX)
    m, width = tokens.shape[2], tokens.shape[3]
    n = up_w.shape[1]
    heads = n // HEAD
    rank = down_w.shape[1] // 2
    positions = m // (ctx // heads)
    mod = modulation.transpose(1, 0, 2)
    grad_scale = (dp * ctx * m) ** (-0.5)
    own = width // dp

    cols = 4 * n
    packed = call(
        functools.partial(pack, 4),
        shape((own, cols), BF16),
        in_specs=[pl.BlockSpec(memory_space=pl.ANY)] * 2,
        out_specs=pl.BlockSpec(memory_space=pl.ANY),
        scratch=[pltpu.VMEM((own, cols), BF16), pltpu.SemaphoreType.DMA((3, 4))],
        moved=4 * own * cols,
        vmem=60,
    )(qkv, out_w.T)
    w = lax.all_gather(packed, "dp", axis=0, tiled=True)
    w = pltpu.with_memory_space_constraint(w, pltpu.HBM)
    own_rows = own // 2 + (2 * rank // dp) * heads
    maps = call(pack_maps, shape((dp, own_rows, HEAD), BF16), moved=2**19)(down_w.T, up_w)
    w_down, up = call(
        unpack_maps, (shape((width, 2 * rank), BF16), shape((2 * rank, n), F32)), moved=2**21
    )(lax.all_to_all(maps, "dp", 0, 0, tiled=True))
    w_down = pltpu.with_memory_space_constraint(w_down, pltpu.HBM)
    up = up.astype(BF16)

    x = tokens.reshape(m, width)
    upstream = output_gradient.reshape(m, width)
    hidden, hidden_t, branch_grad, mean, rstd = call(
        normalize,
        (
            shape((m, width), BF16),
            shape((width, m), BF16),
            shape((m, width), BF16),
            shape((m, 1), F32),
            shape((m, 1), F32),
        ),
        flops=20 * m * width,
        moved=10 * m * width,
    )(x, mod, upstream)

    sent, raw, low = call(
        projections,
        (
            shape((ctx, 4, positions, HEAD), BF16),
            shape((m, 2 * n), F32),
            shape((m, 2 * rank), BF16),
        ),
        in_specs=[pl.BlockSpec(memory_space=pl.ANY)] * 4 + [pl.BlockSpec(memory_space=pltpu.VMEM)],
        out_specs=(pl.BlockSpec(memory_space=pltpu.VMEM),) * 3,
        scratch=[
            pltpu.VMEM((m, width), BF16),
            pltpu.VMEM((m, width), BF16),
            pltpu.VMEM((width, cols), BF16),
            pltpu.VMEM((width, 2 * rank), BF16),
            pltpu.SemaphoreType.DMA((7,)),
        ],
        vmem=32,
        flops=2 * m * width * cols,
        moved=2 * width * cols,
    )(
        pltpu.with_memory_space_constraint(hidden, pltpu.HBM),
        pltpu.with_memory_space_constraint(branch_grad, pltpu.HBM),
        w,
        w_down,
        up,
    )
    rows_in = lax.all_to_all(sent, CTX, 0, 0, tiled=True)

    back_sent = call(
        attention,
        shape((ctx, 4, positions, HEAD), BF16),
        flops=7 * 2 * 2 * 256 * 256 * 128,
        moved=8 * m * n * 2,
        vmem=16,
    )(rows_in)
    back = lax.all_to_all(back_sent, CTX, 0, 0, tiled=True)

    joined, low_grad, sections = call(
        functools.partial(adapter_terms, rank, grad_scale),
        (
            shape((m, 3 * n), BF16),
            shape((m, 2 * rank), BF16),
            shape((dp, own_rows, HEAD), BF16),
        ),
        flops=2 * m * width * HEAD + 8 * m * n * 64,
        moved=m * width * 2 + m * n * 20,
    )(back, raw, low, up, hidden_t)
    arrived = lax.all_to_all(sections, "dp", 0, 0, tiled=True)

    steps = dp // 2
    tokens_grad, mixed, mod_rows = call(
        functools.partial(finish, steps, grad_scale),
        (
            shape((m, width), BF16),
            shape((m, width), BF16),
            shape((3 * width // HEAD, HEAD), F32),
        ),
        in_specs=[pl.BlockSpec(memory_space=pltpu.VMEM)] * 8 + [pl.BlockSpec(memory_space=pl.ANY)] * 2,
        out_specs=(pl.BlockSpec(memory_space=pltpu.VMEM),) * 3,
        scratch=[
            pltpu.VMEM((m, width), F32),
            pltpu.VMEM((width, cols), BF16),
            pltpu.VMEM((width, 2 * rank), BF16),
            pltpu.SemaphoreType.DMA((steps + 1,)),
        ],
        flops=2 * m * width * cols,
        moved=2 * width * cols + 8 * m * width,
        vmem=32,
    )(joined, low_grad, back, x, mean, rstd, mod, upstream, w, w_down)

    near, far = lax.axis_size("near"), lax.axis_size("yh") * lax.axis_size("far")
    rows_a, rows_b = own_rows // near, mod_rows.shape[0] // near
    rows = 16 * -(-(rows_a + rows_b) // 16)
    both = call(spread, shape((near, rows, HEAD), BF16), moved=2**19, vmem=8)(arrived, mod_rows)
    part = call(summed, shape((far, rows, HEAD), BF16), moved=2**17, vmem=8)(
        lax.all_to_all(both, "near", 0, 0, tiled=True)
    )
    part = call(summed, shape((near, rows, HEAD), BF16), moved=2**17, vmem=8)(
        lax.all_to_all(part, ("yh", "far"), 0, 0, tiled=True)
    )
    down_t, up_grad, mod_grad = call(
        functools.partial(collected, rows_a, rows_b),
        (
            shape((2 * rank, own), F32),
            shape((2 * rank // dp, n), F32),
            shape((3, 1, width), F32),
        ),
        moved=2**18,
        vmem=8,
    )(lax.all_to_all(part, "near", 0, 0, tiled=True))
    return (
        mixed.reshape(tokens.shape),
        tokens_grad.reshape(tokens.shape),
        mod_grad.reshape(1, 3, width),
        down_t.T,
        up_grad,
    )


def solution(mesh):
    dp, ctx = mesh.devices.shape
    fine = Mesh(mesh.devices.reshape(dp, 2, ctx // 8, 4), ("dp", *CTX))
    return jax.shard_map(
        per_device,
        mesh=fine,
        in_specs=(
            P("dp", CTX, None, None),
            P("dp", None, None),
            P("dp", None),
            P(None, "dp"),
            P("dp", None),
            P("dp", None),
            P("dp", CTX, None, None),
        ),
        out_specs=(
            P("dp", CTX, None, None),
            P("dp", CTX, None, None),
            P("dp", None, None),
            P("dp", None),
            P("dp", None),
        ),
        check_vma=False,
    )
```
